128 devices in a mesh: bx: 8 (over y_lo, z), by: 16 (over x, y_hi, core).
Axes of the slice: x: 4, y: 4 (y_hi: 2, y_lo: 2; y = y_hi * 2 + y_lo), z: 4, core: 2. Of those that a mesh axis runs over, the one named last changes fastest.
Arguments:
- positions: float32 [3, 16384], P(None, ('bx', 'by')), may hold values from 0 to 16, as said below
- tangent: float32 [3, 16384], P(None, ('bx', 'by')), may hold values from -6 to 6
- embedding: float32 [16384, 256], P(('bx', 'by')), may hold values from -6 to 6
- counts: int32 [128], P(('bx', 'by')), may hold values from 64 to 128, as said below
- neighbours: int32 [32, 16384], P(None, ('bx', 'by')), may hold values from 0 to 191, as said below
- send_rows: int32 [128, 64], P(('bx', 'by')), may hold values from 0 to 127
- w_one_in: float32 [256, 256], replicated, may hold values from -0.375 to 0.375
- w_one_out: float32 [256, 512], replicated, may hold values from -0.375 to 0.375
- filter_one: float32 [20, 512], replicated, may hold values from -0.3125 to 0.3125
- w_left: float32 [256, 256], replicated, may hold values from -0.375 to 0.375
- w_right: float32 [256, 256], replicated, may hold values from -0.375 to 0.375
- w_two_in: float32 [256, 256], replicated, may hold values from -0.375 to 0.375
- w_two_out: float32 [256, 256], replicated, may hold values from -0.375 to 0.375
- filter_two: float32 [20, 256], replicated, may hold values from -0.3125 to 0.3125
- w_hidden: float32 [256, 256], replicated, may hold values from -0.375 to 0.375
- w_energy: float32 [256], replicated, may hold values from -0.375 to 0.375
Outputs:
- forces: float32 [3, 16384], P(None, ('bx', 'by'))
- hessian_tangent: float32 [3, 16384], P(None, ('bx', 'by'))
The draws below stay inside these ranges and needn't reach their ends.
Inputs may be any that keep to these rules, and one draw needn't show every extreme that they name: The live atoms of a brick are its first counts rows; every count is a multiple of 32; some brick holds 128 live atoms and some 128 // 2. `neighbours`: the 32 slots of an atom are distinct; each is a live row of its own brick other than the atom's own row, or a slot of a neighbouring brick that exists in the sheet. `positions`: atom n lies within one unit of its brick's indices along x and y, with the third coordinate in [0, 0.3).
All inputs are finite; a program needn't handle non-finite values.
Results may differ from the reference program's by a relative error of at most 0.0003.
Values sent between devices are 32-bit elements; how exact they have to be, the bound alone decides.
A program may use at most 192 MiB of HBM per device.

```python
import math
import jax
import jax.numpy as jnp
from jax import lax

F = 256
NR = 20
K = 32
ROWS = 128
GH = 8
BRICKS_X = 8
BRICKS_Y = 16
BRICKS = 128
ATOMS = 16384


offsets = ((-1, -1), (-1, 0), (-1, 1), (0, -1), (0, 1), (1, -1), (1, 0), (1, 1))


def shared_counts(key):
    levels = jax.random.randint(jax.random.fold_in(key, 11), (BRICKS,), 2, 5)
    chosen = jax.random.randint(jax.random.fold_in(key, 12), (), 0, BRICKS)
    second = (chosen + 1 + jax.random.randint(jax.random.fold_in(key, 13), (), 0, BRICKS - 1)) % BRICKS
    brick_order = jnp.arange(BRICKS)
    levels = jnp.where(brick_order == chosen, 4, levels)
    levels = jnp.where(brick_order == second, 2, levels)
    return (levels * (ROWS // 4)).astype(jnp.int32)


def draw_counts(key, part):
    return shared_counts(key)


def draw_send_rows(key, part):
    counts = shared_counts(key)
    raw_scores = jax.random.randint(jax.random.fold_in(key, 21), (BRICKS, 8, ROWS), 0, 2 ** 19)
    row_order = jnp.arange(ROWS)
    scores = raw_scores * ROWS + row_order[None, None, :] + jnp.where(row_order[None, None, :] < counts[:, None, None], 0, 2 ** 30)
    picked = jnp.argsort(scores, axis=-1)[:, :, :GH]
    return picked.reshape(BRICKS, 8 * GH).astype(jnp.int32)


def draw_neighbours(key, part):
    counts = shared_counts(key)
    table = ROWS + 8 * GH
    slot_order = jnp.arange(table)
    row_order = jnp.arange(ROWS)
    brick_order = jnp.arange(BRICKS)
    along_x = brick_order // BRICKS_Y
    along_y = brick_order % BRICKS_Y
    shift_x = jnp.array([target[0] for target in offsets])
    shift_y = jnp.array([target[1] for target in offsets])
    source_x = along_x[:, None] + shift_x[None, :]
    source_y = along_y[:, None] + shift_y[None, :]
    exists = (source_x >= 0) & (source_x < BRICKS_X) & (source_y >= 0) & (source_y < BRICKS_Y)
    ghost_group = jnp.clip((slot_order - ROWS) // GH, 0, 7)
    ghost_valid = (slot_order[None, :] >= ROWS) & exists[:, ghost_group]
    own_valid = (slot_order[None, None, :] < counts[:, None, None]) & (slot_order[None, None, :] != row_order[None, :, None])
    valid = own_valid | ghost_valid[:, None, :]
    raw_scores = jax.random.randint(jax.random.fold_in(key, 31), (BRICKS, ROWS, table), 0, 2 ** 17)
    ghost_penalty = jnp.where(slot_order >= ROWS, 2 ** 15, 0)
    scores = (raw_scores + ghost_penalty[None, None, :]) * table + slot_order[None, None, :] + jnp.where(valid, 0, 2 ** 30)
    picked = jnp.argsort(scores, axis=-1)[:, :, :K]
    return jnp.transpose(picked, (2, 0, 1)).reshape(K, BRICKS * ROWS).astype(jnp.int32)


def draw_positions(key, part):
    atom_order = jnp.arange(ATOMS)
    brick_of = atom_order // ROWS
    base_x = (brick_of // BRICKS_Y).astype(jnp.float32)
    base_y = (brick_of % BRICKS_Y).astype(jnp.float32)
    within = jax.random.uniform(key, (3, ATOMS), jnp.float32)
    return jnp.stack([base_x + within[0], base_y + within[1], 0.3 * within[2]])


def shard_levels(own_key, dims, cuts, least, high):
    loudness = 1.0
    for position, shards_of in cuts:
        steps = jax.random.uniform(jax.random.fold_in(jax.random.fold_in(own_key, 6), position), (shards_of,), jnp.float32, least / len(cuts), high / len(cuts))
        loudness = loudness * jnp.repeat(jnp.exp(steps), dims[position] // shards_of).reshape((-1,) + (1,) * (len(dims) - 1 - position))
    return loudness


def scatter_about(own_key, shape, deviation, reach, shards=(), kind=jnp.bfloat16):
    values = deviation * jax.random.normal(own_key, shape, jnp.float32)
    if shards:
        values = values * shard_levels(own_key, shape, shards, -0.22, 0.18)
    return jnp.clip(values, -reach, reach).astype(kind)


def setup_inputs(seed: int = 0) -> dict:
    streams_of = jax.random.split(jax.random.key(seed), 17)
    return {
        "positions": draw_positions(jax.random.fold_in(streams_of[16], 71), 0),
        "tangent": scatter_about(streams_of[1], (3, ATOMS), 1.0, 6.0, ((1, 128),), jnp.float32),
        "embedding": scatter_about(streams_of[2], (ATOMS, F), 1.0, 6.0, ((0, 128),), jnp.float32),
        "counts": draw_counts(jax.random.fold_in(streams_of[16], 71), 0),
        "neighbours": draw_neighbours(jax.random.fold_in(streams_of[16], 71), 0),
        "send_rows": draw_send_rows(jax.random.fold_in(streams_of[16], 71), 0),
        "w_one_in": scatter_about(streams_of[6], (F, F), F ** -0.5, 0.375, (), jnp.float32),
        "w_one_out": scatter_about(streams_of[7], (F, 2 * F), F ** -0.5, 0.375, (), jnp.float32),
        "filter_one": scatter_about(streams_of[8], (NR, 2 * F), (NR * NR) ** -0.5, 0.3125, (), jnp.float32),
        "w_left": scatter_about(streams_of[9], (F, F), F ** -0.5, 0.375, (), jnp.float32),
        "w_right": scatter_about(streams_of[10], (F, F), F ** -0.5, 0.375, (), jnp.float32),
        "w_two_in": scatter_about(streams_of[11], (F, F), F ** -0.5, 0.375, (), jnp.float32),
        "w_two_out": scatter_about(streams_of[12], (F, F), F ** -0.5, 0.375, (), jnp.float32),
        "filter_two": scatter_about(streams_of[13], (NR, F), (NR * NR) ** -0.5, 0.3125, (), jnp.float32),
        "w_hidden": scatter_about(streams_of[14], (F, F), F ** -0.5, 0.375, (), jnp.float32),
        "w_energy": scatter_about(streams_of[15], (F,), F ** -0.5, 0.375, (), jnp.float32),
    }


highest = lax.Precision.HIGHEST
cutoff_radius = 3.0
softening = 0.01
offsets = ((-1, -1), (-1, 0), (-1, 1), (0, -1), (0, 1), (1, -1), (1, 0), (1, 1))

def project_rows(features, w_inner, w_outer):
    inner = jax.nn.silu(jnp.dot(features, w_inner, precision=highest))
    return jnp.dot(inner, w_outer, precision=highest)

def geometry(pos_table, own_lists, basis_count):
    own_rows = own_lists.shape[1]
    centre = pos_table[:, :own_rows]
    others = jnp.take(pos_table, own_lists, axis=1)
    offset = others - centre[:, None, :]
    distance = jnp.sqrt(lax.optimization_barrier(jnp.sum(offset * offset, axis=0)) + softening)
    direction = offset / distance[None]
    orders = jnp.arange(1, basis_count + 1).astype(distance.dtype)
    radial = jnp.sin(orders[:, None, None] * (math.pi / cutoff_radius) * distance[None]) / distance[None]
    envelope = 0.5 * (jnp.cos(math.pi / cutoff_radius * distance) + 1.0)
    return (radial, envelope, direction)

def edge_weights(radial, envelope, filter_table):
    mixed = jnp.einsum('qkr,qc->krc', radial, filter_table, precision=highest)
    return mixed * envelope[:, :, None]

def first_layer(pos_table, phi_table, embed_own, own_lists, filter_one, w_left, w_right):
    radial, envelope, direction = geometry(pos_table, own_lists, filter_one.shape[0])
    scale_edges = 1.0 / math.sqrt(own_lists.shape[0])
    message = jnp.take(phi_table, own_lists, axis=0) * edge_weights(radial, envelope, filter_one)
    channels = embed_own.shape[1]
    scalar_part = scale_edges * lax.optimization_barrier(jnp.sum(message[:, :, :channels], axis=0))
    vector_part = scale_edges * jnp.einsum('ckr,krf->crf', direction, message[:, :, channels:], precision=highest)
    left_map = jnp.einsum('crf,fg->crg', vector_part, w_left, precision=highest)
    right_map = jnp.einsum('crf,fg->crg', vector_part, w_right, precision=highest)
    return embed_own + scalar_part + lax.optimization_barrier(jnp.sum(left_map * right_map, axis=0))

def second_layer(pos_table, phi_table, state_own, own_lists, live_rows, filter_two, w_hidden, w_energy):
    geometry_parts = geometry(pos_table, own_lists, filter_two.shape[0])
    scale_edges = 1.0 / math.sqrt(own_lists.shape[0])
    weighted = jnp.take(phi_table, own_lists, axis=0) * edge_weights(geometry_parts[0], geometry_parts[1], filter_two)
    message = scale_edges * lax.optimization_barrier(jnp.sum(weighted, axis=0))
    hidden_rows = jax.nn.silu(jnp.dot(state_own + message, w_hidden, precision=highest))
    return jnp.sum(live_rows * jnp.dot(hidden_rows, w_energy, precision=highest))

def reference(positions, tangent, embedding, counts, neighbours, send_rows, w_one_in, w_one_out, filter_one, w_left, w_right, w_two_in, w_two_out, filter_two, w_hidden, w_energy):
    bricks = BRICKS_X * BRICKS_Y
    float_type = positions.dtype
    brick_ids = jnp.arange(bricks, dtype=jnp.int32)
    along_x = brick_ids // BRICKS_Y
    along_y = brick_ids % BRICKS_Y
    ghost_ids = []
    ghost_inside = []
    for number, target in enumerate(offsets):
        source_x = along_x + target[0]
        source_y = along_y + target[1]
        inside = (source_x >= 0) & (source_x < BRICKS_X) & (source_y >= 0) & (source_y < BRICKS_Y)
        source = jnp.clip(source_x, 0, BRICKS_X - 1) * BRICKS_Y + jnp.clip(source_y, 0, BRICKS_Y - 1)
        rows_sent = send_rows[source][:, (7 - number) * GH:(8 - number) * GH]
        ghost_ids.append((source[:, None] * ROWS + rows_sent).astype(jnp.int32))
        ghost_inside.append(jnp.broadcast_to(inside[:, None], (bricks, GH)))
    own_ids = (brick_ids[:, None] * ROWS + jnp.arange(ROWS, dtype=jnp.int32)[None, :]).astype(jnp.int32)
    table_ids = jnp.concatenate([own_ids] + ghost_ids, 1).astype(jnp.int32)
    table_inside = jnp.concatenate([jnp.ones((bricks, ROWS), dtype=bool)] + ghost_inside, 1).astype(float_type)

    def brick_tables(brick_index):
        slot_atoms = table_ids[brick_index]
        inside_mask = table_inside[brick_index]
        pos_table = positions[:, slot_atoms] * inside_mask[None]
        tan_table = tangent[:, slot_atoms] * inside_mask[None]
        own_lists = lax.dynamic_slice_in_dim(neighbours, (brick_index * ROWS).astype(jnp.int32), ROWS, 1)
        return (slot_atoms, inside_mask, pos_table, tan_table, own_lists)

    def first_inputs(brick_index):
        slot_atoms, inside_mask, pos_table, tan_table, own_lists = brick_tables(brick_index)
        phi_table = project_rows(embedding[slot_atoms], w_one_in, w_one_out) * inside_mask[:, None]
        embed_own = lax.dynamic_slice_in_dim(embedding, (brick_index * ROWS).astype(jnp.int32), ROWS, 0)

        def first_section(pos_arg):
            return first_layer(pos_arg, phi_table, embed_own, own_lists, filter_one, w_left, w_right)
        return (first_section, pos_table, tan_table)

    def first_pass(brick_index):
        first_section, pos_table, tan_table = first_inputs(brick_index)
        return jax.jvp(first_section, (pos_table,), (tan_table,))
    node_state, state_tangent = lax.map(first_pass, brick_ids)
    node_state = node_state.reshape(bricks * ROWS, -1)
    state_tangent = state_tangent.reshape(bricks * ROWS, -1)

    def second_pass(brick_index):
        slot_atoms, inside_mask, pos_table, tan_table, own_lists = brick_tables(brick_index)
        state_table = node_state[slot_atoms] * inside_mask[:, None]
        tangent_table = state_tangent[slot_atoms] * inside_mask[:, None]
        live_rows = (jnp.arange(ROWS) < counts[brick_index]).astype(float_type)

        def second_section(pos_arg, table_arg):
            phi_table = project_rows(table_arg, w_two_in, w_two_out)
            return second_layer(pos_arg, phi_table, table_arg[:ROWS], own_lists, live_rows, filter_two, w_hidden, w_energy)
        return jax.jvp(jax.grad(second_section, argnums=(0, 1)), (pos_table, state_table), (tan_table, tangent_table))
    grads_second, tangents_second = lax.map(second_pass, brick_ids)
    flat_ids = table_ids.reshape(-1)
    inside_flat = table_inside.reshape(-1)
    channels = node_state.shape[1]

    def scatter_positions(per_brick):
        moved = jnp.transpose(per_brick, (1, 0, 2)).reshape(3, -1) * inside_flat[None]
        return jnp.zeros((3, bricks * ROWS), float_type).at[:, flat_ids].add(moved)

    def scatter_states(per_brick):
        moved = per_brick.reshape(-1, channels) * inside_flat[:, None]
        return jnp.zeros((bricks * ROWS, channels), float_type).at[flat_ids].add(moved)
    pos_grad = scatter_positions(grads_second[0])
    pos_grad_tangent = scatter_positions(tangents_second[0])
    state_cot = scatter_states(grads_second[1])
    state_cot_tangent = scatter_states(tangents_second[1])

    def third_pass(brick_index):
        first_section, pos_table, tan_table = first_inputs(brick_index)
        start = (brick_index * ROWS).astype(jnp.int32)
        own_cot = lax.dynamic_slice_in_dim(state_cot, start, ROWS, 0)
        own_cot_tangent = lax.dynamic_slice_in_dim(state_cot_tangent, start, ROWS, 0)

        def pull_first(pos_arg, cot_arg):
            pullback = jax.vjp(first_section, pos_arg)[1]
            return pullback(cot_arg)[0]
        return jax.jvp(pull_first, (pos_table, own_cot), (tan_table, own_cot_tangent))
    grads_first, tangents_first = lax.map(third_pass, brick_ids)
    pos_grad = pos_grad + scatter_positions(grads_first)
    pos_grad_tangent = pos_grad_tangent + scatter_positions(tangents_first)
    return (-pos_grad, -pos_grad_tangent)
```

```python
import functools
import math

import jax
import jax.numpy as jnp
from jax import lax
from jax.experimental import pallas as pl
from jax.experimental.pallas import tpu as pltpu
from jax.sharding import PartitionSpec as P

MESH = pl.DeviceIdType.MESH
f32 = jnp.float32
bf16 = jnp.bfloat16
offsets = ((-1, -1), (-1, 0), (-1, 1), (0, -1), (0, 1), (1, -1), (1, 0), (1, 1))
NN = (((1,), (0,)), ((), ()))
NT = (((1,), (1,)), ((), ()))
KAPPA = math.pi / 3.0
SOFT = 0.01
ROWS = 128
GHOSTS = 64
TABLE = ROWS + GHOSTS
F = 256
NR = 20
PAIRS = NR // 2
SPAN = 3 * ROWS
WIDE = PAIRS * SPAN
STEP = 768
STEPS = WIDE // STEP


def split(x):
    hi = x.astype(bf16)
    return hi, (x - hi.astype(f32)).astype(bf16)


def split3(x):
    hi = x.astype(bf16)
    rest = x - hi.astype(f32)
    mid = rest.astype(bf16)
    return hi, mid, (rest - mid.astype(f32)).astype(bf16)


def mm(a, b, dims=NN):
    return lax.dot_general(a, b, dims, preferred_element_type=f32)


def mm3(a, b, dims=NN):
    return mm(a[0], b[0], dims) + (mm(a[1], b[0], dims) + mm(a[0], b[1], dims))


def pick(refs, *index):
    return refs[0][index], refs[1][index]


def put(refs, value, *index):
    hi, lo = split(value)
    refs[0][index] = hi
    refs[1][index] = lo


def sin_cos(angle):
    turns = jnp.floor(angle * (0.5 / math.pi) + 0.5)
    half = 0.5 * ((angle - turns * 6.28125) - turns * (2.0 * math.pi - 6.28125))
    sq = half * half
    odd = 1.0 / 39916800.0
    for c in (1.0 / 362880.0, 1.0 / 5040.0, 1.0 / 120.0, 1.0 / 6.0, 1.0):
        odd = c - sq * odd
    sh = half * odd
    even = 1.0 / 479001600.0
    for c in (1.0 / 3628800.0, 1.0 / 40320.0, 1.0 / 720.0, 1.0 / 24.0, 0.5, 1.0):
        even = c - sq * even
    return 2.0 * sh * even, 1.0 - 2.0 * sh * sh


def sigmoid(v):
    return 1.0 / (1.0 + jnp.exp(-v))


def own_waves(s1, c1):
    twice = 2.0 * c1
    before_s, before_c = jnp.zeros_like(s1), jnp.ones_like(c1)
    s, c = s1, c1
    for q in range(NR):
        yield (q // 2) * SPAN + (q % 2) * ROWS, (q + 1) * KAPPA, s, c
        if q < NR - 1:
            s, before_s = twice * s - before_s, s
            c, before_c = twice * c - before_c, c


def ghost_waves(s1, c1):
    upper = lax.broadcasted_iota(jnp.int32, s1.shape, 1) >= GHOSTS
    s2, c2 = 2.0 * s1 * c1, 1.0 - 2.0 * s1 * s1
    twice = 2.0 * c2
    s, before_s = jnp.where(upper, s2, s1), jnp.where(upper, 0.0, -s1)
    c, before_c = jnp.where(upper, c2, c1), jnp.where(upper, 1.0, c1)
    shift = jnp.where(upper, 2.0 * KAPPA, KAPPA)
    for p in range(PAIRS):
        yield p * SPAN + 2 * ROWS, shift + 2.0 * p * KAPPA, s, c
        if p < PAIRS - 1:
            s, before_s = twice * s - before_s, s
            c, before_c = twice * c - before_c, c


E0, E1, E2, DD, IV, S1, C1, U0, W0 = 0, 1, 2, 3, 4, 5, 6, 7, 10
WAVES = (own_waves, ghost_waves)


def kernel(
    nx,
    ny,
    pos,
    tan,
    emb,
    cnt,
    nbr,
    snd,
    w1i,
    w1o,
    f1,
    wl,
    wr,
    w2i,
    w2o,
    f2,
    wh,
    we,
    force,
    hess,
    w1i_s,
    w1o_s,
    wlr_s,
    w2i_s,
    w2o_s,
    wh_s,
    sndpad,
    c8,
    csel,
    crecv,
    sel1,
    gemb,
    sel2,
    gnode,
    src3,
    rnode,
    gpos,
    rpos,
    onehot,
    mask,
    colb,
    geo,
    lbh,
    lbl,
    lvh,
    lvl,
    lth,
    ltl,
    pfs_s,
    pfv_s,
    p2_s,
    p2d_s,
    phi,
    acc,
    lr,
    node,
    pre2,
    phi2,
    mu,
    bar,
    out,
    pg,
    send1,
    recv1,
    sendc,
    recvc,
    send2,
    recv2,
    send3,
    recv3,
    send4,
    recv4,
    loads,
):
    lb, lv, lt = (lbh, lbl), (lvh, lvl), (lth, ltl)
    ix, iy = lax.axis_index("bx"), lax.axis_index("by")

    def device(g, sign):
        dx, dy = offsets[g]
        return (lax.rem(ix + sign * dx + nx, nx), lax.rem(iy + sign * dy + ny, ny))

    barrier = pltpu.get_barrier_semaphore()
    for g in range(8):
        pl.semaphore_signal(barrier, inc=1, device_id=device(g, 1), device_id_type=MESH)

    def block(ref, g):
        return ref.at[pl.ds(g * 8, 8), :]

    def copies(source, target, sends, recvs, sign, whole):
        return [
            pltpu.make_async_remote_copy(
                src_ref=source if whole else block(source, g),
                dst_ref=target.at[g] if whole else block(target, g),
                send_sem=sends.at[g],
                recv_sem=recvs.at[g],
                device_id=device(g, sign),
                device_id_type=MESH,
            )
            for g in range(8)
        ]

    def select(x):
        hi, lo = split(x)
        rows = onehot[1, 0:GHOSTS, :].astype(bf16)
        return mm(rows, hi) + mm(rows, lo)

    lane = lax.broadcasted_iota(jnp.int32, (8, ROWS), 1)
    group = lax.div(lane, 8)

    def merged(ref):
        total = jnp.where(group == 0, ref[0], 0.0)
        for g in range(1, 8):
            total = total + jnp.where(group == g, ref[g], 0.0)
        return total

    weights, at = [], 0
    for number, w in enumerate((w1i, w1o, wl, wr, w2i, w2o, wh)):
        place = out.at[0:F, at : at + w.shape[1]]
        weights.append((pltpu.make_async_copy(w, place, loads.at[number]), place))
        at += w.shape[1]
    for copy, _ in weights:
        copy.start()

    sndpad[...] = jnp.full((8, ROWS), -1, jnp.int32)
    sndpad[0:1, 0:GHOSTS] = snd[...]
    hot = jnp.where(
        lax.broadcasted_iota(jnp.int32, (ROWS, ROWS), 0) == sndpad[0:1, :], 1.0, 0.0
    )
    onehot[0] = hot
    onehot[1] = hot.T
    c8[...] = jnp.zeros((8, ROWS), f32)
    c8[0:3, :] = pos[...]
    c8[3:6, :] = tan[...]
    hi, mid, lo = split3(c8[...])
    hot16 = hot.astype(bf16)
    csel[...] = mm(hi, hot16) + (mm(mid, hot16) + mm(lo, hot16))
    sel1[...] = select(emb[...])
    pl.semaphore_wait(barrier, 8)
    coords = copies(csel, crecv, sendc, recvc, 1, True)
    first = copies(sel1, gemb, send1, recv1, 1, False)
    for copy in coords + first:
        copy.start()

    stores = ((w1i_s, 0), (w1o_s, 0), (wlr_s, 0), (wlr_s, F), (w2i_s, 0), (w2o_s, 0), (wh_s, 0))
    for (refs, at), (copy, place) in zip(stores, weights):
        copy.wait()
        hi, lo = split(place[...])
        refs[0, :, at : at + hi.shape[1]] = hi
        refs[1, :, at : at + hi.shape[1]] = lo

    row = lax.broadcasted_iota(jnp.int32, (ROWS, ROWS), 0)
    ghost = lax.rem(row, GHOSTS)
    for side, slots in ((0, row), (1, ROWS + (7 - lax.div(ghost, 8)) * 8 + lax.rem(ghost, 8))):

        def mark(k, total, slots=slots):
            return jnp.where(slots == nbr[pl.ds(k, 1), :], 1.0, total)

        listed = lax.fori_loop(0, nbr.shape[0], mark, jnp.zeros((ROWS, ROWS), f32))
        mask[side] = listed.T

    def project(rows, first_w, second_w):
        v = mm3(split(rows), first_w)
        return mm3(split(v * sigmoid(v)), second_w)

    w1 = (w1i_s[0], w1i_s[1]), (w1o_s[0], w1o_s[1])
    phi[0:ROWS, :] = project(emb[...], *w1)
    for j in range(6):
        colb[j] = jnp.broadcast_to(c8[j : j + 1, :], (ROWS, ROWS)).T

    for copy in coords + first:
        copy.wait()
    phi[ROWS:TABLE, :] = project(gemb[...], *w1)
    found = merged(crecv)
    twofold = found + pltpu.roll(found, GHOSTS, 1)
    csel2 = (c8[...], twofold)

    scale = 1.0 / math.sqrt(nbr.shape[0])

    def geometry(i, carry):
        rows = pl.ds(pl.multiple_of(i * 8, 8), 8)
        centre = [colb[j, rows, :] for j in range(6)]
        for side in range(2):
            table = csel2[side]
            off = [table[j : j + 1, :] - centre[j] for j in range(3)]
            vel = [table[j : j + 1, :] - centre[j] for j in range(3, 6)]
            listed = mask[side, rows, :]
            sq = off[0] * off[0] + off[1] * off[1] + off[2] * off[2]
            sq = jnp.where(listed > 0.0, sq, 1.0) + SOFT
            inv = lax.rsqrt(sq)
            inv = inv * (1.5 - 0.5 * sq * inv * inv)
            dist = sq * inv
            unit = [x * inv for x in off]
            rate = unit[0] * vel[0] + unit[1] * vel[1] + unit[2] * vel[2]
            s1, c1 = sin_cos(KAPPA * dist)
            weight = scale * listed
            env = 0.5 * (c1 + 1.0)
            env1 = (-0.5 * KAPPA) * s1
            env2 = (-0.5 * KAPPA * KAPPA) * c1
            e0 = weight * env * inv
            slope = env1 - env * inv
            e1 = weight * inv * slope
            e2 = weight * inv * (env2 - 2.0 * inv * slope)
            planes = [e0, e1, e2, rate, inv, s1, c1] + unit
            planes += [(vel[j] - unit[j] * rate) * inv for j in range(3)]
            for number, value in enumerate(planes):
                geo[side, number, rows, :] = value
        return carry

    lax.fori_loop(0, ROWS // 8, geometry, 0)

    def spread_table(refs, table, filters, at):
        def body(p, carry):
            for half in range(2):
                weights = filters[pl.ds(2 * p + half, 1), at : at + F]
                start = pl.multiple_of(p * SPAN + half * ROWS, ROWS)
                hi, lo = split(table(0, ROWS) * weights)
                refs[0, pl.ds(start, ROWS), :] = hi
                refs[1, pl.ds(start, ROWS), :] = lo
                start = pl.multiple_of(p * SPAN + 2 * ROWS + half * GHOSTS, GHOSTS)
                hi, lo = split(table(ROWS, GHOSTS) * weights)
                refs[0, pl.ds(start, GHOSTS), :] = hi
                refs[1, pl.ds(start, GHOSTS), :] = lo
            return carry

        lax.fori_loop(0, PAIRS, body, 0)

    spread_table(pfs_s, lambda at, n: phi[at : at + n, 0:F], f1, 0)
    spread_table(pfv_s, lambda at, n: phi[at : at + n, F : 2 * F], f1, F)

    def pair_rows(i, carry):
        start = pl.multiple_of(i * 16, 16)
        rows = pl.ds(start, 16)
        for side in range(2):
            g = [geo[side, number, rows, :] for number in range(13)]
            e1d, e0d = g[E1] * g[DD], g[E0] * g[DD]
            for at, a, s, c in WAVES[side](g[S1], g[C1]):
                cols = slice(at, at + ROWS)
                b = g[E0] * s
                bd = e1d * s + e0d * (a * c)
                put(lb, b, rows, cols)
                put(lb, bd, pl.ds(start + ROWS, 16), cols)
                for j in range(3):
                    put(lv, b * g[U0 + j], pl.ds(start + j * ROWS, 16), cols)
                    put(
                        lv,
                        bd * g[U0 + j] + b * g[W0 + j],
                        pl.ds(start + (3 + j) * ROWS, 16),
                        cols,
                    )
        return carry

    lax.fori_loop(0, ROWS // 16, pair_rows, 0)

    def gather_messages(target, left, rows, right):
        def body(i, carry):
            cols = pl.ds(pl.multiple_of(i * STEP, STEP), STEP)
            b = right[0, cols, :], right[1, cols, :]
            target[0:rows, :] += mm3((left[0][0:rows, cols], left[1][0:rows, cols]), b)
            return carry

        target[0:rows, :] = jnp.zeros((rows, F), f32)
        lax.fori_loop(0, STEPS, body, 0)

    gather_messages(acc, lv, 6 * ROWS, pfv_s)
    lr[...] = mm3(split(acc[...]), (wlr_s[0], wlr_s[1]))
    gather_messages(acc, lb, 2 * ROWS, pfs_s)

    def part(j, side):
        return lr[j * ROWS : (j + 1) * ROWS, side * F : (side + 1) * F]

    state = emb[...] + acc[0:ROWS, :]
    moved = acc[ROWS : 2 * ROWS, :]
    for j in range(3):
        state = state + part(j, 0) * part(j, 1)
        moved = moved + (part(3 + j, 0) * part(j, 1) + part(j, 0) * part(3 + j, 1))
    node[:, 0:F] = state
    node[:, F : 2 * F] = moved
    sel2[...] = select(node[...])
    second = copies(sel2, gnode, send2, recv2, 1, False)
    for copy in second:
        copy.start()

    w2 = (w2i_s[0], w2i_s[1]), (w2o_s[0], w2o_s[1])

    def table_two(values, moves, at, n):
        v = mm3(split(values), w2[0])
        vd = mm3(split(moves), w2[0])
        sig = sigmoid(v)
        pre2[0, at : at + n, :] = v
        pre2[1, at : at + n, :] = vd
        slope = sig * (1.0 + v * (1.0 - sig))
        phi2[0, at : at + n, :] = mm3(split(v * sig), w2[1])
        phi2[1, at : at + n, :] = mm3(split(slope * vd), w2[1])

    table_two(node[:, 0:F], node[:, F : 2 * F], 0, ROWS)

    for side in range(2):
        rows = ROWS if side == 0 else GHOSTS
        e0, e1, rate = (geo[side, number] for number in (E0, E1, DD))
        pg[side, 0] = e0.T
        pg[side, 1] = (e1 * rate).T
        pg[side, 2] = (e0 * rate).T
        pg[side, 3] = geo[side, S1].T
        pg[side, 4] = geo[side, C1].T

    def turned(side, count):
        def body(i, carry):
            start = pl.multiple_of(i * 16, 16)
            g = [pg[side, number, pl.ds(start, 16), :] for number in range(5)]
            for q, (at, a, s, c) in enumerate(own_waves(g[3], g[4])):
                cols = slice(q * ROWS, (q + 1) * ROWS)
                put(lt, g[0] * s, pl.ds(start + side * ROWS, 16), cols)
                put(
                    lt,
                    g[1] * s + g[2] * (a * c),
                    pl.ds(start + side * ROWS + TABLE, 16),
                    cols,
                )
            return carry

        lax.fori_loop(0, count // 16, body, 0)

    turned(0, ROWS)
    turned(1, GHOSTS)

    for copy in second:
        copy.wait()
    table_two(gnode[:, 0:F], gnode[:, F : 2 * F], ROWS, GHOSTS)
    spread_table(p2_s, lambda at, n: phi2[0, at : at + n, :], f2, 0)
    spread_table(p2d_s, lambda at, n: phi2[1, at : at + n, :], f2, 0)
    gather_messages(acc, lb, 2 * ROWS, p2_s)
    st = node[:, 0:F] + acc[0:ROWS, :]
    std = node[:, F : 2 * F] + acc[ROWS : 2 * ROWS, :]
    gather_messages(acc, lb, ROWS, p2d_s)
    std = std + acc[0:ROWS, :]

    whs = wh_s[0], wh_s[1]
    v = mm3(split(st), whs)
    vd = mm3(split(std), whs)
    sig = sigmoid(v)
    live = lax.broadcasted_iota(jnp.int32, (ROWS, F), 0) < cnt[0]
    top = jnp.where(live, jnp.broadcast_to(we[...], (ROWS, F)), 0.0)
    mu[0] = mm3(split(top * (sig * (1.0 + v * (1.0 - sig)))), whs, NT)
    mu[1] = mm3(
        split(top * (sig * (1.0 - sig) * (2.0 + v * (1.0 - 2.0 * sig))) * vd), whs, NT
    )

    for q in range(NR):
        weights = f2[q : q + 1, :]
        rows = slice(q % 4 * ROWS, (q % 4 + 1) * ROWS)
        for number in range(2):
            at = (number * NR // 4 + q // 4) * F
            put(lv, mu[number] * weights, rows, slice(at, at + F))
    bar[...] = jnp.zeros((2 * TABLE, F), f32)

    def turned_messages(i, carry):
        cols = pl.ds(pl.multiple_of(i * 512, 512), 512)
        place = pl.ds(pl.multiple_of(i * F, F), F)
        b = lvh[0 : 4 * ROWS, place], lvl[0 : 4 * ROWS, place]
        bar[...] += mm3((lth[:, cols], ltl[:, cols]), b)
        place = pl.ds(pl.multiple_of((NR // 4 + i) * F, F), F)
        b = lvh[0 : 4 * ROWS, place], lvl[0 : 4 * ROWS, place]
        bar[TABLE : 2 * TABLE, :] += mm3((lth[0:TABLE, cols], ltl[0:TABLE, cols]), b)
        return carry

    lax.fori_loop(0, NR * ROWS // 512, turned_messages, 0)
    back = mm3(split(bar[...]), w2[1], NT)
    v, vd = pre2[0], pre2[1]
    sig = sigmoid(v)
    slope = sig * (1.0 + v * (1.0 - sig))
    curve = sig * (1.0 - sig) * (2.0 + v * (1.0 - 2.0 * sig))
    bar[0:TABLE, :] = back[0:TABLE] * slope
    bar[TABLE : 2 * TABLE, :] = back[TABLE : 2 * TABLE] * slope + back[0:TABLE] * curve * vd
    bar[...] = mm3(split(bar[...]), w2[0], NT)
    src3[:, 0:F] = bar[ROWS:TABLE, :]
    src3[:, F : 2 * F] = bar[TABLE + ROWS : 2 * TABLE, :]
    third = copies(src3, rnode, send3, recv3, -1, False)
    for copy in third:
        copy.start()

    m = split(mu[0])
    md = split(mu[1])

    def pairs_two(i, carry):
        cols = pl.ds(pl.multiple_of(i * STEP, STEP), STEP)
        b = p2_s[0, cols, :], p2_s[1, cols, :]
        bd = p2d_s[0, cols, :], p2d_s[1, cols, :]
        out[0:ROWS, cols] = mm3(m, b, NT)
        out[ROWS : 2 * ROWS, cols] = mm3(md, b, NT) + mm3(m, bd, NT)
        return carry

    lax.fori_loop(0, STEPS, pairs_two, 0)

    for copy in third:
        copy.wait()
    rows_back = onehot[0, :, 0:GHOSTS].astype(bf16)
    hi, lo = split(rnode[...])
    returned = mm(rows_back, hi) + mm(rows_back, lo)
    nu = mu[0] + bar[0:ROWS, :] + returned[:, 0:F]
    nud = mu[1] + bar[TABLE : TABLE + ROWS, :] + returned[:, F : 2 * F]
    mu[0] = nu
    mu[1] = nud

    wlr = wlr_s[0], wlr_s[1]
    for j in range(3):
        nu, nud = mu[0], mu[1]
        l, r, ld, rd = part(j, 0), part(j, 1), part(3 + j, 0), part(3 + j, 1)
        lr[j * ROWS : (j + 1) * ROWS, 0:F] = nu * r
        lr[j * ROWS : (j + 1) * ROWS, F : 2 * F] = nu * l
        lr[(3 + j) * ROWS : (4 + j) * ROWS, 0:F] = nud * r + nu * rd
        lr[(3 + j) * ROWS : (4 + j) * ROWS, F : 2 * F] = nud * l + nu * ld
    acc[...] = mm3(split(lr[...]), wlr, NT)
    n = split(jnp.concatenate([mu[0], mu[1]], 0))
    vb = split(acc[...])
    lvb = lv[0].at[:, 0:F], lv[1].at[:, 0:F]
    lvb[0][...] = vb[0]
    lvb[1][...] = vb[1]

    def pairs_one(i, carry):
        cols = pl.ds(pl.multiple_of(i * STEP, STEP), STEP)
        out[0 : 2 * ROWS, cols] += mm3(n, (pfs_s[0, cols, :], pfs_s[1, cols, :]), NT)
        out[2 * ROWS :, cols] = mm3(
            (lvb[0][...], lvb[1][...]), (pfv_s[0, cols, :], pfv_s[1, cols, :]), NT
        )
        return carry

    lax.fori_loop(0, STEPS, pairs_one, 0)

    def offsets_back(i, carry):
        start = pl.multiple_of(i * 8, 8)
        rows = pl.ds(start, 8)
        for side in range(2):
            zero = jnp.zeros((8, ROWS), f32)
            z = [[zero] * 4 for _ in range(3)]
            zd = [[zero] * 4 for _ in range(2)]
            for at, a, s, c in WAVES[side](geo[side, S1, rows, :], geo[side, C1, rows, :]):
                cols = slice(at, at + ROWS)
                ac = a * c
                aas = a * (a * s)
                for k in range(4):
                    y = out[pl.ds(start + (0 if k == 3 else 2 + k) * ROWS, 8), cols]
                    yd = out[pl.ds(start + (1 if k == 3 else 5 + k) * ROWS, 8), cols]
                    z[0][k] = z[0][k] + s * y
                    z[1][k] = z[1][k] + ac * y
                    z[2][k] = z[2][k] + aas * y
                    zd[0][k] = zd[0][k] + s * yd
                    zd[1][k] = zd[1][k] + ac * yd
            e0, e1, e2, rate, inv = (geo[side, number, rows, :] for number in range(5))
            unit = [geo[side, U0 + j, rows, :] for j in range(3)]
            turn = [geo[side, W0 + j, rows, :] for j in range(3)]
            a_, ad, ub, ubd = [], [], [], []
            for k in range(4):
                first_d = e1 * z[0][k] + e0 * z[1][k]
                second_d = e2 * z[0][k] + 2.0 * e1 * z[1][k] - e0 * z[2][k]
                a_.append(first_d)
                ad.append(rate * second_d + e1 * zd[0][k] + e0 * zd[1][k])
                if k < 3:
                    ub.append(e0 * z[0][k])
                    ubd.append(rate * first_d + e0 * zd[0][k])
            db, dbd, w, wd = a_[3], ad[3], zero, zero
            for j in range(3):
                db = db + unit[j] * a_[j]
                dbd = dbd + turn[j] * a_[j] + unit[j] * ad[j]
                w = w + unit[j] * ub[j]
                wd = wd + turn[j] * ub[j] + unit[j] * ubd[j]
            for j in range(3):
                t = (ub[j] - unit[j] * w) * inv
                pg[side, j, rows, :] = db * unit[j] + t
                pg[side, 3 + j, rows, :] = (
                    dbd * unit[j]
                    + db * turn[j]
                    + (ubd[j] - turn[j] * w - unit[j] * wd - t * rate) * inv
                )
        return carry

    lax.fori_loop(0, ROWS // 8, offsets_back, 0)

    gpos[...] = jnp.zeros((8, ROWS), f32)
    c8[...] = jnp.zeros((8, ROWS), f32)
    for j in range(6):
        ghosts = pg[1, j]
        own = pg[0, j]
        halves = jnp.sum(ghosts, axis=0, keepdims=True)
        gpos[j : j + 1, :] = halves
        c8[j : j + 1, :] = jnp.sum(own - own.T - ghosts.T, axis=0, keepdims=True)
    both = gpos[...]
    gpos[...] = both + pltpu.roll(both, GHOSTS, 1)
    last = copies(gpos, rpos, send4, recv4, -1, True)
    for copy in last:
        copy.start()
    for copy in last:
        copy.wait()
    hi, mid, lo = split3(merged(rpos))
    slots = onehot[1].astype(bf16)
    total = c8[...] + (mm(hi, slots) + (mm(mid, slots) + mm(lo, slots)))
    force[...] = -total[0:3, :]
    hess[...] = -total[3:6, :]


def per_device(nx, ny, *arrays):
    arrays = list(arrays)
    arrays[15] = arrays[15].reshape(1, F)
    vmem = pl.BlockSpec(memory_space=pltpu.VMEM)
    in_specs = [vmem] * 16
    in_specs[3] = pl.BlockSpec(memory_space=pltpu.SMEM)
    for number in (6, 7, 9, 10, 11, 12, 14):
        in_specs[number] = pl.BlockSpec(memory_space=pl.ANY)

    def v32(*shape):
        return pltpu.VMEM(shape, f32)

    def v16(*shape):
        return pltpu.VMEM(shape, bf16)

    dma = pltpu.SemaphoreType.DMA((8,))
    scratch = [
        v16(2, F, F),
        v16(2, F, 2 * F),
        v16(2, F, 2 * F),
        v16(2, F, F),
        v16(2, F, F),
        v16(2, F, F),
        pltpu.VMEM((8, ROWS), jnp.int32),
        v32(8, ROWS),
        v32(8, ROWS),
        v32(8, 8, ROWS),
        v32(GHOSTS, F),
        v32(GHOSTS, F),
        v32(GHOSTS, 2 * F),
        v32(GHOSTS, 2 * F),
        v32(GHOSTS, 2 * F),
        v32(GHOSTS, 2 * F),
        v32(8, ROWS),
        v32(8, 8, ROWS),
        v32(2, ROWS, ROWS),
        v32(2, ROWS, ROWS),
        v32(6, ROWS, ROWS),
        v32(2, 13, ROWS, ROWS),
        v16(2 * ROWS, WIDE),
        v16(2 * ROWS, WIDE),
        v16(6 * ROWS, WIDE),
        v16(6 * ROWS, WIDE),
        v16(2 * TABLE, NR * ROWS),
        v16(2 * TABLE, NR * ROWS),
        v16(2, WIDE, F),
        v16(2, WIDE, F),
        v16(2, WIDE, F),
        v16(2, WIDE, F),
        v32(TABLE, 2 * F),
        v32(6 * ROWS, F),
        v32(6 * ROWS, 2 * F),
        v32(ROWS, 2 * F),
        v32(2, TABLE, F),
        v32(2, TABLE, F),
        v32(2, ROWS, F),
        v32(2 * TABLE, F),
        v32(8 * ROWS, WIDE),
        v32(2, 6, ROWS, ROWS),
    ] + [dma] * 11
    out = jax.ShapeDtypeStruct((3, ROWS), f32)
    return pl.pallas_call(
        functools.partial(kernel, nx, ny),
        out_shape=(out, out),
        in_specs=in_specs,
        out_specs=(vmem, vmem),
        scratch_shapes=scratch,
        compiler_params=pltpu.CompilerParams(
            collective_id=0, has_side_effects=True, vmem_limit_bytes=67043328
        ),
    )(*arrays)


def solution(mesh):
    placed = (
        P(None, ("bx", "by")),
        P(None, ("bx", "by")),
        P(("bx", "by"), None),
        P(("bx", "by")),
        P(None, ("bx", "by")),
        P(("bx", "by"), None),
    ) + (P(),) * 10
    return jax.shard_map(
        functools.partial(per_device, mesh.shape["bx"], mesh.shape["by"]),
        mesh=mesh,
        in_specs=placed,
        out_specs=(P(None, ("bx", "by")), P(None, ("bx", "by"))),
        check_vma=False,
    )
```

```python
import functools
import math

import jax
import jax.numpy as jnp
from jax import lax
from jax.experimental import pallas as pl
from jax.experimental.pallas import tpu as pltpu
from jax.sharding import PartitionSpec as P

MESH = pl.DeviceIdType.MESH
f32 = jnp.float32
bf16 = jnp.bfloat16
offsets = ((-1, -1), (-1, 0), (-1, 1), (0, -1), (0, 1), (1, -1), (1, 0), (1, 1))
NN = (((1,), (0,)), ((), ()))
NT = (((1,), (1,)), ((), ()))
KAPPA = math.pi / 3.0
SOFT = 0.01
ROWS = 128
GHOSTS = 64
TABLE = ROWS + GHOSTS
F = 256
NR = 20
PAIRS = NR // 2
TILE = 256
TILES = NR * TABLE // TILE
WIDE = TILES * TILE
STEP = 3 * TILE
STEPS = WIDE // STEP


def split(x):
    hi = x.astype(bf16)
    return hi, (x - hi.astype(f32)).astype(bf16)


def split3(x):
    hi = x.astype(bf16)
    rest = x - hi.astype(f32)
    mid = rest.astype(bf16)
    return hi, mid, (rest - mid.astype(f32)).astype(bf16)


def mm(a, b, dims=NN):
    return lax.dot_general(a, b, dims, preferred_element_type=f32)


def mm3(a, b, dims=NN):
    return mm(a[0], b[0], dims) + (mm(a[1], b[0], dims) + mm(a[0], b[1], dims))


def pick(refs, *index):
    return refs[0][index], refs[1][index]


def put(refs, value, *index):
    hi, lo = split(value)
    refs[0][index] = hi
    refs[1][index] = lo


def sin_cos(angle):
    turns = jnp.floor(angle * (0.5 / math.pi) + 0.5)
    half = 0.5 * ((angle - turns * 6.28125) - turns * (2.0 * math.pi - 6.28125))
    sq = half * half
    odd = 1.0 / 39916800.0
    for c in (1.0 / 362880.0, 1.0 / 5040.0, 1.0 / 120.0, 1.0 / 6.0, 1.0):
        odd = c - sq * odd
    sh = half * odd
    even = 1.0 / 479001600.0
    for c in (1.0 / 3628800.0, 1.0 / 40320.0, 1.0 / 720.0, 1.0 / 24.0, 0.5, 1.0):
        even = c - sq * even
    return 2.0 * sh * even, 1.0 - 2.0 * sh * sh


def sigmoid(v):
    return 1.0 / (1.0 + jnp.exp(-v))


def own_waves(s1, c1):
    twice = 2.0 * c1
    before_s, before_c = jnp.zeros_like(s1), jnp.ones_like(c1)
    s, c = s1, c1
    for q in range(NR):
        yield (q + 1) * KAPPA, s, c
        if q < NR - 1:
            s, before_s = twice * s - before_s, s
            c, before_c = twice * c - before_c, c


def ghost_waves(s1, c1):
    upper = lax.broadcasted_iota(jnp.int32, s1.shape, 1) >= GHOSTS
    s2, c2 = 2.0 * s1 * c1, 1.0 - 2.0 * s1 * s1
    twice = 2.0 * c2
    s, before_s = jnp.where(upper, s2, s1), jnp.where(upper, 0.0, -s1)
    c, before_c = jnp.where(upper, c2, c1), jnp.where(upper, 1.0, c1)
    shift = jnp.where(upper, 2.0 * KAPPA, KAPPA)
    for p in range(PAIRS):
        yield shift + 2.0 * p * KAPPA, s, c
        if p < PAIRS - 1:
            s, before_s = twice * s - before_s, s
            c, before_c = twice * c - before_c, c


E0, E1, E2, DD, IV, S1, C1, U0, W0 = 0, 1, 2, 3, 4, 5, 6, 7, 10
WAVES = (own_waves, ghost_waves)


def kernel(
    nx,
    ny,
    pos,
    tan,
    emb,
    cnt,
    nbr,
    snd,
    w1i,
    w1o,
    f1,
    wl,
    wr,
    w2i,
    w2o,
    f2,
    wh,
    we,
    force,
    hess,
    w1i_s,
    w1o_s,
    wlr_s,
    w2i_s,
    w2o_s,
    wh_s,
    sndpad,
    c8,
    csel,
    crecv,
    sel1,
    gemb,
    sel2,
    gnode,
    src3,
    rnode,
    gpos,
    rpos,
    onehot,
    mask,
    colb,
    geo,
    waves,
    lb,
    lv0,
    lv1,
    lt,
    pfs_s,
    pfv_s,
    p2_s,
    p2d_s,
    muf0,
    muf1,
    phi,
    acc,
    accv,
    lr,
    node,
    pre2,
    phi2,
    mu,
    bar,
    out0,
    out1,
    landing,
    two,
    sums,
    vbar,
    nus,
    pg,
    send1,
    recv1,
    sendc,
    recvc,
    send2,
    recv2,
    send3,
    recv3,
    send4,
    recv4,
    loads,
):
    ix, iy = lax.axis_index("bx"), lax.axis_index("by")

    def device(g, sign):
        dx, dy = offsets[g]
        return (lax.rem(ix + sign * dx + nx, nx), lax.rem(iy + sign * dy + ny, ny))

    barrier = pltpu.get_barrier_semaphore()
    for g in range(8):
        pl.semaphore_signal(barrier, inc=1, device_id=device(g, 1), device_id_type=MESH)

    def block(ref, g):
        return ref.at[pl.ds(g * 8, 8), :]

    def copies(source, target, sends, recvs, sign, whole):
        return [
            pltpu.make_async_remote_copy(
                src_ref=source if whole else block(source, g),
                dst_ref=target.at[g] if whole else block(target, g),
                send_sem=sends.at[g],
                recv_sem=recvs.at[g],
                device_id=device(g, sign),
                device_id_type=MESH,
            )
            for g in range(8)
        ]

    def select(x):
        hi, lo = split(x)
        rows = onehot[1, 0:GHOSTS, :].astype(bf16)
        return mm(rows, hi) + mm(rows, lo)

    lane = lax.broadcasted_iota(jnp.int32, (8, ROWS), 1)
    group = lax.div(lane, 8)

    def merged(ref):
        total = jnp.where(group == 0, ref[0], 0.0)
        for g in range(1, 8):
            total = total + jnp.where(group == g, ref[g], 0.0)
        return total

    weights = []
    spots = ((0, 0), (0, F), (1, 0), (1, F), (1, 2 * F), (2, 0), (2, F))
    for number, (w, (down, at)) in enumerate(zip((w1i, w1o, wl, wr, w2i, w2o, wh), spots)):
        place = landing.at[down * F : (down + 1) * F, at : at + w.shape[1]]
        weights.append((pltpu.make_async_copy(w, place, loads.at[number]), place))
    for copy, _ in weights:
        copy.start()

    sndpad[...] = jnp.full((8, ROWS), -1, jnp.int32)
    sndpad[0:1, 0:GHOSTS] = snd[...]
    hot = jnp.where(
        lax.broadcasted_iota(jnp.int32, (ROWS, ROWS), 0) == sndpad[0:1, :], 1.0, 0.0
    )
    onehot[0] = hot
    onehot[1] = hot.T
    c8[...] = jnp.zeros((8, ROWS), f32)
    c8[0:3, :] = pos[...]
    c8[3:6, :] = tan[...]
    hi, mid, lo = split3(c8[...])
    hot16 = hot.astype(bf16)
    csel[...] = mm(hi, hot16) + (mm(mid, hot16) + mm(lo, hot16))
    sel1[...] = select(emb[...])
    pl.semaphore_wait(barrier, 8)
    coords = copies(csel, crecv, sendc, recvc, 1, True)
    first = copies(sel1, gemb, send1, recv1, 1, False)
    for copy in coords + first:
        copy.start()

    stores = ((w1i_s, 0), (w1o_s, 0), (wlr_s, 0), (wlr_s, F), (w2i_s, 0), (w2o_s, 0), (wh_s, 0))
    for (refs, at), (copy, place) in zip(stores, weights):
        copy.wait()
        hi, lo = split(place[...])
        refs[0, :, at : at + hi.shape[1]] = hi
        refs[1, :, at : at + hi.shape[1]] = lo

    row = lax.broadcasted_iota(jnp.int32, (ROWS, ROWS), 0)
    ghost = lax.rem(row, GHOSTS)
    for side, slots in ((0, row), (1, ROWS + (7 - lax.div(ghost, 8)) * 8 + lax.rem(ghost, 8))):

        def mark(k, total, slots=slots):
            return jnp.where(slots == nbr[pl.ds(k, 1), :], 1.0, total)

        listed = lax.fori_loop(0, nbr.shape[0], mark, jnp.zeros((ROWS, ROWS), f32))
        mask[side] = listed.T

    def project(rows, first_w, second_w):
        v = mm3(split(rows), first_w)
        return mm3(split(v * sigmoid(v)), second_w)

    w1 = (w1i_s[0], w1i_s[1]), (w1o_s[0], w1o_s[1])
    phi[0:ROWS, :] = project(emb[...], *w1)
    for j in range(6):
        colb[j] = jnp.broadcast_to(c8[j : j + 1, :], (ROWS, ROWS)).T

    def put2(refs, value, start):
        hi, lo = split(value)
        refs[0, pl.ds(start, value.shape[0]), :] = hi
        refs[1, pl.ds(start, value.shape[0]), :] = lo

    def spread_own(refs, table, filters, at):
        def body(q, carry):
            weights = filters[pl.ds(q, 1), at : at + F]
            put2(refs, table() * weights, pl.multiple_of(q * ROWS, ROWS))
            return carry

        lax.fori_loop(0, NR, body, 0)

    def spread_ghosts(refs, table, filters, at):
        def body(q, carry):
            weights = filters[pl.ds(q, 1), at : at + F]
            put2(refs, table() * weights, pl.multiple_of(NR * ROWS + q * GHOSTS, GHOSTS))
            return carry

        lax.fori_loop(0, NR, body, 0)

    def put_rows(ref, value, first, second, cols):
        hi, lo = split(value)
        ref[first : first + 16, cols] = hi
        ref[second : second + 16, cols] = lo

    spread_own(pfs_s, lambda: phi[0:ROWS, 0:F], f1, 0)
    spread_own(pfv_s, lambda: phi[0:ROWS, F : 2 * F], f1, F)

    for copy in coords + first:
        copy.wait()
    phi[ROWS:TABLE, :] = project(gemb[...], *w1)
    found = merged(crecv)
    twofold = found + pltpu.roll(found, GHOSTS, 1)
    csel2 = (c8[...], twofold)

    spread_ghosts(pfs_s, lambda: phi[ROWS:TABLE, 0:F], f1, 0)
    spread_ghosts(pfv_s, lambda: phi[ROWS:TABLE, F : 2 * F], f1, F)

    scale = 1.0 / math.sqrt(nbr.shape[0])

    def geometry(i, carry):
        rows = pl.ds(pl.multiple_of(i * 8, 8), 8)
        centre = [colb[j, rows, :] for j in range(6)]
        for side in range(2):
            table = csel2[side]
            off = [table[j : j + 1, :] - centre[j] for j in range(3)]
            vel = [table[j : j + 1, :] - centre[j] for j in range(3, 6)]
            listed = mask[side, rows, :]
            sq = off[0] * off[0] + off[1] * off[1] + off[2] * off[2]
            sq = jnp.where(listed > 0.0, sq, 1.0) + SOFT
            inv = lax.rsqrt(sq)
            inv = inv * (1.5 - 0.5 * sq * inv * inv)
            dist = sq * inv
            unit = [x * inv for x in off]
            rate = unit[0] * vel[0] + unit[1] * vel[1] + unit[2] * vel[2]
            s1, c1 = sin_cos(KAPPA * dist)
            weight = scale * listed
            env = 0.5 * (c1 + 1.0)
            env1 = (-0.5 * KAPPA) * s1
            env2 = (-0.5 * KAPPA * KAPPA) * c1
            e0 = weight * env * inv
            slope = env1 - env * inv
            e1 = weight * inv * slope
            e2 = weight * inv * (env2 - 2.0 * inv * slope)
            planes = [e0, e1, e2, rate, inv, s1, c1] + unit
            planes += [(vel[j] - unit[j] * rate) * inv for j in range(3)]
            for number, value in enumerate(planes):
                geo[side, number, rows, :] = value
            for number, (a, s, c) in enumerate(WAVES[side](s1, c1)):
                waves[0, side * NR + number, rows, :] = s
                waves[1, side * NR + number, rows, :] = a * c
        return carry

    lax.fori_loop(0, ROWS // 8, geometry, 0)

    lv = (lv0, lv1)

    def build_pairs(m, target):
        side = jnp.where(m < PAIRS, 0, 1)
        cols = pl.ds(pl.multiple_of(m * TILE, TILE), TILE)
        for start in range(0, ROWS, 16):
            rows = slice(start, start + 16)

            def twice(x):
                return jnp.concatenate([x, x], 1)

            e0, e1, rate = (geo[side, number, rows, :] for number in (E0, E1, DD))
            e1d, e0d = twice(e1 * rate), twice(e0 * rate)
            s = jnp.concatenate([waves[0, 2 * m + half, rows, :] for half in range(2)], 1)
            ac = jnp.concatenate([waves[1, 2 * m + half, rows, :] for half in range(2)], 1)
            b = twice(e0) * s
            bd = e1d * s + e0d * ac
            put_rows(lb, bd, start, start + 3 * ROWS, cols)
            put_rows(lb, b, start + ROWS, start + 2 * ROWS, cols)
            for j in range(3):
                u, w = twice(geo[side, U0 + j, rows, :]), twice(geo[side, W0 + j, rows, :])
                first = start + j * ROWS
                put_rows(target, b * u, first, first + 6 * ROWS, slice(None))
                first += 3 * ROWS
                put_rows(target, bd * u + b * w, first, first + 6 * ROWS, slice(None))

    def add_to(ref, rows, value, i):
        if i == 0:
            ref[rows, :] = value
        else:
            ref[rows, :] += value

    def gather_scalar(refs, cols):
        both = mm(lb[:, cols], refs[0, cols, :])
        rest = mm(lb[0 : 2 * ROWS, cols], refs[1, cols, :])
        acc[0:ROWS, :] += both[ROWS : 2 * ROWS] + both[2 * ROWS : 3 * ROWS] + rest[ROWS:]
        acc[ROWS : 2 * ROWS, :] += both[0:ROWS] + both[3 * ROWS :] + rest[0:ROWS]

    def gather_vector(m, near):
        cols = pl.ds(pl.multiple_of(m * TILE, TILE), TILE)
        both = mm(near[...], pfv_s[0, cols, :])
        rest = mm(near[0 : 6 * ROWS, :], pfv_s[1, cols, :])
        accv[...] += both[0 : 6 * ROWS] + both[6 * ROWS :] + rest

    acc[...] = jnp.zeros((2 * ROWS, F), f32)
    accv[...] = jnp.zeros((6 * ROWS, F), f32)
    build_pairs(0, lv0)

    def two_tiles(k, carry):
        for half in range(2):
            gather_vector(2 * k + half, lv[half])
            build_pairs(2 * k + half + 1, lv[1 - half])
        return carry

    lax.fori_loop(0, TILES // 2, two_tiles, 0)
    gather_vector(TILES - 1, lv0)

    def scalar_step(i, carry):
        gather_scalar(pfs_s, pl.ds(pl.multiple_of(i * STEP, STEP), STEP))
        return carry

    lax.fori_loop(0, STEPS, scalar_step, 0)
    lr[...] = mm3(split(accv[...]), (wlr_s[0], wlr_s[1]))

    def part(j, side):
        return lr[j * ROWS : (j + 1) * ROWS, side * F : (side + 1) * F]

    state = emb[...] + acc[0:ROWS, :]
    moved = acc[ROWS : 2 * ROWS, :]
    for j in range(3):
        state = state + part(j, 0) * part(j, 1)
        moved = moved + (part(3 + j, 0) * part(j, 1) + part(j, 0) * part(3 + j, 1))
    node[:, 0:F] = state
    node[:, F : 2 * F] = moved
    sel2[...] = select(node[...])
    second = copies(sel2, gnode, send2, recv2, 1, False)
    for copy in second:
        copy.start()

    w2 = (w2i_s[0], w2i_s[1]), (w2o_s[0], w2o_s[1])

    def table_two(values, moves, at, n):
        v = mm3(split(values), w2[0])
        vd = mm3(split(moves), w2[0])
        sig = sigmoid(v)
        pre2[0, at : at + n, :] = v
        pre2[1, at : at + n, :] = vd
        slope = sig * (1.0 + v * (1.0 - sig))
        phi2[0, at : at + n, :] = mm3(split(v * sig), w2[1])
        phi2[1, at : at + n, :] = mm3(split(slope * vd), w2[1])

    table_two(node[:, 0:F], node[:, F : 2 * F], 0, ROWS)

    for side in range(2):
        rows = ROWS if side == 0 else GHOSTS
        e0, e1, rate = (geo[side, number] for number in (E0, E1, DD))
        pg[side, 0] = e0.T
        pg[side, 1] = (e1 * rate).T
        pg[side, 2] = (e0 * rate).T
        pg[side, 3] = geo[side, S1].T
        pg[side, 4] = geo[side, C1].T

    def turned(side, count):
        def body(i, carry):
            start = pl.multiple_of(i * 16, 16)
            g = [pg[side, number, pl.ds(start, 16), :] for number in range(5)]
            held = None
            for q, (a, s, c) in enumerate(own_waves(g[3], g[4])):
                new = (g[0] * s, g[1] * s + g[2] * (a * c))
                if q % 2 == 0:
                    held = new
                    continue
                cols = slice((q - 1) * ROWS, (q + 1) * ROWS)
                for value, first, second in ((1, 0, 3), (0, 1, 2)):
                    hi, lo = split(jnp.concatenate([held[value], new[value]], 1))
                    lt[pl.ds(start + side * ROWS + first * TABLE, 16), cols] = hi
                    lt[pl.ds(start + side * ROWS + second * TABLE, 16), cols] = lo
            return carry

        lax.fori_loop(0, count // 16, body, 0)

    turned(0, ROWS)
    turned(1, GHOSTS)

    spread_own(p2_s, lambda: phi2[0, 0:ROWS, :], f2, 0)
    spread_own(p2d_s, lambda: phi2[1, 0:ROWS, :], f2, 0)

    for copy in second:
        copy.wait()
    table_two(gnode[:, 0:F], gnode[:, F : 2 * F], ROWS, GHOSTS)
    spread_ghosts(p2_s, lambda: phi2[0, ROWS:TABLE, :], f2, 0)
    spread_ghosts(p2d_s, lambda: phi2[1, ROWS:TABLE, :], f2, 0)
    acc[...] = jnp.zeros((2 * ROWS, F), f32)

    def messages_two(i, carry):
        cols = pl.ds(pl.multiple_of(i * STEP, STEP), STEP)
        gather_scalar(p2_s, cols)
        both = mm(lb[ROWS : 3 * ROWS, cols], p2d_s[0, cols, :])
        rest = mm(lb[ROWS : 2 * ROWS, cols], p2d_s[1, cols, :])
        acc[ROWS : 2 * ROWS, :] += both[0:ROWS] + both[ROWS:] + rest
        return carry

    lax.fori_loop(0, STEPS, messages_two, 0)
    st = node[:, 0:F] + acc[0:ROWS, :]
    std = node[:, F : 2 * F] + acc[ROWS : 2 * ROWS, :]

    whs = wh_s[0], wh_s[1]
    v = mm3(split(st), whs)
    vd = mm3(split(std), whs)
    sig = sigmoid(v)
    live = lax.broadcasted_iota(jnp.int32, (ROWS, F), 0) < cnt[0]
    top = jnp.where(live, jnp.broadcast_to(we[...], (ROWS, F)), 0.0)
    mu[0] = mm3(split(top * (sig * (1.0 + v * (1.0 - sig)))), whs, NT)
    mu[1] = mm3(
        split(top * (sig * (1.0 - sig) * (2.0 + v * (1.0 - 2.0 * sig))) * vd), whs, NT
    )

    muf = (muf0, muf1)

    def scaled(i):
        for q in range(4 * i, 4 * i + 4):
            weights = f2[q : q + 1, :]
            rows = slice(q % 4 * ROWS, (q % 4 + 1) * ROWS)
            for number in range(2):
                hi, lo = split(mu[number] * weights)
                muf[i % 2][2 * number, rows, :] = hi
                muf[i % 2][2 * number + 1, rows, :] = lo

    def turned_messages(i):
        cols = slice(i * 4 * ROWS, (i + 1) * 4 * ROWS)
        right = muf[i % 2]
        both = mm(lt[:, cols], right[0])
        rest = mm(lt[0 : 2 * TABLE, cols], right[1])
        also = mm(lt[TABLE : 3 * TABLE, cols], right[2])
        more = mm(lt[TABLE : 2 * TABLE, cols], right[3])
        add_to(
            bar,
            slice(0, TABLE),
            both[TABLE : 2 * TABLE] + both[2 * TABLE : 3 * TABLE] + rest[TABLE:],
            i,
        )
        add_to(
            bar,
            slice(TABLE, 2 * TABLE),
            (both[0:TABLE] + both[3 * TABLE :] + rest[0:TABLE])
            + (also[0:TABLE] + also[TABLE:] + more),
            i,
        )

    for i in range(NR // 4 + 1):
        if i < NR // 4:
            scaled(i)
        if i > 0:
            turned_messages(i - 1)
    back = mm3(split(bar[...]), w2[1], NT)
    v, vd = pre2[0], pre2[1]
    sig = sigmoid(v)
    slope = sig * (1.0 + v * (1.0 - sig))
    curve = sig * (1.0 - sig) * (2.0 + v * (1.0 - 2.0 * sig))
    bar[0:TABLE, :] = back[0:TABLE] * slope
    bar[TABLE : 2 * TABLE, :] = back[TABLE : 2 * TABLE] * slope + back[0:TABLE] * curve * vd
    bar[...] = mm3(split(bar[...]), w2[0], NT)
    src3[:, 0:F] = bar[ROWS:TABLE, :]
    src3[:, F : 2 * F] = bar[TABLE + ROWS : 2 * TABLE, :]
    third = copies(src3, rnode, send3, recv3, -1, False)
    for copy in third:
        copy.start()

    m = split(mu[0])
    md = split(mu[1])
    high = jnp.concatenate([m[0], md[0]], 0)
    full = jnp.concatenate([high, m[1], md[1]], 0)
    ours = jnp.concatenate(m, 0)

    def pairs_two(i, carry):
        cols = pl.ds(pl.multiple_of(i * STEP, STEP), STEP)
        both = mm(full, p2_s[0, cols, :], NT)
        rest = mm(high, p2_s[1, cols, :], NT)
        also = mm(ours, p2d_s[0, cols, :], NT)
        more = mm(m[0], p2d_s[1, cols, :], NT)
        two[0:ROWS, cols] = both[0:ROWS] + both[2 * ROWS : 3 * ROWS] + rest[0:ROWS]
        two[ROWS : 2 * ROWS, cols] = (
            both[ROWS : 2 * ROWS] + both[3 * ROWS :] + rest[ROWS:]
        ) + (also[0:ROWS] + also[ROWS:] + more)
        return carry

    lax.fori_loop(0, STEPS, pairs_two, 0)

    for copy in third:
        copy.wait()
    rows_back = onehot[0, :, 0:GHOSTS].astype(bf16)
    hi, lo = split(rnode[...])
    returned = mm(rows_back, hi) + mm(rows_back, lo)
    nu = mu[0] + bar[0:ROWS, :] + returned[:, 0:F]
    nud = mu[1] + bar[TABLE : TABLE + ROWS, :] + returned[:, F : 2 * F]
    mu[0] = nu
    mu[1] = nud

    wlr = wlr_s[0], wlr_s[1]
    for j in range(3):
        nu, nud = mu[0], mu[1]
        l, r, ld, rd = part(j, 0), part(j, 1), part(3 + j, 0), part(3 + j, 1)
        lr[j * ROWS : (j + 1) * ROWS, 0:F] = nu * r
        lr[j * ROWS : (j + 1) * ROWS, F : 2 * F] = nu * l
        lr[(3 + j) * ROWS : (4 + j) * ROWS, 0:F] = nud * r + nu * rd
        lr[(3 + j) * ROWS : (4 + j) * ROWS, F : 2 * F] = nud * l + nu * ld
    hi, lo = split(mm3(split(lr[...]), wlr, NT))
    vbar[0 : 6 * ROWS, :] = hi
    vbar[6 * ROWS :, :] = lo
    for number in range(2):
        hi, lo = split(mu[number])
        nus[number * ROWS : (number + 1) * ROWS, :] = hi
        nus[(2 + number) * ROWS : (3 + number) * ROWS, :] = lo
    out = (out0, out1)

    def pairs_one(m, target):
        cols = pl.ds(pl.multiple_of(m * TILE, TILE), TILE)
        both = mm(nus[...], pfs_s[0, cols, :], NT)
        rest = mm(nus[0 : 2 * ROWS, :], pfs_s[1, cols, :], NT)
        target[0 : 2 * ROWS, :] = two[:, cols] + (both[0 : 2 * ROWS] + both[2 * ROWS :] + rest)
        both = mm(vbar[...], pfv_s[0, cols, :], NT)
        rest = mm(vbar[0 : 6 * ROWS, :], pfv_s[1, cols, :], NT)
        target[2 * ROWS :, :] = both[0 : 6 * ROWS] + both[6 * ROWS :] + rest

    upper = lax.broadcasted_iota(jnp.int32, (8, ROWS), 1) >= GHOSTS

    def sum_waves(m, source):
        side = jnp.where(m < PAIRS, 0, 1)
        base = jnp.where(m < PAIRS, 2 * m + 1, 4 * (m - PAIRS) + 1).astype(f32)
        jump = jnp.where(m < PAIRS, 1.0, 2.0)
        ghosts_on = jnp.where(m < PAIRS, 0.0, 1.0)
        a = [
            KAPPA * (base + half * jump + ghosts_on * jnp.where(upper, 1.0, 0.0))
            for half in range(2)
        ]
        aa = [x * x for x in a]
        for start in range(0, ROWS, 8):
            rows = slice(start, start + 8)
            u = [geo[side, U0 + j, rows, :] for j in range(3)]
            total = [sums[side, number, rows, :] for number in range(14)]
            for half in range(2):
                s = waves[0, 2 * m + half, rows, :]
                ac = waves[1, 2 * m + half, rows, :]
                ss = s * aa[half]
                cols = slice(half * ROWS, (half + 1) * ROWS)
                y = [source[start + k * ROWS : start + k * ROWS + 8, cols] for k in range(8)]
                along = y[0] + u[0] * y[2] + u[1] * y[3] + u[2] * y[4]
                along_d = y[1] + u[0] * y[5] + u[1] * y[6] + u[2] * y[7]
                for j in range(3):
                    total[j] += s * y[2 + j]
                    total[3 + j] += ac * y[2 + j]
                    total[6 + j] += s * y[5 + j]
                total[9] += s * y[0]
                total[10] += ac * y[0]
                total[11] += ss * along
                total[12] += s * y[1]
                total[13] += ac * along_d
            for number in range(14):
                sums[side, number, rows, :] = total[number]

    sums[...] = jnp.zeros(sums.shape, f32)
    pairs_one(0, out0)

    def two_sums(k, carry):
        for half in range(2):
            pairs_one(2 * k + half + 1, out[1 - half])
            sum_waves(2 * k + half, out[half])
        return carry

    lax.fori_loop(0, TILES // 2, two_sums, 0)
    sum_waves(TILES - 1, out0)

    def offsets_back(i, carry):
        rows = pl.ds(pl.multiple_of(i * 8, 8), 8)
        for side in range(2):
            e0, e1, e2, rate, inv = (geo[side, number, rows, :] for number in range(5))
            unit = [geo[side, U0 + j, rows, :] for j in range(3)]
            turn = [geo[side, W0 + j, rows, :] for j in range(3)]
            z = [sums[side, number, rows, :] for number in range(14)]
            db = e1 * z[9] + e0 * z[10]
            dbd = e2 * z[9] + 2.0 * e1 * z[10] - e0 * z[11]
            inner = z[12]
            w = jnp.zeros((8, ROWS), f32)
            wd = w
            spin = w
            ub, ubd = [], []
            for j in range(3):
                slope = e1 * z[j] + e0 * z[3 + j]
                ub.append(e0 * z[j])
                ubd.append(rate * slope + e0 * z[6 + j])
                db = db + unit[j] * slope
                dbd = dbd + unit[j] * (e2 * z[j] + 2.0 * e1 * z[3 + j])
                inner = inner + unit[j] * z[6 + j]
                spin = spin + turn[j] * slope
                w = w + unit[j] * ub[j]
                wd = wd + turn[j] * ub[j] + unit[j] * ubd[j]
            dbd = rate * dbd + e1 * inner + e0 * z[13] + spin
            for j in range(3):
                t = (ub[j] - unit[j] * w) * inv
                pg[side, j, rows, :] = db * unit[j] + t
                pg[side, 3 + j, rows, :] = (
                    dbd * unit[j]
                    + db * turn[j]
                    + (ubd[j] - turn[j] * w - unit[j] * wd - t * rate) * inv
                )
        return carry

    lax.fori_loop(0, ROWS // 8, offsets_back, 0)

    gpos[...] = jnp.zeros((8, ROWS), f32)
    c8[...] = jnp.zeros((8, ROWS), f32)
    for j in range(6):
        ghosts = pg[1, j]
        own = pg[0, j]
        halves = jnp.sum(ghosts, axis=0, keepdims=True)
        gpos[j : j + 1, :] = halves
        c8[j : j + 1, :] = jnp.sum(own - own.T - ghosts.T, axis=0, keepdims=True)
    both = gpos[...]
    gpos[...] = both + pltpu.roll(both, GHOSTS, 1)
    last = copies(gpos, rpos, send4, recv4, -1, True)
    for copy in last:
        copy.start()
    for copy in last:
        copy.wait()
    hi, mid, lo = split3(merged(rpos))
    slots = onehot[1].astype(bf16)
    total = c8[...] + (mm(hi, slots) + (mm(mid, slots) + mm(lo, slots)))
    force[...] = -total[0:3, :]
    hess[...] = -total[3:6, :]


def per_device(nx, ny, *arrays):
    arrays = list(arrays)
    arrays[15] = arrays[15].reshape(1, F)
    vmem = pl.BlockSpec(memory_space=pltpu.VMEM)
    in_specs = [vmem] * 16
    in_specs[3] = pl.BlockSpec(memory_space=pltpu.SMEM)
    for number in (6, 7, 9, 10, 11, 12, 14):
        in_specs[number] = pl.BlockSpec(memory_space=pl.ANY)

    def v32(*shape):
        return pltpu.VMEM(shape, f32)

    def v16(*shape):
        return pltpu.VMEM(shape, bf16)

    dma = pltpu.SemaphoreType.DMA((8,))
    scratch = [
        v16(2, F, F),
        v16(2, F, 2 * F),
        v16(2, F, 2 * F),
        v16(2, F, F),
        v16(2, F, F),
        v16(2, F, F),
        pltpu.VMEM((8, ROWS), jnp.int32),
        v32(8, ROWS),
        v32(8, ROWS),
        v32(8, 8, ROWS),
        v32(GHOSTS, F),
        v32(GHOSTS, F),
        v32(GHOSTS, 2 * F),
        v32(GHOSTS, 2 * F),
        v32(GHOSTS, 2 * F),
        v32(GHOSTS, 2 * F),
        v32(8, ROWS),
        v32(8, 8, ROWS),
        v32(2, ROWS, ROWS),
        v32(2, ROWS, ROWS),
        v32(6, ROWS, ROWS),
        v32(2, 13, ROWS, ROWS),
        v32(2, NR + PAIRS, ROWS, ROWS),
        v16(4 * ROWS, WIDE),
        v16(12 * ROWS, TILE),
        v16(12 * ROWS, TILE),
        v16(4 * TABLE, NR * ROWS),
        v16(2, WIDE, F),
        v16(2, WIDE, F),
        v16(2, WIDE, F),
        v16(2, WIDE, F),
        v16(4, 4 * ROWS, F),
        v16(4, 4 * ROWS, F),
        v32(TABLE, 2 * F),
        v32(2 * ROWS, F),
        v32(6 * ROWS, F),
        v32(6 * ROWS, 2 * F),
        v32(ROWS, 2 * F),
        v32(2, TABLE, F),
        v32(2, TABLE, F),
        v32(2, ROWS, F),
        v32(2 * TABLE, F),
        v32(8 * ROWS, TILE),
        v32(8 * ROWS, TILE),
        v32(3 * F, 3 * F),
        v32(2 * ROWS, WIDE),
        v32(2, 14, ROWS, ROWS),
        v16(12 * ROWS, F),
        v16(4 * ROWS, F),
        v32(2, 6, ROWS, ROWS),
    ] + [dma] * 11
    out = jax.ShapeDtypeStruct((3, ROWS), f32)
    return pl.pallas_call(
        functools.partial(kernel, nx, ny),
        out_shape=(out, out),
        in_specs=in_specs,
        out_specs=(vmem, vmem),
        scratch_shapes=scratch,
        compiler_params=pltpu.CompilerParams(
            collective_id=0, has_side_effects=True, vmem_limit_bytes=67043328
        ),
    )(*arrays)


def solution(mesh):
    placed = (
        P(None, ("bx", "by")),
        P(None, ("bx", "by")),
        P(("bx", "by"), None),
        P(("bx", "by")),
        P(None, ("bx", "by")),
        P(("bx", "by"), None),
    ) + (P(),) * 10
    return jax.shard_map(
        functools.partial(per_device, mesh.shape["bx"], mesh.shape["by"]),
        mesh=mesh,
        in_specs=placed,
        out_specs=(P(None, ("bx", "by")), P(None, ("bx", "by"))),
        check_vma=False,
    )
```

```python
import functools
import math

import jax
import jax.numpy as jnp
from jax import lax
from jax.experimental import pallas as pl
from jax.experimental.pallas import tpu as pltpu
from jax.sharding import PartitionSpec as P

MESH = pl.DeviceIdType.MESH
f32 = jnp.float32
bf16 = jnp.bfloat16
offsets = ((-1, -1), (-1, 0), (-1, 1), (0, -1), (0, 1), (1, -1), (1, 0), (1, 1))
NN = (((1,), (0,)), ((), ()))
NT = (((1,), (1,)), ((), ()))
KAPPA = math.pi / 3.0
SOFT = 0.01
ROWS = 128
GHOSTS = 64
TABLE = ROWS + GHOSTS
F = 256
NR = 20
PAIRS = NR // 2
TILE = 256
TILES = NR * TABLE // TILE
WIDE = TILES * TILE
STEP = 3 * TILE
STEPS = WIDE // STEP


def split(x):
    hi = x.astype(bf16)
    return hi, (x - hi.astype(f32)).astype(bf16)


def split3(x):
    hi = x.astype(bf16)
    rest = x - hi.astype(f32)
    mid = rest.astype(bf16)
    return hi, mid, (rest - mid.astype(f32)).astype(bf16)


def mm(a, b, dims=NN):
    return lax.dot_general(a, b, dims, preferred_element_type=f32)


def mm3(a, b, dims=NN):
    return mm(a[0], b[0], dims) + (mm(a[1], b[0], dims) + mm(a[0], b[1], dims))


def pick(refs, *index):
    return refs[0][index], refs[1][index]


def put(refs, value, *index):
    hi, lo = split(value)
    refs[0][index] = hi
    refs[1][index] = lo


def sin_cos(angle):
    turns = jnp.floor(angle * (0.5 / math.pi) + 0.5)
    half = 0.5 * ((angle - turns * 6.28125) - turns * (2.0 * math.pi - 6.28125))
    sq = half * half
    odd = 1.0 / 39916800.0
    for c in (1.0 / 362880.0, 1.0 / 5040.0, 1.0 / 120.0, 1.0 / 6.0, 1.0):
        odd = c - sq * odd
    sh = half * odd
    even = 1.0 / 479001600.0
    for c in (1.0 / 3628800.0, 1.0 / 40320.0, 1.0 / 720.0, 1.0 / 24.0, 0.5, 1.0):
        even = c - sq * even
    return 2.0 * sh * even, 1.0 - 2.0 * sh * sh


def sigmoid(v):
    return 1.0 / (1.0 + jnp.exp(-v))


def own_waves(s1, c1):
    twice = 2.0 * c1
    before_s, before_c = jnp.zeros_like(s1), jnp.ones_like(c1)
    s, c = s1, c1
    for q in range(NR):
        yield (q + 1) * KAPPA, s, c
        if q < NR - 1:
            s, before_s = twice * s - before_s, s
            c, before_c = twice * c - before_c, c


def ghost_waves(s1, c1):
    upper = lax.broadcasted_iota(jnp.int32, s1.shape, 1) >= GHOSTS
    s2, c2 = 2.0 * s1 * c1, 1.0 - 2.0 * s1 * s1
    twice = 2.0 * c2
    s, before_s = jnp.where(upper, s2, s1), jnp.where(upper, 0.0, -s1)
    c, before_c = jnp.where(upper, c2, c1), jnp.where(upper, 1.0, c1)
    shift = jnp.where(upper, 2.0 * KAPPA, KAPPA)
    for p in range(PAIRS):
        yield shift + 2.0 * p * KAPPA, s, c
        if p < PAIRS - 1:
            s, before_s = twice * s - before_s, s
            c, before_c = twice * c - before_c, c


E0, E1, E2, DD, IV, S1, C1, U0, W0 = 0, 1, 2, 3, 4, 5, 6, 7, 10
WAVES = (own_waves, ghost_waves)


def kernel(
    nx,
    ny,
    pos_in,
    tan_in,
    emb_in,
    cnt,
    nbr_in,
    snd_in,
    w1i,
    w1o,
    f1_in,
    wl,
    wr,
    w2i,
    w2o,
    f2_in,
    wh,
    we_in,
    force,
    hess,
    pos,
    tan,
    emb,
    nbr,
    snd,
    f1,
    f2,
    we,
    w1i_s,
    w1o_s,
    wlr_s,
    w2i_s,
    w2o_s,
    wh_s,
    sndpad,
    c8,
    csel,
    crecv,
    sel1,
    gemb,
    sel2,
    gnode,
    src3,
    rnode,
    gpos,
    rpos,
    onehot,
    mask,
    colb,
    geo,
    waves,
    lb,
    lv0,
    lv1,
    lt,
    pfs_s,
    pfv_s,
    p2_s,
    p2d_s,
    muf0,
    muf1,
    phi,
    acc,
    accv,
    lr,
    node,
    pre2,
    phi2,
    mu,
    bar,
    out0,
    out1,
    landing,
    two,
    sums,
    vbar,
    nus,
    pg,
    send1,
    recv1,
    sendc,
    recvc,
    send2,
    recv2,
    send3,
    recv3,
    send4,
    recv4,
    loads,
):
    ix, iy = lax.axis_index("bx"), lax.axis_index("by")

    def device(g, sign):
        dx, dy = offsets[g]
        return (lax.rem(ix + sign * dx + nx, nx), lax.rem(iy + sign * dy + ny, ny))

    barrier = pltpu.get_barrier_semaphore()
    for g in range(8):
        pl.semaphore_signal(barrier, inc=1, device_id=device(g, 1), device_id_type=MESH)

    def block(ref, g):
        return ref.at[pl.ds(g * 8, 8), :]

    def copies(source, target, sends, recvs, sign, whole):
        return [
            pltpu.make_async_remote_copy(
                src_ref=source if whole else block(source, g),
                dst_ref=target.at[g] if whole else block(target, g),
                send_sem=sends.at[g],
                recv_sem=recvs.at[g],
                device_id=device(g, sign),
                device_id_type=MESH,
            )
            for g in range(8)
        ]

    def select(x):
        hi, lo = split(x)
        rows = onehot[1, 0:GHOSTS, :].astype(bf16)
        return mm(rows, hi) + mm(rows, lo)

    lane = lax.broadcasted_iota(jnp.int32, (8, ROWS), 1)
    group = lax.div(lane, 8)

    def merged(ref):
        total = jnp.where(group == 0, ref[0], 0.0)
        for g in range(1, 8):
            total = total + jnp.where(group == g, ref[g], 0.0)
        return total

    weights = []
    spots = ((0, 0), (0, F), (1, 0), (1, F), (1, 2 * F), (2, 0), (2, F))
    for number, (w, (down, at)) in enumerate(zip((w1i, w1o, wl, wr, w2i, w2o, wh), spots)):
        place = landing.at[down * F : (down + 1) * F, at : at + w.shape[1]]
        weights.append((pltpu.make_async_copy(w, place, loads.at[number]), place))
    small = {}
    named = ((snd_in, snd), (pos_in, pos), (tan_in, tan), (emb_in, emb), (nbr_in, nbr))
    named += ((f1_in, f1), (f2_in, f2), (we_in, we))
    for number, (source, place) in enumerate(named):
        small[number] = pltpu.make_async_copy(source, place, loads.at[7 + number])
        small[number].start()
    for copy, _ in weights:
        copy.start()
    for number in range(4):
        small[number].wait()

    sndpad[...] = jnp.full((8, ROWS), -1, jnp.int32)
    sndpad[0:1, 0:GHOSTS] = snd[...]
    hot = jnp.where(
        lax.broadcasted_iota(jnp.int32, (ROWS, ROWS), 0) == sndpad[0:1, :], 1.0, 0.0
    )
    onehot[0] = hot
    onehot[1] = hot.T
    c8[...] = jnp.zeros((8, ROWS), f32)
    c8[0:3, :] = pos[...]
    c8[3:6, :] = tan[...]
    hi, mid, lo = split3(c8[...])
    hot16 = hot.astype(bf16)
    csel[...] = mm(hi, hot16) + (mm(mid, hot16) + mm(lo, hot16))
    sel1[...] = select(emb[...])
    stores = ((w1i_s, 0), (w1o_s, 0), (wlr_s, 0), (wlr_s, F), (w2i_s, 0), (w2o_s, 0), (wh_s, 0))
    for (refs, at), (copy, place) in zip(stores, weights):
        copy.wait()
        hi, lo = split(place[...])
        refs[0, :, at : at + hi.shape[1]] = hi
        refs[1, :, at : at + hi.shape[1]] = lo

    small[4].wait()
    row = lax.broadcasted_iota(jnp.int32, (ROWS, ROWS), 0)
    ghost = lax.rem(row, GHOSTS)
    for side, slots in ((0, row), (1, ROWS + (7 - lax.div(ghost, 8)) * 8 + lax.rem(ghost, 8))):

        def mark(k, total, slots=slots):
            return jnp.where(slots == nbr[pl.ds(k, 1), :], 1.0, total)

        listed = lax.fori_loop(0, nbr.shape[0], mark, jnp.zeros((ROWS, ROWS), f32))
        mask[side] = listed.T

    for number in (5, 6, 7):
        small[number].wait()

    def project(rows, first_w, second_w):
        v = mm3(split(rows), first_w)
        return mm3(split(v * sigmoid(v)), second_w)

    w1 = (w1i_s[0], w1i_s[1]), (w1o_s[0], w1o_s[1])
    phi[0:ROWS, :] = project(emb[...], *w1)
    for j in range(6):
        colb[j] = jnp.broadcast_to(c8[j : j + 1, :], (ROWS, ROWS)).T

    def put2(refs, value, start):
        hi, lo = split(value)
        refs[0, pl.ds(start, value.shape[0]), :] = hi
        refs[1, pl.ds(start, value.shape[0]), :] = lo

    def spread_own(refs, table, filters, at):
        def body(q, carry):
            weights = filters[pl.ds(q, 1), at : at + F]
            put2(refs, table() * weights, pl.multiple_of(q * ROWS, ROWS))
            return carry

        lax.fori_loop(0, NR, body, 0)

    def spread_ghosts(refs, table, filters, at):
        def body(q, carry):
            weights = filters[pl.ds(q, 1), at : at + F]
            put2(refs, table() * weights, pl.multiple_of(NR * ROWS + q * GHOSTS, GHOSTS))
            return carry

        lax.fori_loop(0, NR, body, 0)

    def put_rows(ref, value, first, second, cols):
        hi, lo = split(value)
        ref[first : first + 16, cols] = hi
        ref[second : second + 16, cols] = lo

    spread_own(pfs_s, lambda: phi[0:ROWS, 0:F], f1, 0)
    spread_own(pfv_s, lambda: phi[0:ROWS, F : 2 * F], f1, F)

    scale = 1.0 / math.sqrt(nbr.shape[0])

    def geometry(i, carry, side, table):
        rows = pl.ds(pl.multiple_of(i * 8, 8), 8)
        centre = [colb[j, rows, :] for j in range(6)]
        off = [table[j : j + 1, :] - centre[j] for j in range(3)]
        vel = [table[j : j + 1, :] - centre[j] for j in range(3, 6)]
        listed = mask[side, rows, :]
        sq = off[0] * off[0] + off[1] * off[1] + off[2] * off[2]
        sq = jnp.where(listed > 0.0, sq, 1.0) + SOFT
        inv = lax.rsqrt(sq)
        inv = inv * (1.5 - 0.5 * sq * inv * inv)
        dist = sq * inv
        unit = [x * inv for x in off]
        rate = unit[0] * vel[0] + unit[1] * vel[1] + unit[2] * vel[2]
        s1, c1 = sin_cos(KAPPA * dist)
        weight = scale * listed
        env = 0.5 * (c1 + 1.0)
        env1 = (-0.5 * KAPPA) * s1
        env2 = (-0.5 * KAPPA * KAPPA) * c1
        e0 = weight * env * inv
        slope = env1 - env * inv
        e1 = weight * inv * slope
        e2 = weight * inv * (env2 - 2.0 * inv * slope)
        planes = [e0, e1, e2, rate, inv, s1, c1] + unit
        planes += [(vel[j] - unit[j] * rate) * inv for j in range(3)]
        for number, value in enumerate(planes):
            geo[side, number, rows, :] = value
        for number, (a, s, c) in enumerate(WAVES[side](s1, c1)):
            waves[0, side * NR + number, rows, :] = s
            waves[1, side * NR + number, rows, :] = a * c
        return carry

    lv = (lv0, lv1)

    def build_pairs(m, target):
        side = jnp.where(m < PAIRS, 0, 1)
        cols = pl.ds(pl.multiple_of(m * TILE, TILE), TILE)
        for start in range(0, ROWS, 16):
            rows = slice(start, start + 16)

            def twice(x):
                return jnp.concatenate([x, x], 1)

            e0, e1, rate = (geo[side, number, rows, :] for number in (E0, E1, DD))
            e1d, e0d = twice(e1 * rate), twice(e0 * rate)
            s = jnp.concatenate([waves[0, 2 * m + half, rows, :] for half in range(2)], 1)
            ac = jnp.concatenate([waves[1, 2 * m + half, rows, :] for half in range(2)], 1)
            b = twice(e0) * s
            bd = e1d * s + e0d * ac
            put_rows(lb, bd, start, start + 3 * ROWS, cols)
            put_rows(lb, b, start + ROWS, start + 2 * ROWS, cols)
            for j in range(3):
                u, w = twice(geo[side, U0 + j, rows, :]), twice(geo[side, W0 + j, rows, :])
                first = start + j * ROWS
                put_rows(target, b * u, first, first + 6 * ROWS, slice(None))
                first += 3 * ROWS
                put_rows(target, bd * u + b * w, first, first + 6 * ROWS, slice(None))

    def add_to(ref, rows, value, i):
        if i == 0:
            ref[rows, :] = value
        else:
            ref[rows, :] += value

    def gather_scalar(refs, cols):
        both = mm(lb[:, cols], refs[0, cols, :])
        rest = mm(lb[0 : 2 * ROWS, cols], refs[1, cols, :])
        acc[0:ROWS, :] += both[ROWS : 2 * ROWS] + both[2 * ROWS : 3 * ROWS] + rest[ROWS:]
        acc[ROWS : 2 * ROWS, :] += both[0:ROWS] + both[3 * ROWS :] + rest[0:ROWS]

    def gather_vector(m, near):
        cols = pl.ds(pl.multiple_of(m * TILE, TILE), TILE)
        both = mm(near[...], pfv_s[0, cols, :])
        rest = mm(near[0 : 6 * ROWS, :], pfv_s[1, cols, :])
        accv[...] += both[0 : 6 * ROWS] + both[6 * ROWS :] + rest

    lax.fori_loop(0, ROWS // 8, functools.partial(geometry, side=0, table=c8[...]), 0)
    build_pairs(0, lv0)
    pl.semaphore_wait(barrier, 8)
    coords = copies(csel, crecv, sendc, recvc, 1, True)
    first = copies(sel1, gemb, send1, recv1, 1, False)
    for copy in coords + first:
        copy.start()

    acc[...] = jnp.zeros((2 * ROWS, F), f32)
    accv[...] = jnp.zeros((6 * ROWS, F), f32)

    def two_tiles(k, carry, base, last):
        for half in range(2):
            m = base + 2 * k + half
            gather_vector(m, lv[half])
            build_pairs(jnp.minimum(m + 1, last), lv[1 - half])
        return carry

    lax.fori_loop(0, PAIRS // 2, functools.partial(two_tiles, base=0, last=PAIRS - 1), 0)

    for copy in coords + first:
        copy.wait()
    phi[ROWS:TABLE, :] = project(gemb[...], *w1)
    found = merged(crecv)
    twofold = found + pltpu.roll(found, GHOSTS, 1)
    lax.fori_loop(0, ROWS // 8, functools.partial(geometry, side=1, table=twofold), 0)
    build_pairs(PAIRS, lv0)

    spread_ghosts(pfs_s, lambda: phi[ROWS:TABLE, 0:F], f1, 0)
    spread_ghosts(pfv_s, lambda: phi[ROWS:TABLE, F : 2 * F], f1, F)
    lax.fori_loop(
        0, (TILES - PAIRS) // 2, functools.partial(two_tiles, base=PAIRS, last=TILES - 1), 0
    )
    gather_vector(TILES - 1, lv0)


    def scalar_step(i, carry):
        gather_scalar(pfs_s, pl.ds(pl.multiple_of(i * STEP, STEP), STEP))
        return carry

    lax.fori_loop(0, STEPS, scalar_step, 0)
    lr[...] = mm3(split(accv[...]), (wlr_s[0], wlr_s[1]))

    def part(j, side):
        return lr[j * ROWS : (j + 1) * ROWS, side * F : (side + 1) * F]

    state = emb[...] + acc[0:ROWS, :]
    moved = acc[ROWS : 2 * ROWS, :]
    for j in range(3):
        state = state + part(j, 0) * part(j, 1)
        moved = moved + (part(3 + j, 0) * part(j, 1) + part(j, 0) * part(3 + j, 1))
    node[:, 0:F] = state
    node[:, F : 2 * F] = moved
    sel2[...] = select(node[...])
    second = copies(sel2, gnode, send2, recv2, 1, False)
    for copy in second:
        copy.start()

    w2 = (w2i_s[0], w2i_s[1]), (w2o_s[0], w2o_s[1])

    def table_two(values, moves, at, n):
        v = mm3(split(values), w2[0])
        vd = mm3(split(moves), w2[0])
        sig = sigmoid(v)
        pre2[0, at : at + n, :] = v
        pre2[1, at : at + n, :] = vd
        slope = sig * (1.0 + v * (1.0 - sig))
        phi2[0, at : at + n, :] = mm3(split(v * sig), w2[1])
        phi2[1, at : at + n, :] = mm3(split(slope * vd), w2[1])

    table_two(node[:, 0:F], node[:, F : 2 * F], 0, ROWS)

    for side in range(2):
        rows = ROWS if side == 0 else GHOSTS
        e0, e1, rate = (geo[side, number] for number in (E0, E1, DD))
        pg[side, 0] = e0.T
        pg[side, 1] = (e1 * rate).T
        pg[side, 2] = (e0 * rate).T
        pg[side, 3] = geo[side, S1].T
        pg[side, 4] = geo[side, C1].T

    def turned(side, count):
        def body(i, carry):
            start = pl.multiple_of(i * 16, 16)
            g = [pg[side, number, pl.ds(start, 16), :] for number in range(5)]
            held = None
            for q, (a, s, c) in enumerate(own_waves(g[3], g[4])):
                new = (g[0] * s, g[1] * s + g[2] * (a * c))
                if q % 2 == 0:
                    held = new
                    continue
                cols = slice((q - 1) * ROWS, (q + 1) * ROWS)
                for value, first, second in ((1, 0, 3), (0, 1, 2)):
                    hi, lo = split(jnp.concatenate([held[value], new[value]], 1))
                    lt[pl.ds(start + side * ROWS + first * TABLE, 16), cols] = hi
                    lt[pl.ds(start + side * ROWS + second * TABLE, 16), cols] = lo
            return carry

        lax.fori_loop(0, count // 16, body, 0)

    turned(0, ROWS)
    turned(1, GHOSTS)

    spread_own(p2_s, lambda: phi2[0, 0:ROWS, :], f2, 0)
    spread_own(p2d_s, lambda: phi2[1, 0:ROWS, :], f2, 0)

    for copy in second:
        copy.wait()
    table_two(gnode[:, 0:F], gnode[:, F : 2 * F], ROWS, GHOSTS)
    spread_ghosts(p2_s, lambda: phi2[0, ROWS:TABLE, :], f2, 0)
    spread_ghosts(p2d_s, lambda: phi2[1, ROWS:TABLE, :], f2, 0)
    acc[...] = jnp.zeros((2 * ROWS, F), f32)

    def messages_two(i, carry):
        cols = pl.ds(pl.multiple_of(i * STEP, STEP), STEP)
        gather_scalar(p2_s, cols)
        both = mm(lb[ROWS : 3 * ROWS, cols], p2d_s[0, cols, :])
        rest = mm(lb[ROWS : 2 * ROWS, cols], p2d_s[1, cols, :])
        acc[ROWS : 2 * ROWS, :] += both[0:ROWS] + both[ROWS:] + rest
        return carry

    lax.fori_loop(0, STEPS, messages_two, 0)
    st = node[:, 0:F] + acc[0:ROWS, :]
    std = node[:, F : 2 * F] + acc[ROWS : 2 * ROWS, :]

    whs = wh_s[0], wh_s[1]
    v = mm3(split(st), whs)
    vd = mm3(split(std), whs)
    sig = sigmoid(v)
    live = lax.broadcasted_iota(jnp.int32, (ROWS, F), 0) < cnt[0]
    top = jnp.where(live, jnp.broadcast_to(we[...], (ROWS, F)), 0.0)
    mu[0] = mm3(split(top * (sig * (1.0 + v * (1.0 - sig)))), whs, NT)
    mu[1] = mm3(
        split(top * (sig * (1.0 - sig) * (2.0 + v * (1.0 - 2.0 * sig))) * vd), whs, NT
    )

    muf = (muf0, muf1)

    def scaled(i):
        for q in range(4 * i, 4 * i + 4):
            weights = f2[q : q + 1, :]
            rows = slice(q % 4 * ROWS, (q % 4 + 1) * ROWS)
            for number in range(2):
                hi, lo = split(mu[number] * weights)
                muf[i % 2][2 * number, rows, :] = hi
                muf[i % 2][2 * number + 1, rows, :] = lo

    def turned_messages(i):
        cols = slice(i * 4 * ROWS, (i + 1) * 4 * ROWS)
        right = muf[i % 2]
        both = mm(lt[:, cols], right[0])
        rest = mm(lt[0 : 2 * TABLE, cols], right[1])
        also = mm(lt[TABLE : 3 * TABLE, cols], right[2])
        more = mm(lt[TABLE : 2 * TABLE, cols], right[3])
        add_to(
            bar,
            slice(0, TABLE),
            both[TABLE : 2 * TABLE] + both[2 * TABLE : 3 * TABLE] + rest[TABLE:],
            i,
        )
        add_to(
            bar,
            slice(TABLE, 2 * TABLE),
            (both[0:TABLE] + both[3 * TABLE :] + rest[0:TABLE])
            + (also[0:TABLE] + also[TABLE:] + more),
            i,
        )

    for i in range(NR // 4 + 1):
        if i < NR // 4:
            scaled(i)
        if i > 0:
            turned_messages(i - 1)
    back = mm3(split(bar[...]), w2[1], NT)
    v, vd = pre2[0], pre2[1]
    sig = sigmoid(v)
    slope = sig * (1.0 + v * (1.0 - sig))
    curve = sig * (1.0 - sig) * (2.0 + v * (1.0 - 2.0 * sig))
    bar[0:TABLE, :] = back[0:TABLE] * slope
    bar[TABLE : 2 * TABLE, :] = back[TABLE : 2 * TABLE] * slope + back[0:TABLE] * curve * vd
    bar[...] = mm3(split(bar[...]), w2[0], NT)
    src3[:, 0:F] = bar[ROWS:TABLE, :]
    src3[:, F : 2 * F] = bar[TABLE + ROWS : 2 * TABLE, :]
    third = copies(src3, rnode, send3, recv3, -1, False)
    for copy in third:
        copy.start()

    m = split(mu[0])
    md = split(mu[1])
    high = jnp.concatenate([m[0], md[0]], 0)
    full = jnp.concatenate([high, m[1], md[1]], 0)
    ours = jnp.concatenate(m, 0)

    def pairs_two(i, carry):
        cols = pl.ds(pl.multiple_of(i * STEP, STEP), STEP)
        both = mm(full, p2_s[0, cols, :], NT)
        rest = mm(high, p2_s[1, cols, :], NT)
        also = mm(ours, p2d_s[0, cols, :], NT)
        more = mm(m[0], p2d_s[1, cols, :], NT)
        two[0:ROWS, cols] = both[0:ROWS] + both[2 * ROWS : 3 * ROWS] + rest[0:ROWS]
        two[ROWS : 2 * ROWS, cols] = (
            both[ROWS : 2 * ROWS] + both[3 * ROWS :] + rest[ROWS:]
        ) + (also[0:ROWS] + also[ROWS:] + more)
        return carry

    lax.fori_loop(0, STEPS, pairs_two, 0)

    for copy in third:
        copy.wait()
    rows_back = onehot[0, :, 0:GHOSTS].astype(bf16)
    hi, lo = split(rnode[...])
    returned = mm(rows_back, hi) + mm(rows_back, lo)
    nu = mu[0] + bar[0:ROWS, :] + returned[:, 0:F]
    nud = mu[1] + bar[TABLE : TABLE + ROWS, :] + returned[:, F : 2 * F]
    mu[0] = nu
    mu[1] = nud

    wlr = wlr_s[0], wlr_s[1]
    for j in range(3):
        nu, nud = mu[0], mu[1]
        l, r, ld, rd = part(j, 0), part(j, 1), part(3 + j, 0), part(3 + j, 1)
        lr[j * ROWS : (j + 1) * ROWS, 0:F] = nu * r
        lr[j * ROWS : (j + 1) * ROWS, F : 2 * F] = nu * l
        lr[(3 + j) * ROWS : (4 + j) * ROWS, 0:F] = nud * r + nu * rd
        lr[(3 + j) * ROWS : (4 + j) * ROWS, F : 2 * F] = nud * l + nu * ld
    hi, lo = split(mm3(split(lr[...]), wlr, NT))
    vbar[0 : 6 * ROWS, :] = hi
    vbar[6 * ROWS :, :] = lo
    for number in range(2):
        hi, lo = split(mu[number])
        nus[number * ROWS : (number + 1) * ROWS, :] = hi
        nus[(2 + number) * ROWS : (3 + number) * ROWS, :] = lo
    out = (out0, out1)

    def pairs_one(m, target):
        cols = pl.ds(pl.multiple_of(m * TILE, TILE), TILE)
        both = mm(nus[...], pfs_s[0, cols, :], NT)
        rest = mm(nus[0 : 2 * ROWS, :], pfs_s[1, cols, :], NT)
        target[0 : 2 * ROWS, :] = two[:, cols] + (both[0 : 2 * ROWS] + both[2 * ROWS :] + rest)
        both = mm(vbar[...], pfv_s[0, cols, :], NT)
        rest = mm(vbar[0 : 6 * ROWS, :], pfv_s[1, cols, :], NT)
        target[2 * ROWS :, :] = both[0 : 6 * ROWS] + both[6 * ROWS :] + rest

    upper = lax.broadcasted_iota(jnp.int32, (8, ROWS), 1) >= GHOSTS

    def sum_waves(m, source):
        side = jnp.where(m < PAIRS, 0, 1)
        base = jnp.where(m < PAIRS, 2 * m + 1, 4 * (m - PAIRS) + 1).astype(f32)
        jump = jnp.where(m < PAIRS, 1.0, 2.0)
        ghosts_on = jnp.where(m < PAIRS, 0.0, 1.0)
        a = [
            KAPPA * (base + half * jump + ghosts_on * jnp.where(upper, 1.0, 0.0))
            for half in range(2)
        ]
        aa = [x * x for x in a]
        for start in range(0, ROWS, 8):
            rows = slice(start, start + 8)
            u = [geo[side, U0 + j, rows, :] for j in range(3)]
            total = [sums[side, number, rows, :] for number in range(14)]
            for half in range(2):
                s = waves[0, 2 * m + half, rows, :]
                ac = waves[1, 2 * m + half, rows, :]
                ss = s * aa[half]
                cols = slice(half * ROWS, (half + 1) * ROWS)
                y = [source[start + k * ROWS : start + k * ROWS + 8, cols] for k in range(8)]
                along = y[0] + u[0] * y[2] + u[1] * y[3] + u[2] * y[4]
                along_d = y[1] + u[0] * y[5] + u[1] * y[6] + u[2] * y[7]
                for j in range(3):
                    total[j] += s * y[2 + j]
                    total[3 + j] += ac * y[2 + j]
                    total[6 + j] += s * y[5 + j]
                total[9] += s * y[0]
                total[10] += ac * y[0]
                total[11] += ss * along
                total[12] += s * y[1]
                total[13] += ac * along_d
            for number in range(14):
                sums[side, number, rows, :] = total[number]

    sums[...] = jnp.zeros(sums.shape, f32)
    pairs_one(PAIRS, out0)

    def two_sums(k, carry, first, second, base, last):
        for half in range(2):
            ahead, behind = (first, second) if half == 0 else (second, first)
            m = base + 2 * k + half
            pairs_one(jnp.minimum(m + 1, last), ahead)
            sum_waves(m, behind)
        return carry

    lax.fori_loop(
        0,
        (TILES - PAIRS) // 2,
        functools.partial(two_sums, first=out1, second=out0, base=PAIRS, last=TILES - 1),
        0,
    )
    pairs_one(0, out1)
    sum_waves(TILES - 1, out0)

    def offsets_back(i, carry, side):
        rows = pl.ds(pl.multiple_of(i * 8, 8), 8)
        e0, e1, e2, rate, inv = (geo[side, number, rows, :] for number in range(5))
        unit = [geo[side, U0 + j, rows, :] for j in range(3)]
        turn = [geo[side, W0 + j, rows, :] for j in range(3)]
        z = [sums[side, number, rows, :] for number in range(14)]
        db = e1 * z[9] + e0 * z[10]
        dbd = e2 * z[9] + 2.0 * e1 * z[10] - e0 * z[11]
        inner = z[12]
        w = jnp.zeros((8, ROWS), f32)
        wd = w
        spin = w
        ub, ubd = [], []
        for j in range(3):
            slope = e1 * z[j] + e0 * z[3 + j]
            ub.append(e0 * z[j])
            ubd.append(rate * slope + e0 * z[6 + j])
            db = db + unit[j] * slope
            dbd = dbd + unit[j] * (e2 * z[j] + 2.0 * e1 * z[3 + j])
            inner = inner + unit[j] * z[6 + j]
            spin = spin + turn[j] * slope
            w = w + unit[j] * ub[j]
            wd = wd + turn[j] * ub[j] + unit[j] * ubd[j]
        dbd = rate * dbd + e1 * inner + e0 * z[13] + spin
        for j in range(3):
            t = (ub[j] - unit[j] * w) * inv
            pg[side, j, rows, :] = db * unit[j] + t
            pg[side, 3 + j, rows, :] = (
                dbd * unit[j]
                + db * turn[j]
                + (ubd[j] - turn[j] * w - unit[j] * wd - t * rate) * inv
            )
        return carry

    lax.fori_loop(0, ROWS // 8, functools.partial(offsets_back, side=1), 0)
    gpos[...] = jnp.zeros((8, ROWS), f32)
    c8[...] = jnp.zeros((8, ROWS), f32)
    for j in range(6):
        ghosts = pg[1, j]
        gpos[j : j + 1, :] = jnp.sum(ghosts, axis=0, keepdims=True)
        c8[j : j + 1, :] = jnp.sum(ghosts.T, axis=0, keepdims=True)
    both = gpos[...]
    gpos[...] = both + pltpu.roll(both, GHOSTS, 1)
    last = copies(gpos, rpos, send4, recv4, -1, True)
    for copy in last:
        copy.start()

    lax.fori_loop(
        0,
        PAIRS // 2,
        functools.partial(two_sums, first=out0, second=out1, base=0, last=PAIRS - 1),
        0,
    )
    lax.fori_loop(0, ROWS // 8, functools.partial(offsets_back, side=0), 0)
    for j in range(6):
        own = pg[0, j]
        c8[j : j + 1, :] = jnp.sum(own - own.T, axis=0, keepdims=True) - c8[j : j + 1, :]
    for copy in last:
        copy.wait()
    hi, mid, lo = split3(merged(rpos))
    slots = onehot[1].astype(bf16)
    total = c8[...] + (mm(hi, slots) + (mm(mid, slots) + mm(lo, slots)))
    force[...] = -total[0:3, :]
    hess[...] = -total[3:6, :]


def per_device(nx, ny, *arrays):
    arrays = list(arrays)
    arrays[15] = arrays[15].reshape(1, F)
    vmem = pl.BlockSpec(memory_space=pltpu.VMEM)
    in_specs = [pl.BlockSpec(memory_space=pl.ANY)] * 16
    in_specs[3] = pl.BlockSpec(memory_space=pltpu.SMEM)

    def v32(*shape):
        return pltpu.VMEM(shape, f32)

    def v16(*shape):
        return pltpu.VMEM(shape, bf16)

    dma = pltpu.SemaphoreType.DMA((8,))
    scratch = [
        v32(3, ROWS),
        v32(3, ROWS),
        v32(ROWS, F),
        pltpu.VMEM(arrays[4].shape, jnp.int32),
        pltpu.VMEM((1, GHOSTS), jnp.int32),
        v32(NR, 2 * F),
        v32(NR, F),
        v32(1, F),
        v16(2, F, F),
        v16(2, F, 2 * F),
        v16(2, F, 2 * F),
        v16(2, F, F),
        v16(2, F, F),
        v16(2, F, F),
        pltpu.VMEM((8, ROWS), jnp.int32),
        v32(8, ROWS),
        v32(8, ROWS),
        v32(8, 8, ROWS),
        v32(GHOSTS, F),
        v32(GHOSTS, F),
        v32(GHOSTS, 2 * F),
        v32(GHOSTS, 2 * F),
        v32(GHOSTS, 2 * F),
        v32(GHOSTS, 2 * F),
        v32(8, ROWS),
        v32(8, 8, ROWS),
        v32(2, ROWS, ROWS),
        v32(2, ROWS, ROWS),
        v32(6, ROWS, ROWS),
        v32(2, 13, ROWS, ROWS),
        v32(2, NR + PAIRS, ROWS, ROWS),
        v16(4 * ROWS, WIDE),
        v16(12 * ROWS, TILE),
        v16(12 * ROWS, TILE),
        v16(4 * TABLE, NR * ROWS),
        v16(2, WIDE, F),
        v16(2, WIDE, F),
        v16(2, WIDE, F),
        v16(2, WIDE, F),
        v16(4, 4 * ROWS, F),
        v16(4, 4 * ROWS, F),
        v32(TABLE, 2 * F),
        v32(2 * ROWS, F),
        v32(6 * ROWS, F),
        v32(6 * ROWS, 2 * F),
        v32(ROWS, 2 * F),
        v32(2, TABLE, F),
        v32(2, TABLE, F),
        v32(2, ROWS, F),
        v32(2 * TABLE, F),
        v32(8 * ROWS, TILE),
        v32(8 * ROWS, TILE),
        v32(3 * F, 3 * F),
        v32(2 * ROWS, WIDE),
        v32(2, 14, ROWS, ROWS),
        v16(12 * ROWS, F),
        v16(4 * ROWS, F),
        v32(2, 6, ROWS, ROWS),
    ] + [dma] * 10 + [pltpu.SemaphoreType.DMA((15,))]
    out = jax.ShapeDtypeStruct((3, ROWS), f32)
    return pl.pallas_call(
        functools.partial(kernel, nx, ny),
        out_shape=(out, out),
        in_specs=in_specs,
        out_specs=(vmem, vmem),
        scratch_shapes=scratch,
        compiler_params=pltpu.CompilerParams(
            collective_id=0, has_side_effects=True, vmem_limit_bytes=67043328
        ),
    )(*arrays)


def solution(mesh):
    placed = (
        P(None, ("bx", "by")),
        P(None, ("bx", "by")),
        P(("bx", "by"), None),
        P(("bx", "by")),
        P(None, ("bx", "by")),
        P(("bx", "by"), None),
    ) + (P(),) * 10
    return jax.shard_map(
        functools.partial(per_device, mesh.shape["bx"], mesh.shape["by"]),
        mesh=mesh,
        in_specs=placed,
        out_specs=(P(None, ("bx", "by")), P(None, ("bx", "by"))),
        check_vma=False,
    )
```

```python
import functools
import math

import jax
import jax.numpy as jnp
from jax import lax
from jax.experimental import pallas as pl
from jax.experimental.pallas import tpu as pltpu
from jax.sharding import PartitionSpec as P

MESH = pl.DeviceIdType.MESH
f32 = jnp.float32
bf16 = jnp.bfloat16
offsets = ((-1, -1), (-1, 0), (-1, 1), (0, -1), (0, 1), (1, -1), (1, 0), (1, 1))
NN = (((1,), (0,)), ((), ()))
NT = (((1,), (1,)), ((), ()))
KAPPA = math.pi / 3.0
SOFT = 0.01
ROWS = 128
GHOSTS = 64
TABLE = ROWS + GHOSTS
F = 256
NR = 20
PAIRS = NR // 2
TILE = 256
TILES = NR * TABLE // TILE
WIDE = TILES * TILE
GROUP = 5
GROUPS = NR // GROUP


def split(x):
    hi = x.astype(bf16)
    return hi, (x - hi.astype(f32)).astype(bf16)


def split3(x):
    hi = x.astype(bf16)
    rest = x - hi.astype(f32)
    mid = rest.astype(bf16)
    return hi, mid, (rest - mid.astype(f32)).astype(bf16)


def mm(a, b, dims=NN):
    return lax.dot_general(a, b, dims, preferred_element_type=f32)


def mm3(a, b, dims=NN):
    return mm(a[0], b[0], dims) + (mm(a[1], b[0], dims) + mm(a[0], b[1], dims))


def pick(refs, *index):
    return refs[0][index], refs[1][index]


def put(refs, value, *index):
    hi, lo = split(value)
    refs[0][index] = hi
    refs[1][index] = lo


def sin_cos(angle):
    turns = jnp.floor(angle * (0.5 / math.pi) + 0.5)
    half = 0.5 * ((angle - turns * 6.28125) - turns * (2.0 * math.pi - 6.28125))
    sq = half * half
    odd = 1.0 / 39916800.0
    for c in (1.0 / 362880.0, 1.0 / 5040.0, 1.0 / 120.0, 1.0 / 6.0, 1.0):
        odd = c - sq * odd
    sh = half * odd
    even = 1.0 / 479001600.0
    for c in (1.0 / 3628800.0, 1.0 / 40320.0, 1.0 / 720.0, 1.0 / 24.0, 0.5, 1.0):
        even = c - sq * even
    return 2.0 * sh * even, 1.0 - 2.0 * sh * sh


def sigmoid(v):
    return 1.0 / (1.0 + jnp.exp(-v))


def own_waves(s1, c1):
    twice = 2.0 * c1
    before_s, before_c = jnp.zeros_like(s1), jnp.ones_like(c1)
    s, c = s1, c1
    for q in range(NR):
        yield (q + 1) * KAPPA, s, c
        if q < NR - 1:
            s, before_s = twice * s - before_s, s
            c, before_c = twice * c - before_c, c


def ghost_waves(s1, c1):
    upper = lax.broadcasted_iota(jnp.int32, s1.shape, 1) >= GHOSTS
    s2, c2 = 2.0 * s1 * c1, 1.0 - 2.0 * s1 * s1
    twice = 2.0 * c2
    s, before_s = jnp.where(upper, s2, s1), jnp.where(upper, 0.0, -s1)
    c, before_c = jnp.where(upper, c2, c1), jnp.where(upper, 1.0, c1)
    shift = jnp.where(upper, 2.0 * KAPPA, KAPPA)
    for p in range(PAIRS):
        yield shift + 2.0 * p * KAPPA, s, c
        if p < PAIRS - 1:
            s, before_s = twice * s - before_s, s
            c, before_c = twice * c - before_c, c


E0, E1, E2, DD, IV, S1, C1, U0, W0 = 0, 1, 2, 3, 4, 5, 6, 7, 10
WAVES = (own_waves, ghost_waves)


def kernel(
    nx,
    ny,
    pos_in,
    tan_in,
    emb_in,
    cnt,
    nbr_in,
    snd_in,
    w1i,
    w1o,
    f1_in,
    wl,
    wr,
    w2i,
    w2o,
    f2_in,
    wh,
    we_in,
    force,
    hess,
    pos,
    tan,
    emb,
    nbr,
    snd,
    f1,
    f2,
    we,
    w1i_s,
    w1o_s,
    wlr_s,
    w2i_s,
    w2o_s,
    wh_s,
    sndpad,
    c8,
    csel,
    crecv,
    sel1,
    gemb,
    sel2,
    gnode,
    src3,
    rnode,
    gpos,
    rpos,
    onehot,
    mask,
    colb,
    geo,
    waves,
    bq,
    lv0,
    lv1,
    lt,
    pfv_s,
    tab,
    wmu,
    scaled,
    phi,
    acc,
    accv,
    lr,
    node,
    pre2,
    phi2,
    mu,
    bar,
    out0,
    out1,
    landing,
    two,
    sums,
    vbar,
    pg,
    send1,
    recv1,
    sendc,
    recvc,
    send2,
    recv2,
    send3,
    recv3,
    send4,
    recv4,
    loads,
):
    ix, iy = lax.axis_index("bx"), lax.axis_index("by")

    def device(g, sign):
        dx, dy = offsets[g]
        return (lax.rem(ix + sign * dx + nx, nx), lax.rem(iy + sign * dy + ny, ny))

    barrier = pltpu.get_barrier_semaphore()
    for g in range(8):
        pl.semaphore_signal(barrier, inc=1, device_id=device(g, 1), device_id_type=MESH)

    def block(ref, g):
        return ref.at[pl.ds(g * 8, 8), :]

    def copies(source, target, sends, recvs, sign, whole):
        return [
            pltpu.make_async_remote_copy(
                src_ref=source if whole else block(source, g),
                dst_ref=target.at[g] if whole else block(target, g),
                send_sem=sends.at[g],
                recv_sem=recvs.at[g],
                device_id=device(g, sign),
                device_id_type=MESH,
            )
            for g in range(8)
        ]

    def select(x):
        hi, lo = split(x)
        rows = onehot[1, 0:GHOSTS, :].astype(bf16)
        return mm(rows, hi) + mm(rows, lo)

    lane = lax.broadcasted_iota(jnp.int32, (8, ROWS), 1)
    group = lax.div(lane, 8)

    def merged(ref):
        total = jnp.where(group == 0, ref[0], 0.0)
        for g in range(1, 8):
            total = total + jnp.where(group == g, ref[g], 0.0)
        return total

    weights = []
    spots = ((0, 0), (0, F), (1, 0), (1, F), (1, 2 * F), (2, 0), (2, F))
    for number, (w, (down, at)) in enumerate(zip((w1i, w1o, wl, wr, w2i, w2o, wh), spots)):
        place = landing.at[down * F : (down + 1) * F, at : at + w.shape[1]]
        weights.append((pltpu.make_async_copy(w, place, loads.at[number]), place))
    small = {}
    named = ((snd_in, snd), (pos_in, pos), (tan_in, tan), (emb_in, emb), (nbr_in, nbr))
    named += ((f1_in, f1), (f2_in, f2), (we_in, we))
    for number, (source, place) in enumerate(named):
        small[number] = pltpu.make_async_copy(source, place, loads.at[7 + number])
        small[number].start()
    for copy, _ in weights:
        copy.start()
    for number in range(4):
        small[number].wait()

    sndpad[...] = jnp.full((8, ROWS), -1, jnp.int32)
    sndpad[0:1, 0:GHOSTS] = snd[...]
    hot = jnp.where(
        lax.broadcasted_iota(jnp.int32, (ROWS, ROWS), 0) == sndpad[0:1, :], 1.0, 0.0
    )
    onehot[0] = hot
    onehot[1] = hot.T
    c8[...] = jnp.zeros((8, ROWS), f32)
    c8[0:3, :] = pos[...]
    c8[3:6, :] = tan[...]
    hi, mid, lo = split3(c8[...])
    hot16 = hot.astype(bf16)
    csel[...] = mm(hi, hot16) + (mm(mid, hot16) + mm(lo, hot16))
    sel1[...] = select(emb[...])
    stores = ((w1i_s, 0), (w1o_s, 0), (wlr_s, 0), (wlr_s, F), (w2i_s, 0), (w2o_s, 0), (wh_s, 0))
    for (refs, at), (copy, place) in zip(stores, weights):
        copy.wait()
        hi, lo = split(place[...])
        refs[0, :, at : at + hi.shape[1]] = hi
        refs[1, :, at : at + hi.shape[1]] = lo

    small[4].wait()
    row = lax.broadcasted_iota(jnp.int32, (ROWS, ROWS), 0)
    ghost = lax.rem(row, GHOSTS)
    for side, slots in ((0, row), (1, ROWS + (7 - lax.div(ghost, 8)) * 8 + lax.rem(ghost, 8))):

        def mark(k, total, slots=slots):
            return jnp.where(slots == nbr[pl.ds(k, 1), :], 1.0, total)

        listed = lax.fori_loop(0, nbr.shape[0], mark, jnp.zeros((ROWS, ROWS), f32))
        mask[side] = listed.T

    for number in (5, 6, 7):
        small[number].wait()

    def project(rows, first_w, second_w):
        v = mm3(split(rows), first_w)
        return mm3(split(v * sigmoid(v)), second_w)

    w1 = (w1i_s[0], w1i_s[1]), (w1o_s[0], w1o_s[1])
    phi[0:ROWS, :] = project(emb[...], *w1)
    for j in range(6):
        colb[j] = jnp.broadcast_to(c8[j : j + 1, :], (ROWS, ROWS)).T

    def put2(refs, value, start):
        hi, lo = split(value)
        refs[0, pl.ds(start, value.shape[0]), :] = hi
        refs[1, pl.ds(start, value.shape[0]), :] = lo

    def spread_own(refs, table, filters, at):
        def body(q, carry):
            weights = filters[pl.ds(q, 1), at : at + F]
            put2(refs, table() * weights, pl.multiple_of(q * ROWS, ROWS))
            return carry

        lax.fori_loop(0, NR, body, 0)

    def spread_ghosts(refs, table, filters, at):
        def body(q, carry):
            weights = filters[pl.ds(q, 1), at : at + F]
            put2(refs, table() * weights, pl.multiple_of(NR * ROWS + q * GHOSTS, GHOSTS))
            return carry

        lax.fori_loop(0, NR, body, 0)

    def put_rows(ref, value, first, second):
        hi, lo = split(value)
        ref[first : first + 16, :] = hi
        ref[second : second + 16, :] = lo

    def fill_own(number, value):
        put2(tab.at[number], value, 0)

    def fill_ghosts(number, value):
        for start in (ROWS, TABLE):
            put2(tab.at[number], value, start)

    def place(q, rows):
        i, k = (q // GROUP, q % GROUP) if isinstance(q, int) else (lax.div(q, GROUP), lax.rem(q, GROUP))
        return 2 * GROUP * rows * i + rows * k

    fill_own(0, phi[0:ROWS, 0:F])
    spread_own(pfv_s, lambda: phi[0:ROWS, F : 2 * F], f1, F)

    scale = 1.0 / math.sqrt(nbr.shape[0])

    def geometry(i, carry, side, table):
        rows = pl.ds(pl.multiple_of(i * 8, 8), 8)
        centre = [colb[j, rows, :] for j in range(6)]
        off = [table[j : j + 1, :] - centre[j] for j in range(3)]
        vel = [table[j : j + 1, :] - centre[j] for j in range(3, 6)]
        listed = mask[side, rows, :]
        sq = off[0] * off[0] + off[1] * off[1] + off[2] * off[2]
        sq = jnp.where(listed > 0.0, sq, 1.0) + SOFT
        inv = lax.rsqrt(sq)
        inv = inv * (1.5 - 0.5 * sq * inv * inv)
        dist = sq * inv
        unit = [x * inv for x in off]
        rate = unit[0] * vel[0] + unit[1] * vel[1] + unit[2] * vel[2]
        s1, c1 = sin_cos(KAPPA * dist)
        weight = scale * listed
        env = 0.5 * (c1 + 1.0)
        env1 = (-0.5 * KAPPA) * s1
        env2 = (-0.5 * KAPPA * KAPPA) * c1
        e0 = weight * env * inv
        slope = env1 - env * inv
        e1 = weight * inv * slope
        e2 = weight * inv * (env2 - 2.0 * inv * slope)
        planes = [e0, e1, e2, rate, inv, s1, c1] + unit
        planes += [(vel[j] - unit[j] * rate) * inv for j in range(3)]
        for number, value in enumerate(planes):
            geo[side, number, rows, :] = value
        for number, (a, s, c) in enumerate(WAVES[side](s1, c1)):
            waves[0, side * NR + number, rows, :] = s
            waves[1, side * NR + number, rows, :] = a * c
        return carry

    lv = (lv0, lv1)

    def build_pairs(m, target, side):
        upper = lax.broadcasted_iota(jnp.int32, (16, ROWS), 1) >= GHOSTS
        for start in range(0, ROWS, 16):
            rows = slice(start, start + 16)

            def twice(x):
                return jnp.concatenate([x, x], 1)

            e0, e1, rate = (geo[side, number, rows, :] for number in (E0, E1, DD))
            e1d, e0d = twice(e1 * rate), twice(e0 * rate)
            s = jnp.concatenate([waves[0, 2 * m + half, rows, :] for half in range(2)], 1)
            ac = jnp.concatenate([waves[1, 2 * m + half, rows, :] for half in range(2)], 1)
            b = twice(e0) * s
            bd = e1d * s + e0d * ac
            for number, value in enumerate((b, bd)):
                for half in range(2):
                    x = value[:, half * ROWS : (half + 1) * ROWS]
                    if side == 0:
                        found = ((2 * m + half, x),)
                    else:
                        q = 4 * (m - PAIRS) + 2 * half
                        found = ((q, jnp.where(upper, 0.0, x)), (q + 1, jnp.where(upper, x, 0.0)))
                    for q, x in found:
                        hi, lo = split(x)
                        cols = slice(side * ROWS, (side + 1) * ROWS)
                        at = place(q, ROWS) + start
                        bq[number, pl.ds(pl.multiple_of(at, 16), 16), cols] = hi
                        at = at + GROUP * ROWS
                        bq[number, pl.ds(pl.multiple_of(at, 16), 16), cols] = lo
            for j in range(3):
                u, w = twice(geo[side, U0 + j, rows, :]), twice(geo[side, W0 + j, rows, :])
                first = start + j * ROWS
                put_rows(target, b * u, first, first + 6 * ROWS)
                first += 3 * ROWS
                put_rows(target, bd * u + b * w, first, first + 6 * ROWS)

    def stream(left, i, rows, right, dims=NN):
        start = 2 * GROUP * rows * i
        full = pl.ds(pl.multiple_of(start, GROUP * rows), 2 * GROUP * rows)
        high = pl.ds(pl.multiple_of(start, GROUP * rows), GROUP * rows)
        both = mm(left[full, :], right[0], dims)
        rest = mm(left[high, :], right[1], dims)
        return both[0 : GROUP * rows] + both[GROUP * rows :] + rest

    def weighted(target, value, i, rows, filters):
        for k in range(GROUP):
            target[...] += value[k * rows : (k + 1) * rows, :] * filters[pl.ds(GROUP * i + k, 1), 0:F]

    def gather_vector(m, near):
        cols = pl.ds(pl.multiple_of(m * TILE, TILE), TILE)
        both = mm(near[...], pfv_s[0, cols, :])
        rest = mm(near[0 : 6 * ROWS, :], pfv_s[1, cols, :])
        accv[...] += both[0 : 6 * ROWS] + both[6 * ROWS :] + rest

    lax.fori_loop(0, ROWS // 8, functools.partial(geometry, side=0, table=c8[...]), 0)
    build_pairs(0, lv0, 0)
    pl.semaphore_wait(barrier, 8)
    coords = copies(csel, crecv, sendc, recvc, 1, True)
    first = copies(sel1, gemb, send1, recv1, 1, False)
    for copy in coords + first:
        copy.start()

    acc[...] = jnp.zeros((2 * ROWS, F), f32)
    accv[...] = jnp.zeros((6 * ROWS, F), f32)

    def two_tiles(k, carry, base, last, side):
        for half in range(2):
            m = base + 2 * k + half
            gather_vector(m, lv[half])
            build_pairs(jnp.minimum(m + 1, last), lv[1 - half], side)
        return carry

    lax.fori_loop(0, PAIRS // 2, functools.partial(two_tiles, base=0, last=PAIRS - 1, side=0), 0)

    for copy in coords + first:
        copy.wait()
    phi[ROWS:TABLE, :] = project(gemb[...], *w1)
    found = merged(crecv)
    twofold = found + pltpu.roll(found, GHOSTS, 1)
    lax.fori_loop(0, ROWS // 8, functools.partial(geometry, side=1, table=twofold), 0)
    build_pairs(PAIRS, lv0, 1)

    fill_ghosts(0, phi[ROWS:TABLE, 0:F])
    spread_ghosts(pfv_s, lambda: phi[ROWS:TABLE, F : 2 * F], f1, F)
    lax.fori_loop(
        0,
        (TILES - PAIRS) // 2,
        functools.partial(two_tiles, base=PAIRS, last=TILES - 1, side=1),
        0,
    )
    gather_vector(TILES - 1, lv0)


    def scalar_messages(i, carry):
        for number in range(2):
            value = stream(bq.at[number], i, ROWS, tab.at[0])
            weighted(acc.at[number * ROWS : (number + 1) * ROWS, :], value, i, ROWS, f1)
        return carry

    lax.fori_loop(0, GROUPS, scalar_messages, 0)
    lr[...] = mm3(split(accv[...]), (wlr_s[0], wlr_s[1]))

    def part(j, side):
        return lr[j * ROWS : (j + 1) * ROWS, side * F : (side + 1) * F]

    state = emb[...] + acc[0:ROWS, :]
    moved = acc[ROWS : 2 * ROWS, :]
    for j in range(3):
        state = state + part(j, 0) * part(j, 1)
        moved = moved + (part(3 + j, 0) * part(j, 1) + part(j, 0) * part(3 + j, 1))
    node[:, 0:F] = state
    node[:, F : 2 * F] = moved
    sel2[...] = select(node[...])
    second = copies(sel2, gnode, send2, recv2, 1, False)
    for copy in second:
        copy.start()

    w2 = (w2i_s[0], w2i_s[1]), (w2o_s[0], w2o_s[1])

    def table_two(values, moves, at, n):
        v = mm3(split(values), w2[0])
        vd = mm3(split(moves), w2[0])
        sig = sigmoid(v)
        pre2[0, at : at + n, :] = v
        pre2[1, at : at + n, :] = vd
        slope = sig * (1.0 + v * (1.0 - sig))
        phi2[0, at : at + n, :] = mm3(split(v * sig), w2[1])
        phi2[1, at : at + n, :] = mm3(split(slope * vd), w2[1])

    table_two(node[:, 0:F], node[:, F : 2 * F], 0, ROWS)

    for side in range(2):
        rows = ROWS if side == 0 else GHOSTS
        e0, e1, rate = (geo[side, number] for number in (E0, E1, DD))
        pg[side, 0] = e0.T
        pg[side, 1] = (e1 * rate).T
        pg[side, 2] = (e0 * rate).T
        pg[side, 3] = geo[side, S1].T
        pg[side, 4] = geo[side, C1].T

    def turned(side, count):
        def body(i, carry):
            start = pl.multiple_of(i * 16, 16)
            g = [pg[side, number, pl.ds(start, 16), :] for number in range(5)]
            for q, (a, s, c) in enumerate(own_waves(g[3], g[4])):
                hi, lo = split(jnp.concatenate([g[0] * s, g[1] * s + g[2] * (a * c)], 1))
                at = start + place(q, TABLE) + side * ROWS
                lt[pl.ds(pl.multiple_of(at, 16), 16), :] = hi
                lt[pl.ds(pl.multiple_of(at + GROUP * TABLE, 16), 16), :] = lo
            return carry

        lax.fori_loop(0, count // 16, body, 0)

    turned(0, ROWS)
    turned(1, GHOSTS)

    fill_own(1, phi2[0, 0:ROWS, :])
    fill_own(2, phi2[1, 0:ROWS, :])

    for copy in second:
        copy.wait()
    table_two(gnode[:, 0:F], gnode[:, F : 2 * F], ROWS, GHOSTS)
    fill_ghosts(1, phi2[0, ROWS:TABLE, :])
    fill_ghosts(2, phi2[1, ROWS:TABLE, :])
    acc[...] = jnp.zeros((2 * ROWS, F), f32)

    def messages_two(i, carry):
        value = stream(bq.at[0], i, ROWS, tab.at[1])
        weighted(acc.at[0:ROWS, :], value, i, ROWS, f2)
        value = stream(bq.at[1], i, ROWS, tab.at[1]) + stream(bq.at[0], i, ROWS, tab.at[2])
        weighted(acc.at[ROWS : 2 * ROWS, :], value, i, ROWS, f2)
        return carry

    lax.fori_loop(0, GROUPS, messages_two, 0)
    st = node[:, 0:F] + acc[0:ROWS, :]
    std = node[:, F : 2 * F] + acc[ROWS : 2 * ROWS, :]

    whs = wh_s[0], wh_s[1]
    v = mm3(split(st), whs)
    vd = mm3(split(std), whs)
    sig = sigmoid(v)
    live = lax.broadcasted_iota(jnp.int32, (ROWS, F), 0) < cnt[0]
    top = jnp.where(live, jnp.broadcast_to(we[...], (ROWS, F)), 0.0)
    mu[0] = mm3(split(top * (sig * (1.0 + v * (1.0 - sig)))), whs, NT)
    mu[1] = mm3(
        split(top * (sig * (1.0 - sig) * (2.0 + v * (1.0 - 2.0 * sig))) * vd), whs, NT
    )

    for number in range(2):
        hi, lo = split(mu[number])
        for part_of, value in ((0, hi), (1, lo)):
            wmu[part_of, 0:ROWS, number * F : (number + 1) * F] = value
            if number == 0:
                wmu[part_of, ROWS : 2 * ROWS, F : 2 * F] = value
    wmu[:, ROWS : 2 * ROWS, 0:F] = jnp.zeros((2, ROWS, F), bf16)
    bar[...] = jnp.zeros((2 * TABLE, F), f32)

    def turned_messages(i, carry):
        value = stream(lt, i, TABLE, wmu)
        weighted(bar.at[0:TABLE, :], value[:, 0:F], i, TABLE, f2)
        weighted(bar.at[TABLE : 2 * TABLE, :], value[:, F : 2 * F], i, TABLE, f2)
        return carry

    lax.fori_loop(0, GROUPS, turned_messages, 0)
    back = mm3(split(bar[...]), w2[1], NT)
    v, vd = pre2[0], pre2[1]
    sig = sigmoid(v)
    slope = sig * (1.0 + v * (1.0 - sig))
    curve = sig * (1.0 - sig) * (2.0 + v * (1.0 - 2.0 * sig))
    bar[0:TABLE, :] = back[0:TABLE] * slope
    bar[TABLE : 2 * TABLE, :] = back[TABLE : 2 * TABLE] * slope + back[0:TABLE] * curve * vd
    bar[...] = mm3(split(bar[...]), w2[0], NT)
    src3[:, 0:F] = bar[ROWS:TABLE, :]
    src3[:, F : 2 * F] = bar[TABLE + ROWS : 2 * TABLE, :]
    third = copies(src3, rnode, send3, recv3, -1, False)
    for copy in third:
        copy.start()

    def scale_rows(q, carry, filters):
        weights = filters[pl.ds(q, 1), 0:F]
        for number in range(2):
            hi, lo = split(mu[number] * weights)
            at = place(q, ROWS)
            scaled[number, pl.ds(pl.multiple_of(at, ROWS), ROWS), :] = hi
            scaled[number, pl.ds(pl.multiple_of(at + GROUP * ROWS, ROWS), ROWS), :] = lo
        return carry

    lax.fori_loop(0, NR, functools.partial(scale_rows, filters=f2), 0)

    def pairs_two(i, carry):
        rows = pl.ds(pl.multiple_of(i * GROUP * ROWS, ROWS), GROUP * ROWS)
        two[0, rows, :] = stream(scaled.at[0], i, ROWS, tab.at[1], NT)
        two[1, rows, :] = stream(scaled.at[1], i, ROWS, tab.at[1], NT) + stream(
            scaled.at[0], i, ROWS, tab.at[2], NT
        )
        return carry

    lax.fori_loop(0, GROUPS, pairs_two, 0)

    for copy in third:
        copy.wait()
    rows_back = onehot[0, :, 0:GHOSTS].astype(bf16)
    hi, lo = split(rnode[...])
    returned = mm(rows_back, hi) + mm(rows_back, lo)
    nu = mu[0] + bar[0:ROWS, :] + returned[:, 0:F]
    nud = mu[1] + bar[TABLE : TABLE + ROWS, :] + returned[:, F : 2 * F]
    mu[0] = nu
    mu[1] = nud

    wlr = wlr_s[0], wlr_s[1]
    for j in range(3):
        nu, nud = mu[0], mu[1]
        l, r, ld, rd = part(j, 0), part(j, 1), part(3 + j, 0), part(3 + j, 1)
        lr[j * ROWS : (j + 1) * ROWS, 0:F] = nu * r
        lr[j * ROWS : (j + 1) * ROWS, F : 2 * F] = nu * l
        lr[(3 + j) * ROWS : (4 + j) * ROWS, 0:F] = nud * r + nu * rd
        lr[(3 + j) * ROWS : (4 + j) * ROWS, F : 2 * F] = nud * l + nu * ld
    hi, lo = split(mm3(split(lr[...]), wlr, NT))
    vbar[0 : 6 * ROWS, :] = hi
    vbar[6 * ROWS :, :] = lo
    lax.fori_loop(0, NR, functools.partial(scale_rows, filters=f1), 0)

    def pairs_scalar(i, carry):
        rows = pl.ds(pl.multiple_of(i * GROUP * ROWS, ROWS), GROUP * ROWS)
        for number in range(2):
            two[number, rows, :] += stream(scaled.at[number], i, ROWS, tab.at[0], NT)
        return carry

    lax.fori_loop(0, GROUPS, pairs_scalar, 0)
    out = (out0, out1)

    def pairs_one(m, target):
        cols = pl.ds(pl.multiple_of(m * TILE, TILE), TILE)
        both = mm(vbar[...], pfv_s[0, cols, :], NT)
        rest = mm(vbar[0 : 6 * ROWS, :], pfv_s[1, cols, :], NT)
        target[...] = both[0 : 6 * ROWS] + both[6 * ROWS :] + rest

    upper = lax.broadcasted_iota(jnp.int32, (8, ROWS), 1) >= GHOSTS

    def sum_waves(m, source, side):
        if side == 0:
            first = [2 * m + half for half in range(2)]
            a = [KAPPA * (q + 1).astype(f32) for q in first]
        else:
            first = [4 * (m - PAIRS) + 2 * half for half in range(2)]
            a = [KAPPA * ((q + 1).astype(f32) + jnp.where(upper, 1.0, 0.0)) for q in first]
        aa = [x * x for x in a]
        for start in range(0, ROWS, 8):
            rows = slice(start, start + 8)
            u = [geo[side, U0 + j, rows, :] for j in range(3)]
            total = [sums[side, number, rows, :] for number in range(14)]
            for half in range(2):
                s = waves[0, 2 * m + half, rows, :]
                ac = waves[1, 2 * m + half, rows, :]
                ss = s * aa[half]
                cols = slice(half * ROWS, (half + 1) * ROWS)
                y = [source[start + k * ROWS : start + k * ROWS + 8, cols] for k in range(6)]
                own = slice(side * ROWS, (side + 1) * ROWS)
                near = []
                for number in range(2):
                    at = pl.multiple_of(first[half] * ROWS + start, 8)
                    value = two[number, pl.ds(at, 8), own]
                    if side == 1:
                        at = pl.multiple_of(at + ROWS, 8)
                        value = jnp.where(upper, two[number, pl.ds(at, 8), own], value)
                    near.append(value)
                along = near[0] + u[0] * y[0] + u[1] * y[1] + u[2] * y[2]
                along_d = near[1] + u[0] * y[3] + u[1] * y[4] + u[2] * y[5]
                for j in range(3):
                    total[j] += s * y[j]
                    total[3 + j] += ac * y[j]
                    total[6 + j] += s * y[3 + j]
                total[9] += s * near[0]
                total[10] += ac * near[0]
                total[11] += ss * along
                total[12] += s * near[1]
                total[13] += ac * along_d
            for number in range(14):
                sums[side, number, rows, :] = total[number]

    sums[...] = jnp.zeros(sums.shape, f32)
    pairs_one(PAIRS, out0)

    def two_sums(k, carry, first, second, base, last, side):
        for half in range(2):
            ahead, behind = (first, second) if half == 0 else (second, first)
            m = base + 2 * k + half
            pairs_one(jnp.minimum(m + 1, last), ahead)
            sum_waves(m, behind, side)
        return carry

    lax.fori_loop(
        0,
        (TILES - PAIRS) // 2,
        functools.partial(two_sums, first=out1, second=out0, base=PAIRS, last=TILES - 1, side=1),
        0,
    )
    pairs_one(0, out1)
    sum_waves(jnp.int32(TILES - 1), out0, 1)

    def offsets_back(i, carry, side):
        rows = pl.ds(pl.multiple_of(i * 8, 8), 8)
        e0, e1, e2, rate, inv = (geo[side, number, rows, :] for number in range(5))
        unit = [geo[side, U0 + j, rows, :] for j in range(3)]
        turn = [geo[side, W0 + j, rows, :] for j in range(3)]
        z = [sums[side, number, rows, :] for number in range(14)]
        db = e1 * z[9] + e0 * z[10]
        dbd = e2 * z[9] + 2.0 * e1 * z[10] - e0 * z[11]
        inner = z[12]
        w = jnp.zeros((8, ROWS), f32)
        wd = w
        spin = w
        ub, ubd = [], []
        for j in range(3):
            slope = e1 * z[j] + e0 * z[3 + j]
            ub.append(e0 * z[j])
            ubd.append(rate * slope + e0 * z[6 + j])
            db = db + unit[j] * slope
            dbd = dbd + unit[j] * (e2 * z[j] + 2.0 * e1 * z[3 + j])
            inner = inner + unit[j] * z[6 + j]
            spin = spin + turn[j] * slope
            w = w + unit[j] * ub[j]
            wd = wd + turn[j] * ub[j] + unit[j] * ubd[j]
        dbd = rate * dbd + e1 * inner + e0 * z[13] + spin
        for j in range(3):
            t = (ub[j] - unit[j] * w) * inv
            pg[side, j, rows, :] = db * unit[j] + t
            pg[side, 3 + j, rows, :] = (
                dbd * unit[j]
                + db * turn[j]
                + (ubd[j] - turn[j] * w - unit[j] * wd - t * rate) * inv
            )
        return carry

    lax.fori_loop(0, ROWS // 8, functools.partial(offsets_back, side=1), 0)
    gpos[...] = jnp.zeros((8, ROWS), f32)
    c8[...] = jnp.zeros((8, ROWS), f32)
    for j in range(6):
        ghosts = pg[1, j]
        gpos[j : j + 1, :] = jnp.sum(ghosts, axis=0, keepdims=True)
        c8[j : j + 1, :] = jnp.sum(ghosts.T, axis=0, keepdims=True)
    both = gpos[...]
    gpos[...] = both + pltpu.roll(both, GHOSTS, 1)
    last = copies(gpos, rpos, send4, recv4, -1, True)
    for copy in last:
        copy.start()

    lax.fori_loop(
        0,
        PAIRS // 2,
        functools.partial(two_sums, first=out0, second=out1, base=0, last=PAIRS - 1, side=0),
        0,
    )
    lax.fori_loop(0, ROWS // 8, functools.partial(offsets_back, side=0), 0)
    for j in range(6):
        own = pg[0, j]
        c8[j : j + 1, :] = jnp.sum(own - own.T, axis=0, keepdims=True) - c8[j : j + 1, :]
    for copy in last:
        copy.wait()
    hi, mid, lo = split3(merged(rpos))
    slots = onehot[1].astype(bf16)
    total = c8[...] + (mm(hi, slots) + (mm(mid, slots) + mm(lo, slots)))
    force[...] = -total[0:3, :]
    hess[...] = -total[3:6, :]


def per_device(nx, ny, *arrays):
    arrays = list(arrays)
    arrays[15] = arrays[15].reshape(1, F)
    vmem = pl.BlockSpec(memory_space=pltpu.VMEM)
    in_specs = [pl.BlockSpec(memory_space=pl.ANY)] * 16
    in_specs[3] = pl.BlockSpec(memory_space=pltpu.SMEM)

    def v32(*shape):
        return pltpu.VMEM(shape, f32)

    def v16(*shape):
        return pltpu.VMEM(shape, bf16)

    dma = pltpu.SemaphoreType.DMA((8,))
    scratch = [
        v32(3, ROWS),
        v32(3, ROWS),
        v32(ROWS, F),
        pltpu.VMEM(arrays[4].shape, jnp.int32),
        pltpu.VMEM((1, GHOSTS), jnp.int32),
        v32(NR, 2 * F),
        v32(NR, F),
        v32(1, F),
        v16(2, F, F),
        v16(2, F, 2 * F),
        v16(2, F, 2 * F),
        v16(2, F, F),
        v16(2, F, F),
        v16(2, F, F),
        pltpu.VMEM((8, ROWS), jnp.int32),
        v32(8, ROWS),
        v32(8, ROWS),
        v32(8, 8, ROWS),
        v32(GHOSTS, F),
        v32(GHOSTS, F),
        v32(GHOSTS, 2 * F),
        v32(GHOSTS, 2 * F),
        v32(GHOSTS, 2 * F),
        v32(GHOSTS, 2 * F),
        v32(8, ROWS),
        v32(8, 8, ROWS),
        v32(2, ROWS, ROWS),
        v32(2, ROWS, ROWS),
        v32(6, ROWS, ROWS),
        v32(2, 13, ROWS, ROWS),
        v32(2, NR + PAIRS, ROWS, ROWS),
        v16(2, 2 * NR * ROWS, TILE),
        v16(12 * ROWS, TILE),
        v16(12 * ROWS, TILE),
        v16(2 * NR * TABLE, 2 * ROWS),
        v16(2, WIDE, F),
        v16(3, 2, 2 * ROWS, F),
        v16(2, 2 * ROWS, 2 * F),
        v16(2, 2 * NR * ROWS, F),
        v32(TABLE, 2 * F),
        v32(2 * ROWS, F),
        v32(6 * ROWS, F),
        v32(6 * ROWS, 2 * F),
        v32(ROWS, 2 * F),
        v32(2, TABLE, F),
        v32(2, TABLE, F),
        v32(2, ROWS, F),
        v32(2 * TABLE, F),
        v32(6 * ROWS, TILE),
        v32(6 * ROWS, TILE),
        v32(3 * F, 3 * F),
        v32(2, NR * ROWS, TILE),
        v32(2, 14, ROWS, ROWS),
        v16(12 * ROWS, F),
        v32(2, 6, ROWS, ROWS),
    ] + [dma] * 10 + [pltpu.SemaphoreType.DMA((15,))]
    out = jax.ShapeDtypeStruct((3, ROWS), f32)
    return pl.pallas_call(
        functools.partial(kernel, nx, ny),
        out_shape=(out, out),
        in_specs=in_specs,
        out_specs=(vmem, vmem),
        scratch_shapes=scratch,
        compiler_params=pltpu.CompilerParams(
            collective_id=0, has_side_effects=True, vmem_limit_bytes=67043328
        ),
    )(*arrays)


def solution(mesh):
    placed = (
        P(None, ("bx", "by")),
        P(None, ("bx", "by")),
        P(("bx", "by"), None),
        P(("bx", "by")),
        P(None, ("bx", "by")),
        P(("bx", "by"), None),
    ) + (P(),) * 10
    return jax.shard_map(
        functools.partial(per_device, mesh.shape["bx"], mesh.shape["by"]),
        mesh=mesh,
        in_specs=placed,
        out_specs=(P(None, ("bx", "by")), P(None, ("bx", "by"))),
        check_vma=False,
    )
```

```python
import functools
import math

import jax
import jax.numpy as jnp
from jax import lax
from jax.experimental import pallas as pl
from jax.experimental.pallas import tpu as pltpu
from jax.sharding import PartitionSpec as P

MESH = pl.DeviceIdType.MESH
f32 = jnp.float32
bf16 = jnp.bfloat16
offsets = ((-1, -1), (-1, 0), (-1, 1), (0, -1), (0, 1), (1, -1), (1, 0), (1, 1))
NN = (((1,), (0,)), ((), ()))
NT = (((1,), (1,)), ((), ()))
KAPPA = math.pi / 3.0
SOFT = 0.01
ROWS = 128
GHOSTS = 64
TABLE = ROWS + GHOSTS
F = 256
NR = 20
PAIRS = NR // 2
TILE = 256
TILES = NR * TABLE // TILE
WIDE = TILES * TILE
STEP = 5 * TILE
STEPS = WIDE // STEP
OWN_STEPS = 2


def split(x):
    hi = x.astype(bf16)
    return hi, (x - hi.astype(f32)).astype(bf16)


def split3(x):
    hi = x.astype(bf16)
    rest = x - hi.astype(f32)
    mid = rest.astype(bf16)
    return hi, mid, (rest - mid.astype(f32)).astype(bf16)


def mm(a, b, dims=NN):
    return lax.dot_general(a, b, dims, preferred_element_type=f32)


def mm3(a, b, dims=NN):
    return mm(a[0], b[0], dims) + (mm(a[1], b[0], dims) + mm(a[0], b[1], dims))


def pick(refs, *index):
    return refs[0][index], refs[1][index]


def put(refs, value, *index):
    hi, lo = split(value)
    refs[0][index] = hi
    refs[1][index] = lo


def sin_cos(angle):
    turns = jnp.floor(angle * (0.5 / math.pi) + 0.5)
    half = 0.5 * ((angle - turns * 6.28125) - turns * (2.0 * math.pi - 6.28125))
    sq = half * half
    odd = 1.0 / 39916800.0
    for c in (1.0 / 362880.0, 1.0 / 5040.0, 1.0 / 120.0, 1.0 / 6.0, 1.0):
        odd = c - sq * odd
    sh = half * odd
    even = 1.0 / 479001600.0
    for c in (1.0 / 3628800.0, 1.0 / 40320.0, 1.0 / 720.0, 1.0 / 24.0, 0.5, 1.0):
        even = c - sq * even
    return 2.0 * sh * even, 1.0 - 2.0 * sh * sh


def sigmoid(v):
    return 1.0 / (1.0 + jnp.exp(-v))


def own_waves(s1, c1):
    twice = 2.0 * c1
    before_s, before_c = jnp.zeros_like(s1), jnp.ones_like(c1)
    s, c = s1, c1
    for q in range(NR):
        yield (q + 1) * KAPPA, s, c
        if q < NR - 1:
            s, before_s = twice * s - before_s, s
            c, before_c = twice * c - before_c, c


def ghost_waves(s1, c1):
    upper = lax.broadcasted_iota(jnp.int32, s1.shape, 1) >= GHOSTS
    s2, c2 = 2.0 * s1 * c1, 1.0 - 2.0 * s1 * s1
    twice = 2.0 * c2
    s, before_s = jnp.where(upper, s2, s1), jnp.where(upper, 0.0, -s1)
    c, before_c = jnp.where(upper, c2, c1), jnp.where(upper, 1.0, c1)
    shift = jnp.where(upper, 2.0 * KAPPA, KAPPA)
    for p in range(PAIRS):
        yield shift + 2.0 * p * KAPPA, s, c
        if p < PAIRS - 1:
            s, before_s = twice * s - before_s, s
            c, before_c = twice * c - before_c, c


E0, E1, E2, DD, IV, S1, C1, U0, W0 = 0, 1, 2, 3, 4, 5, 6, 7, 10
WAVES = (own_waves, ghost_waves)


def kernel(
    nx,
    ny,
    pos_in,
    tan_in,
    emb_in,
    cnt,
    nbr_in,
    snd_in,
    w1i,
    w1o,
    f1_in,
    wl,
    wr,
    w2i,
    w2o,
    f2_in,
    wh,
    we_in,
    force,
    hess,
    pos,
    tan,
    emb,
    nbr,
    snd,
    f1,
    f2,
    we,
    w1i_s,
    w1o_s,
    wlr_s,
    w2i_s,
    w2o_s,
    wh_s,
    sndpad,
    c8,
    csel,
    crecv,
    sel1,
    gemb,
    sel2,
    gnode,
    src3,
    rnode,
    gpos,
    rpos,
    onehot,
    mask,
    colb,
    geo,
    waves,
    lb,
    lv0,
    lv1,
    lt,
    pfs_s,
    pfv_s,
    p2_s,
    p2d_s,
    muf,
    phi,
    acc,
    accv,
    lr,
    node,
    pre2,
    phi2,
    mu,
    bar,
    out0,
    out1,
    landing,
    two,
    sums,
    vbar,
    nus,
    pg,
    send1,
    recv1,
    sendc,
    recvc,
    send2,
    recv2,
    send3,
    recv3,
    send4,
    recv4,
    loads,
):
    ix, iy = lax.axis_index("bx"), lax.axis_index("by")

    def device(g, sign):
        dx, dy = offsets[g]
        return (lax.rem(ix + sign * dx + nx, nx), lax.rem(iy + sign * dy + ny, ny))

    barrier = pltpu.get_barrier_semaphore()
    for g in range(8):
        pl.semaphore_signal(barrier, inc=1, device_id=device(g, 1), device_id_type=MESH)

    def block(ref, g):
        return ref.at[pl.ds(g * 8, 8), :]

    def copies(source, target, sends, recvs, sign, whole):
        return [
            pltpu.make_async_remote_copy(
                src_ref=source if whole else block(source, g),
                dst_ref=target.at[g] if whole else block(target, g),
                send_sem=sends.at[g],
                recv_sem=recvs.at[g],
                device_id=device(g, sign),
                device_id_type=MESH,
            )
            for g in range(8)
        ]

    def select(x):
        hi, lo = split(x)
        rows = onehot[1, 0:GHOSTS, :].astype(bf16)
        return mm(rows, hi) + mm(rows, lo)

    lane = lax.broadcasted_iota(jnp.int32, (8, ROWS), 1)
    group = lax.div(lane, 8)

    def merged(ref):
        total = jnp.where(group == 0, ref[0], 0.0)
        for g in range(1, 8):
            total = total + jnp.where(group == g, ref[g], 0.0)
        return total

    weights = []
    spots = ((0, 0), (0, F), (1, 0), (1, F), (1, 2 * F), (2, 0), (2, F))
    for number, (w, (down, at)) in enumerate(zip((w1i, w1o, wl, wr, w2i, w2o, wh), spots)):
        place = landing.at[down * F : (down + 1) * F, at : at + w.shape[1]]
        weights.append((pltpu.make_async_copy(w, place, loads.at[number]), place))
    small = {}
    named = ((snd_in, snd), (pos_in, pos), (tan_in, tan), (emb_in, emb), (nbr_in, nbr))
    named += ((f1_in, f1), (f2_in, f2), (we_in, we))
    for number, (source, place) in enumerate(named):
        small[number] = pltpu.make_async_copy(source, place, loads.at[7 + number])
        small[number].start()
    for copy, _ in weights:
        copy.start()
    for number in range(4):
        small[number].wait()

    sndpad[...] = jnp.full((8, ROWS), -1, jnp.int32)
    sndpad[0:1, 0:GHOSTS] = snd[...]
    hot = jnp.where(
        lax.broadcasted_iota(jnp.int32, (ROWS, ROWS), 0) == sndpad[0:1, :], 1.0, 0.0
    )
    onehot[0] = hot
    onehot[1] = hot.T
    c8[...] = jnp.zeros((8, ROWS), f32)
    c8[0:3, :] = pos[...]
    c8[3:6, :] = tan[...]
    hi, mid, lo = split3(c8[...])
    hot16 = hot.astype(bf16)
    csel[...] = mm(hi, hot16) + (mm(mid, hot16) + mm(lo, hot16))
    sel1[...] = select(emb[...])
    stores = ((w1i_s, 0), (w1o_s, 0), (wlr_s, 0), (wlr_s, F), (w2i_s, 0), (w2o_s, 0), (wh_s, 0))
    for (refs, at), (copy, place) in zip(stores, weights):
        copy.wait()
        hi, lo = split(place[...])
        refs[0, :, at : at + hi.shape[1]] = hi
        refs[1, :, at : at + hi.shape[1]] = lo

    small[4].wait()
    row = lax.broadcasted_iota(jnp.int32, (ROWS, ROWS), 0)
    ghost = lax.rem(row, GHOSTS)
    for side, slots in ((0, row), (1, ROWS + (7 - lax.div(ghost, 8)) * 8 + lax.rem(ghost, 8))):

        def mark(k, total, slots=slots):
            return jnp.where(slots == nbr[pl.ds(k, 1), :], 1.0, total)

        listed = lax.fori_loop(0, nbr.shape[0], mark, jnp.zeros((ROWS, ROWS), f32))
        mask[side] = listed.T

    for number in (5, 6, 7):
        small[number].wait()

    def project(rows, first_w, second_w):
        v = mm3(split(rows), first_w)
        return mm3(split(v * sigmoid(v)), second_w)

    w1 = (w1i_s[0], w1i_s[1]), (w1o_s[0], w1o_s[1])
    phi[0:ROWS, :] = project(emb[...], *w1)
    for j in range(6):
        colb[j] = jnp.broadcast_to(c8[j : j + 1, :], (ROWS, ROWS)).T

    def put2(refs, value, start):
        hi, lo = split(value)
        refs[0, pl.ds(start, value.shape[0]), :] = hi
        refs[1, pl.ds(start, value.shape[0]), :] = lo

    def spread_own(refs, table, filters, at):
        def body(q, carry):
            weights = filters[pl.ds(q, 1), at : at + F]
            put2(refs, table() * weights, pl.multiple_of(q * ROWS, ROWS))
            return carry

        lax.fori_loop(0, NR, body, 0)

    def spread_ghosts(refs, table, filters, at):
        def body(q, carry):
            weights = filters[pl.ds(q, 1), at : at + F]
            put2(refs, table() * weights, pl.multiple_of(NR * ROWS + q * GHOSTS, GHOSTS))
            return carry

        lax.fori_loop(0, NR, body, 0)

    def put_rows(ref, value, first, second, cols):
        hi, lo = split(value)
        ref[first : first + 16, cols] = hi
        ref[second : second + 16, cols] = lo

    spread_own(pfs_s, lambda: phi[0:ROWS, 0:F], f1, 0)
    spread_own(pfv_s, lambda: phi[0:ROWS, F : 2 * F], f1, F)

    scale = 1.0 / math.sqrt(nbr.shape[0])

    def geometry(i, carry, side, table):
        rows = pl.ds(pl.multiple_of(i * 8, 8), 8)
        centre = [colb[j, rows, :] for j in range(6)]
        off = [table[j : j + 1, :] - centre[j] for j in range(3)]
        vel = [table[j : j + 1, :] - centre[j] for j in range(3, 6)]
        listed = mask[side, rows, :]
        sq = off[0] * off[0] + off[1] * off[1] + off[2] * off[2]
        sq = jnp.where(listed > 0.0, sq, 1.0) + SOFT
        inv = lax.rsqrt(sq)
        inv = inv * (1.5 - 0.5 * sq * inv * inv)
        dist = sq * inv
        unit = [x * inv for x in off]
        rate = unit[0] * vel[0] + unit[1] * vel[1] + unit[2] * vel[2]
        s1, c1 = sin_cos(KAPPA * dist)
        weight = scale * listed
        env = 0.5 * (c1 + 1.0)
        env1 = (-0.5 * KAPPA) * s1
        env2 = (-0.5 * KAPPA * KAPPA) * c1
        e0 = weight * env * inv
        slope = env1 - env * inv
        e1 = weight * inv * slope
        e2 = weight * inv * (env2 - 2.0 * inv * slope)
        planes = [e0, e1, e2, rate, inv, s1, c1] + unit
        planes += [(vel[j] - unit[j] * rate) * inv for j in range(3)]
        for number, value in enumerate(planes):
            geo[side, number, rows, :] = value
        for number, (a, s, c) in enumerate(WAVES[side](s1, c1)):
            waves[0, side * NR + number, rows, :] = s
            waves[1, side * NR + number, rows, :] = a * c
        return carry

    lv = (lv0, lv1)

    def build_pairs(m, target):
        side = jnp.where(m < PAIRS, 0, 1)
        cols = pl.ds(pl.multiple_of(m * TILE, TILE), TILE)
        for start in range(0, ROWS, 16):
            rows = slice(start, start + 16)

            def twice(x):
                return jnp.concatenate([x, x], 1)

            e0, e1, rate = (geo[side, number, rows, :] for number in (E0, E1, DD))
            e1d, e0d = twice(e1 * rate), twice(e0 * rate)
            s = jnp.concatenate([waves[0, 2 * m + half, rows, :] for half in range(2)], 1)
            ac = jnp.concatenate([waves[1, 2 * m + half, rows, :] for half in range(2)], 1)
            b = twice(e0) * s
            bd = e1d * s + e0d * ac
            put_rows(lb, bd, start, start + 3 * ROWS, cols)
            put_rows(lb, b, start + ROWS, start + 2 * ROWS, cols)
            for j in range(3):
                u, w = twice(geo[side, U0 + j, rows, :]), twice(geo[side, W0 + j, rows, :])
                first = start + j * ROWS
                put_rows(target, b * u, first, first + 6 * ROWS, slice(None))
                first += 3 * ROWS
                put_rows(target, bd * u + b * w, first, first + 6 * ROWS, slice(None))

    def add_to(ref, rows, value, i):
        if i == 0:
            ref[rows, :] = value
        else:
            ref[rows, :] += value

    def gather_scalar(refs, cols):
        both = mm(lb[:, cols], refs[0, cols, :])
        rest = mm(lb[0 : 2 * ROWS, cols], refs[1, cols, :])
        acc[0:ROWS, :] += both[ROWS : 2 * ROWS] + both[2 * ROWS : 3 * ROWS] + rest[ROWS:]
        acc[ROWS : 2 * ROWS, :] += both[0:ROWS] + both[3 * ROWS :] + rest[0:ROWS]

    def gather_vector(m, near):
        cols = pl.ds(pl.multiple_of(m * TILE, TILE), TILE)
        both = mm(near[...], pfv_s[0, cols, :])
        rest = mm(near[0 : 6 * ROWS, :], pfv_s[1, cols, :])
        accv[...] += both[0 : 6 * ROWS] + both[6 * ROWS :] + rest

    lax.fori_loop(0, ROWS // 8, functools.partial(geometry, side=0, table=c8[...]), 0)
    build_pairs(0, lv0)
    pl.semaphore_wait(barrier, 8)
    coords = copies(csel, crecv, sendc, recvc, 1, True)
    first = copies(sel1, gemb, send1, recv1, 1, False)
    for copy in coords + first:
        copy.start()

    acc[...] = jnp.zeros((2 * ROWS, F), f32)
    accv[...] = jnp.zeros((6 * ROWS, F), f32)

    def two_tiles(k, carry, base, last):
        for half in range(2):
            m = base + 2 * k + half
            gather_vector(m, lv[half])
            build_pairs(jnp.minimum(m + 1, last), lv[1 - half])
        return carry

    lax.fori_loop(0, PAIRS // 2, functools.partial(two_tiles, base=0, last=PAIRS - 1), 0)

    for copy in coords + first:
        copy.wait()
    phi[ROWS:TABLE, :] = project(gemb[...], *w1)
    found = merged(crecv)
    twofold = found + pltpu.roll(found, GHOSTS, 1)
    lax.fori_loop(0, ROWS // 8, functools.partial(geometry, side=1, table=twofold), 0)
    build_pairs(PAIRS, lv0)

    spread_ghosts(pfs_s, lambda: phi[ROWS:TABLE, 0:F], f1, 0)
    spread_ghosts(pfv_s, lambda: phi[ROWS:TABLE, F : 2 * F], f1, F)
    lax.fori_loop(
        0, (TILES - PAIRS) // 2, functools.partial(two_tiles, base=PAIRS, last=TILES - 1), 0
    )
    gather_vector(TILES - 1, lv0)


    def scalar_step(i, carry):
        gather_scalar(pfs_s, pl.ds(pl.multiple_of(i * STEP, STEP), STEP))
        return carry

    lax.fori_loop(0, STEPS, scalar_step, 0)
    lr[...] = mm3(split(accv[...]), (wlr_s[0], wlr_s[1]))

    def part(j, side):
        return lr[j * ROWS : (j + 1) * ROWS, side * F : (side + 1) * F]

    state = emb[...] + acc[0:ROWS, :]
    moved = acc[ROWS : 2 * ROWS, :]
    for j in range(3):
        state = state + part(j, 0) * part(j, 1)
        moved = moved + (part(3 + j, 0) * part(j, 1) + part(j, 0) * part(3 + j, 1))
    node[:, 0:F] = state
    node[:, F : 2 * F] = moved
    sel2[...] = select(node[...])
    second = copies(sel2, gnode, send2, recv2, 1, False)
    for copy in second:
        copy.start()

    w2 = (w2i_s[0], w2i_s[1]), (w2o_s[0], w2o_s[1])

    def table_two(values, moves, at, n):
        v = mm3(split(values), w2[0])
        vd = mm3(split(moves), w2[0])
        sig = sigmoid(v)
        pre2[0, at : at + n, :] = v
        pre2[1, at : at + n, :] = vd
        slope = sig * (1.0 + v * (1.0 - sig))
        phi2[0, at : at + n, :] = mm3(split(v * sig), w2[1])
        phi2[1, at : at + n, :] = mm3(split(slope * vd), w2[1])

    table_two(node[:, 0:F], node[:, F : 2 * F], 0, ROWS)

    for side in range(2):
        rows = ROWS if side == 0 else GHOSTS
        e0, e1, rate = (geo[side, number] for number in (E0, E1, DD))
        pg[side, 0] = e0.T
        pg[side, 1] = (e1 * rate).T
        pg[side, 2] = (e0 * rate).T
        pg[side, 3] = geo[side, S1].T
        pg[side, 4] = geo[side, C1].T

    def turned(side, count):
        def body(i, carry):
            start = pl.multiple_of(i * 16, 16)
            g = [pg[side, number, pl.ds(start, 16), :] for number in range(5)]
            held = None
            for q, (a, s, c) in enumerate(own_waves(g[3], g[4])):
                new = (g[0] * s, g[1] * s + g[2] * (a * c))
                if q % 2 == 0:
                    held = new
                    continue
                cols = slice((q - 1) * ROWS, (q + 1) * ROWS)
                for value, first, second in ((1, 0, 3), (0, 1, 2)):
                    hi, lo = split(jnp.concatenate([held[value], new[value]], 1))
                    at = 4 * side * ROWS
                    lt[pl.ds(start + at + first * count, 16), cols] = hi
                    lt[pl.ds(start + at + second * count, 16), cols] = lo
            return carry

        lax.fori_loop(0, count // 16, body, 0)

    turned(0, ROWS)
    turned(1, GHOSTS)

    spread_own(p2_s, lambda: phi2[0, 0:ROWS, :], f2, 0)
    spread_own(p2d_s, lambda: phi2[1, 0:ROWS, :], f2, 0)
    acc[...] = jnp.zeros((2 * ROWS, F), f32)

    def messages_two(i, carry):
        cols = pl.ds(pl.multiple_of(i * STEP, STEP), STEP)
        gather_scalar(p2_s, cols)
        both = mm(lb[ROWS : 3 * ROWS, cols], p2d_s[0, cols, :])
        rest = mm(lb[ROWS : 2 * ROWS, cols], p2d_s[1, cols, :])
        acc[ROWS : 2 * ROWS, :] += both[0:ROWS] + both[ROWS:] + rest
        return carry

    lax.fori_loop(0, OWN_STEPS, messages_two, 0)

    for copy in second:
        copy.wait()
    table_two(gnode[:, 0:F], gnode[:, F : 2 * F], ROWS, GHOSTS)
    spread_ghosts(p2_s, lambda: phi2[0, ROWS:TABLE, :], f2, 0)
    spread_ghosts(p2d_s, lambda: phi2[1, ROWS:TABLE, :], f2, 0)
    messages_two(OWN_STEPS, 0)
    st = node[:, 0:F] + acc[0:ROWS, :]
    std = node[:, F : 2 * F] + acc[ROWS : 2 * ROWS, :]

    whs = wh_s[0], wh_s[1]
    v = mm3(split(st), whs)
    vd = mm3(split(std), whs)
    sig = sigmoid(v)
    live = lax.broadcasted_iota(jnp.int32, (ROWS, F), 0) < cnt[0]
    top = jnp.where(live, jnp.broadcast_to(we[...], (ROWS, F)), 0.0)
    mu[0] = mm3(split(top * (sig * (1.0 + v * (1.0 - sig)))), whs, NT)
    mu[1] = mm3(
        split(top * (sig * (1.0 - sig) * (2.0 + v * (1.0 - 2.0 * sig))) * vd), whs, NT
    )

    def scaled(i):
        for q in range(4 * i, 4 * i + 4):
            weights = f2[q : q + 1, :]
            rows = slice(q % 4 * ROWS, (q % 4 + 1) * ROWS)
            for number in range(2):
                hi, lo = split(mu[number] * weights)
                muf[i, 2 * number, rows, :] = hi
                muf[i, 2 * number + 1, rows, :] = lo

    def turned_messages(i, at, count):
        cols = slice(i * 4 * ROWS, (i + 1) * 4 * ROWS)
        top = 4 * at
        both = mm(lt[top : top + 4 * count, cols], muf[i, 0])
        rest = mm(lt[top : top + 2 * count, cols], muf[i, 1])
        also = mm(lt[top + count : top + 3 * count, cols], muf[i, 2])
        more = mm(lt[top + count : top + 2 * count, cols], muf[i, 3])
        add_to(
            bar,
            slice(at, at + count),
            both[count : 2 * count] + both[2 * count : 3 * count] + rest[count:],
            i,
        )
        add_to(
            bar,
            slice(TABLE + at, TABLE + at + count),
            (both[0:count] + both[3 * count :] + rest[0:count])
            + (also[0:count] + also[count:] + more),
            i,
        )

    def back_to_states(at, count):
        near, far = slice(at, at + count), slice(TABLE + at, TABLE + at + count)
        v, vd = pre2[0, near, :], pre2[1, near, :]
        sig = sigmoid(v)
        slope = sig * (1.0 + v * (1.0 - sig))
        curve = sig * (1.0 - sig) * (2.0 + v * (1.0 - 2.0 * sig))
        both = mm3(split(jnp.concatenate([bar[near, :], bar[far, :]], 0)), w2[1], NT)
        first, second = both[0:count], both[count:]
        both = jnp.concatenate([first * slope, second * slope + first * curve * vd], 0)
        both = mm3(split(both), w2[0], NT)
        bar[near, :] = both[0:count]
        bar[far, :] = both[count:]

    for i in range(NR // 4 + 1):
        if i < NR // 4:
            scaled(i)
        if i > 0:
            turned_messages(i - 1, ROWS, GHOSTS)
    back_to_states(ROWS, GHOSTS)
    src3[:, 0:F] = bar[ROWS:TABLE, :]
    src3[:, F : 2 * F] = bar[TABLE + ROWS : 2 * TABLE, :]
    third = copies(src3, rnode, send3, recv3, -1, False)
    for copy in third:
        copy.start()

    for i in range(NR // 4):
        turned_messages(i, 0, ROWS)
    back_to_states(0, ROWS)

    m = split(mu[0])
    md = split(mu[1])
    high = jnp.concatenate([m[0], md[0]], 0)
    full = jnp.concatenate([high, m[1], md[1]], 0)
    ours = jnp.concatenate(m, 0)

    def pairs_two(i, carry):
        cols = pl.ds(pl.multiple_of(i * 3 * TILE, 3 * TILE), 3 * TILE)
        both = mm(full, p2_s[0, cols, :], NT)
        rest = mm(high, p2_s[1, cols, :], NT)
        also = mm(ours, p2d_s[0, cols, :], NT)
        more = mm(m[0], p2d_s[1, cols, :], NT)
        two[0:ROWS, cols] = both[0:ROWS] + both[2 * ROWS : 3 * ROWS] + rest[0:ROWS]
        two[ROWS : 2 * ROWS, cols] = (
            both[ROWS : 2 * ROWS] + both[3 * ROWS :] + rest[ROWS:]
        ) + (also[0:ROWS] + also[ROWS:] + more)
        return carry

    lax.fori_loop(0, TILES // 3, pairs_two, 0)

    for copy in third:
        copy.wait()
    rows_back = onehot[0, :, 0:GHOSTS].astype(bf16)
    hi, lo = split(rnode[...])
    returned = mm(rows_back, hi) + mm(rows_back, lo)
    nu = mu[0] + bar[0:ROWS, :] + returned[:, 0:F]
    nud = mu[1] + bar[TABLE : TABLE + ROWS, :] + returned[:, F : 2 * F]
    mu[0] = nu
    mu[1] = nud

    wlr = wlr_s[0], wlr_s[1]
    for j in range(3):
        nu, nud = mu[0], mu[1]
        l, r, ld, rd = part(j, 0), part(j, 1), part(3 + j, 0), part(3 + j, 1)
        lr[j * ROWS : (j + 1) * ROWS, 0:F] = nu * r
        lr[j * ROWS : (j + 1) * ROWS, F : 2 * F] = nu * l
        lr[(3 + j) * ROWS : (4 + j) * ROWS, 0:F] = nud * r + nu * rd
        lr[(3 + j) * ROWS : (4 + j) * ROWS, F : 2 * F] = nud * l + nu * ld
    hi, lo = split(mm3(split(lr[...]), wlr, NT))
    vbar[0 : 6 * ROWS, :] = hi
    vbar[6 * ROWS :, :] = lo
    for number in range(2):
        hi, lo = split(mu[number])
        nus[number * ROWS : (number + 1) * ROWS, :] = hi
        nus[(2 + number) * ROWS : (3 + number) * ROWS, :] = lo
    out = (out0, out1)

    def pairs_one(m, target):
        cols = pl.ds(pl.multiple_of(m * TILE, TILE), TILE)
        both = mm(nus[...], pfs_s[0, cols, :], NT)
        rest = mm(nus[0 : 2 * ROWS, :], pfs_s[1, cols, :], NT)
        target[0 : 2 * ROWS, :] = two[:, cols] + (both[0 : 2 * ROWS] + both[2 * ROWS :] + rest)
        both = mm(vbar[...], pfv_s[0, cols, :], NT)
        rest = mm(vbar[0 : 6 * ROWS, :], pfv_s[1, cols, :], NT)
        target[2 * ROWS :, :] = both[0 : 6 * ROWS] + both[6 * ROWS :] + rest

    upper = lax.broadcasted_iota(jnp.int32, (8, ROWS), 1) >= GHOSTS

    def sum_waves(m, source):
        side = jnp.where(m < PAIRS, 0, 1)
        base = jnp.where(m < PAIRS, 2 * m + 1, 4 * (m - PAIRS) + 1).astype(f32)
        jump = jnp.where(m < PAIRS, 1.0, 2.0)
        ghosts_on = jnp.where(m < PAIRS, 0.0, 1.0)
        a = [
            KAPPA * (base + half * jump + ghosts_on * jnp.where(upper, 1.0, 0.0))
            for half in range(2)
        ]
        aa = [x * x for x in a]
        for start in range(0, ROWS, 8):
            rows = slice(start, start + 8)
            u = [geo[side, U0 + j, rows, :] for j in range(3)]
            total = [sums[side, number, rows, :] for number in range(14)]
            for half in range(2):
                s = waves[0, 2 * m + half, rows, :]
                ac = waves[1, 2 * m + half, rows, :]
                ss = s * aa[half]
                cols = slice(half * ROWS, (half + 1) * ROWS)
                y = [source[start + k * ROWS : start + k * ROWS + 8, cols] for k in range(8)]
                along = y[0] + u[0] * y[2] + u[1] * y[3] + u[2] * y[4]
                along_d = y[1] + u[0] * y[5] + u[1] * y[6] + u[2] * y[7]
                for j in range(3):
                    total[j] += s * y[2 + j]
                    total[3 + j] += ac * y[2 + j]
                    total[6 + j] += s * y[5 + j]
                total[9] += s * y[0]
                total[10] += ac * y[0]
                total[11] += ss * along
                total[12] += s * y[1]
                total[13] += ac * along_d
            for number in range(14):
                sums[side, number, rows, :] = total[number]

    sums[...] = jnp.zeros(sums.shape, f32)
    pairs_one(PAIRS, out0)

    def two_sums(k, carry, first, second, base, last):
        for half in range(2):
            ahead, behind = (first, second) if half == 0 else (second, first)
            m = base + 2 * k + half
            pairs_one(jnp.minimum(m + 1, last), ahead)
            sum_waves(m, behind)
        return carry

    lax.fori_loop(
        0,
        (TILES - PAIRS) // 2,
        functools.partial(two_sums, first=out1, second=out0, base=PAIRS, last=TILES - 1),
        0,
    )
    pairs_one(0, out1)
    sum_waves(TILES - 1, out0)

    def offsets_back(i, carry, side):
        rows = pl.ds(pl.multiple_of(i * 8, 8), 8)
        e0, e1, e2, rate, inv = (geo[side, number, rows, :] for number in range(5))
        unit = [geo[side, U0 + j, rows, :] for j in range(3)]
        turn = [geo[side, W0 + j, rows, :] for j in range(3)]
        z = [sums[side, number, rows, :] for number in range(14)]
        db = e1 * z[9] + e0 * z[10]
        dbd = e2 * z[9] + 2.0 * e1 * z[10] - e0 * z[11]
        inner = z[12]
        w = jnp.zeros((8, ROWS), f32)
        wd = w
        spin = w
        ub, ubd = [], []
        for j in range(3):
            slope = e1 * z[j] + e0 * z[3 + j]
            ub.append(e0 * z[j])
            ubd.append(rate * slope + e0 * z[6 + j])
            db = db + unit[j] * slope
            dbd = dbd + unit[j] * (e2 * z[j] + 2.0 * e1 * z[3 + j])
            inner = inner + unit[j] * z[6 + j]
            spin = spin + turn[j] * slope
            w = w + unit[j] * ub[j]
            wd = wd + turn[j] * ub[j] + unit[j] * ubd[j]
        dbd = rate * dbd + e1 * inner + e0 * z[13] + spin
        for j in range(3):
            t = (ub[j] - unit[j] * w) * inv
            pg[side, j, rows, :] = db * unit[j] + t
            pg[side, 3 + j, rows, :] = (
                dbd * unit[j]
                + db * turn[j]
                + (ubd[j] - turn[j] * w - unit[j] * wd - t * rate) * inv
            )
        return carry

    lax.fori_loop(0, ROWS // 8, functools.partial(offsets_back, side=1), 0)
    gpos[...] = jnp.zeros((8, ROWS), f32)
    c8[...] = jnp.zeros((8, ROWS), f32)
    for j in range(6):
        ghosts = pg[1, j]
        gpos[j : j + 1, :] = jnp.sum(ghosts, axis=0, keepdims=True)
        c8[j : j + 1, :] = jnp.sum(ghosts.T, axis=0, keepdims=True)
    both = gpos[...]
    gpos[...] = both + pltpu.roll(both, GHOSTS, 1)
    last = copies(gpos, rpos, send4, recv4, -1, True)
    for copy in last:
        copy.start()

    lax.fori_loop(
        0,
        PAIRS // 2,
        functools.partial(two_sums, first=out0, second=out1, base=0, last=PAIRS - 1),
        0,
    )
    lax.fori_loop(0, ROWS // 8, functools.partial(offsets_back, side=0), 0)
    for j in range(6):
        own = pg[0, j]
        c8[j : j + 1, :] = jnp.sum(own - own.T, axis=0, keepdims=True) - c8[j : j + 1, :]
    for copy in last:
        copy.wait()
    hi, mid, lo = split3(merged(rpos))
    slots = onehot[1].astype(bf16)
    total = c8[...] + (mm(hi, slots) + (mm(mid, slots) + mm(lo, slots)))
    force[...] = -total[0:3, :]
    hess[...] = -total[3:6, :]


def per_device(nx, ny, *arrays):
    arrays = list(arrays)
    arrays[15] = arrays[15].reshape(1, F)
    vmem = pl.BlockSpec(memory_space=pltpu.VMEM)
    in_specs = [pl.BlockSpec(memory_space=pl.ANY)] * 16
    in_specs[3] = pl.BlockSpec(memory_space=pltpu.SMEM)

    def v32(*shape):
        return pltpu.VMEM(shape, f32)

    def v16(*shape):
        return pltpu.VMEM(shape, bf16)

    dma = pltpu.SemaphoreType.DMA((8,))
    scratch = [
        v32(3, ROWS),
        v32(3, ROWS),
        v32(ROWS, F),
        pltpu.VMEM(arrays[4].shape, jnp.int32),
        pltpu.VMEM((1, GHOSTS), jnp.int32),
        v32(NR, 2 * F),
        v32(NR, F),
        v32(1, F),
        v16(2, F, F),
        v16(2, F, 2 * F),
        v16(2, F, 2 * F),
        v16(2, F, F),
        v16(2, F, F),
        v16(2, F, F),
        pltpu.VMEM((8, ROWS), jnp.int32),
        v32(8, ROWS),
        v32(8, ROWS),
        v32(8, 8, ROWS),
        v32(GHOSTS, F),
        v32(GHOSTS, F),
        v32(GHOSTS, 2 * F),
        v32(GHOSTS, 2 * F),
        v32(GHOSTS, 2 * F),
        v32(GHOSTS, 2 * F),
        v32(8, ROWS),
        v32(8, 8, ROWS),
        v32(2, ROWS, ROWS),
        v32(2, ROWS, ROWS),
        v32(6, ROWS, ROWS),
        v32(2, 13, ROWS, ROWS),
        v32(2, NR + PAIRS, ROWS, ROWS),
        v16(4 * ROWS, WIDE),
        v16(12 * ROWS, TILE),
        v16(12 * ROWS, TILE),
        v16(4 * TABLE, NR * ROWS),
        v16(2, WIDE, F),
        v16(2, WIDE, F),
        v16(2, WIDE, F),
        v16(2, WIDE, F),
        v16(NR // 4, 4, 4 * ROWS, F),
        v32(TABLE, 2 * F),
        v32(2 * ROWS, F),
        v32(6 * ROWS, F),
        v32(6 * ROWS, 2 * F),
        v32(ROWS, 2 * F),
        v32(2, TABLE, F),
        v32(2, TABLE, F),
        v32(2, ROWS, F),
        v32(2 * TABLE, F),
        v32(8 * ROWS, TILE),
        v32(8 * ROWS, TILE),
        v32(3 * F, 3 * F),
        v32(2 * ROWS, WIDE),
        v32(2, 14, ROWS, ROWS),
        v16(12 * ROWS, F),
        v16(4 * ROWS, F),
        v32(2, 6, ROWS, ROWS),
    ] + [dma] * 10 + [pltpu.SemaphoreType.DMA((15,))]
    out = jax.ShapeDtypeStruct((3, ROWS), f32)
    return pl.pallas_call(
        functools.partial(kernel, nx, ny),
        out_shape=(out, out),
        in_specs=in_specs,
        out_specs=(vmem, vmem),
        scratch_shapes=scratch,
        compiler_params=pltpu.CompilerParams(
            collective_id=0, has_side_effects=True, vmem_limit_bytes=67043328
        ),
    )(*arrays)


def solution(mesh):
    placed = (
        P(None, ("bx", "by")),
        P(None, ("bx", "by")),
        P(("bx", "by"), None),
        P(("bx", "by")),
        P(None, ("bx", "by")),
        P(("bx", "by"), None),
    ) + (P(),) * 10
    return jax.shard_map(
        functools.partial(per_device, mesh.shape["bx"], mesh.shape["by"]),
        mesh=mesh,
        in_specs=placed,
        out_specs=(P(None, ("bx", "by")), P(None, ("bx", "by"))),
        check_vma=False,
    )
```

```python
import functools
import math

import jax
import jax.numpy as jnp
from jax import lax
from jax.experimental import pallas as pl
from jax.experimental.pallas import tpu as pltpu
from jax.sharding import PartitionSpec as P

MESH = pl.DeviceIdType.MESH
f32 = jnp.float32
bf16 = jnp.bfloat16
offsets = ((-1, -1), (-1, 0), (-1, 1), (0, -1), (0, 1), (1, -1), (1, 0), (1, 1))
NN = (((1,), (0,)), ((), ()))
NT = (((1,), (1,)), ((), ()))
KAPPA = math.pi / 3.0
SOFT = 0.01
ROWS = 128
GHOSTS = 64
TABLE = ROWS + GHOSTS
F = 256
NR = 20
PAIRS = NR // 2
TILE = 256
TILES = NR * TABLE // TILE
WIDE = TILES * TILE
STEP = 5 * TILE
STEPS = WIDE // STEP
OWN_STEPS = 2


def split(x):
    hi = x.astype(bf16)
    return hi, (x - hi.astype(f32)).astype(bf16)


def split3(x):
    hi = x.astype(bf16)
    rest = x - hi.astype(f32)
    mid = rest.astype(bf16)
    return hi, mid, (rest - mid.astype(f32)).astype(bf16)


def mm(a, b, dims=NN):
    return lax.dot_general(a, b, dims, preferred_element_type=f32)


def mm3(a, b, dims=NN):
    return mm(a[0], b[0], dims) + (mm(a[1], b[0], dims) + mm(a[0], b[1], dims))


def pick(refs, *index):
    return refs[0][index], refs[1][index]


def put(refs, value, *index):
    hi, lo = split(value)
    refs[0][index] = hi
    refs[1][index] = lo


def sin_cos(angle):
    turns = jnp.floor(angle * (0.5 / math.pi) + 0.5)
    half = 0.5 * ((angle - turns * 6.28125) - turns * (2.0 * math.pi - 6.28125))
    sq = half * half
    odd = 1.0 / 39916800.0
    for c in (1.0 / 362880.0, 1.0 / 5040.0, 1.0 / 120.0, 1.0 / 6.0, 1.0):
        odd = c - sq * odd
    sh = half * odd
    even = 1.0 / 479001600.0
    for c in (1.0 / 3628800.0, 1.0 / 40320.0, 1.0 / 720.0, 1.0 / 24.0, 0.5, 1.0):
        even = c - sq * even
    return 2.0 * sh * even, 1.0 - 2.0 * sh * sh


def sigmoid(v):
    return 1.0 / (1.0 + jnp.exp(-v))


def own_waves(s1, c1):
    twice = 2.0 * c1
    before_s, before_c = jnp.zeros_like(s1), jnp.ones_like(c1)
    s, c = s1, c1
    for q in range(NR):
        yield (q + 1) * KAPPA, s, c
        if q < NR - 1:
            s, before_s = twice * s - before_s, s
            c, before_c = twice * c - before_c, c


def ghost_waves(s1, c1):
    upper = lax.broadcasted_iota(jnp.int32, s1.shape, 1) >= GHOSTS
    s2, c2 = 2.0 * s1 * c1, 1.0 - 2.0 * s1 * s1
    twice = 2.0 * c2
    s, before_s = jnp.where(upper, s2, s1), jnp.where(upper, 0.0, -s1)
    c, before_c = jnp.where(upper, c2, c1), jnp.where(upper, 1.0, c1)
    shift = jnp.where(upper, 2.0 * KAPPA, KAPPA)
    for p in range(PAIRS):
        yield shift + 2.0 * p * KAPPA, s, c
        if p < PAIRS - 1:
            s, before_s = twice * s - before_s, s
            c, before_c = twice * c - before_c, c


E0, E1, E2, DD, IV, S1, C1, U0, W0 = 0, 1, 2, 3, 4, 5, 6, 7, 10
WAVES = (own_waves, ghost_waves)


def kernel(
    nx,
    ny,
    pos_in,
    tan_in,
    emb_in,
    cnt,
    nbr_in,
    snd_in,
    w1i,
    w1o,
    f1_in,
    wl,
    wr,
    w2i,
    w2o,
    f2_in,
    wh,
    we_in,
    force,
    hess,
    pos,
    tan,
    emb,
    nbr,
    snd,
    f1,
    f2,
    we,
    w1i_s,
    w1o_s,
    wlr_s,
    w2i_s,
    w2o_s,
    wh_s,
    sndpad,
    c8,
    csel,
    crecv,
    sel1,
    gemb,
    sel2,
    gnode,
    src3,
    rnode,
    gpos,
    rpos,
    onehot,
    mask,
    colb,
    geo,
    waves,
    lb,
    lv0,
    lv1,
    lt,
    pfs_s,
    pfv_s,
    p2_s,
    p2d_s,
    muf,
    phi,
    acc,
    accv,
    lr,
    node,
    pre2,
    phi2,
    mu,
    bar,
    out0,
    out1,
    landing,
    two,
    sums,
    vbar,
    nus,
    pg,
    send1,
    recv1,
    sendc,
    recvc,
    send2,
    recv2,
    send3,
    recv3,
    send4,
    recv4,
    loads,
):
    ix, iy = lax.axis_index("bx"), lax.axis_index("by")

    def device(g, sign):
        dx, dy = offsets[g]
        return (lax.rem(ix + sign * dx + nx, nx), lax.rem(iy + sign * dy + ny, ny))

    barrier = pltpu.get_barrier_semaphore()
    for g in range(8):
        pl.semaphore_signal(barrier, inc=1, device_id=device(g, 1), device_id_type=MESH)

    def block(ref, g):
        return ref.at[pl.ds(g * 8, 8), :]

    def copies(source, target, sends, recvs, sign, whole):
        return [
            pltpu.make_async_remote_copy(
                src_ref=source if whole else block(source, g),
                dst_ref=target.at[g] if whole else block(target, g),
                send_sem=sends.at[g],
                recv_sem=recvs.at[g],
                device_id=device(g, sign),
                device_id_type=MESH,
            )
            for g in range(8)
        ]

    def select(x):
        hi, lo = split(x)
        rows = onehot[1, 0:GHOSTS, :].astype(bf16)
        return mm(rows, hi) + mm(rows, lo)

    lane = lax.broadcasted_iota(jnp.int32, (8, ROWS), 1)
    group = lax.div(lane, 8)

    def merged(ref):
        total = jnp.where(group == 0, ref[0], 0.0)
        for g in range(1, 8):
            total = total + jnp.where(group == g, ref[g], 0.0)
        return total

    weights = []
    spots = ((0, 0), (0, F), (1, 0), (1, F), (1, 2 * F), (2, 0), (2, F))
    for number, (w, (down, at)) in enumerate(zip((w1i, w1o, wl, wr, w2i, w2o, wh), spots)):
        place = landing.at[down * F : (down + 1) * F, at : at + w.shape[1]]
        weights.append((pltpu.make_async_copy(w, place, loads.at[number]), place))
    small = {}
    named = ((snd_in, snd), (pos_in, pos), (tan_in, tan), (emb_in, emb), (nbr_in, nbr))
    named += ((f1_in, f1), (f2_in, f2), (we_in, we))
    for number, (source, place) in enumerate(named):
        small[number] = pltpu.make_async_copy(source, place, loads.at[7 + number])
        small[number].start()
    for copy, _ in weights:
        copy.start()
    for number in range(4):
        small[number].wait()

    sndpad[...] = jnp.full((8, ROWS), -1, jnp.int32)
    sndpad[0:1, 0:GHOSTS] = snd[...]
    hot = jnp.where(
        lax.broadcasted_iota(jnp.int32, (ROWS, ROWS), 0) == sndpad[0:1, :], 1.0, 0.0
    )
    onehot[0] = hot
    onehot[1] = hot.T
    c8[...] = jnp.zeros((8, ROWS), f32)
    c8[0:3, :] = pos[...]
    c8[3:6, :] = tan[...]
    hi, mid, lo = split3(c8[...])
    hot16 = hot.astype(bf16)
    csel[...] = mm(hi, hot16) + (mm(mid, hot16) + mm(lo, hot16))
    sel1[...] = select(emb[...])
    stores = ((w1i_s, 0), (w1o_s, 0), (wlr_s, 0), (wlr_s, F), (w2i_s, 0), (w2o_s, 0), (wh_s, 0))
    for (refs, at), (copy, place) in zip(stores, weights):
        copy.wait()
        hi, lo = split(place[...])
        refs[0, :, at : at + hi.shape[1]] = hi
        refs[1, :, at : at + hi.shape[1]] = lo

    small[4].wait()
    row = lax.broadcasted_iota(jnp.int32, (ROWS, ROWS), 0)
    ghost = lax.rem(row, GHOSTS)
    for side, slots in ((0, row), (1, ROWS + (7 - lax.div(ghost, 8)) * 8 + lax.rem(ghost, 8))):

        def mark(k, total, slots=slots):
            return jnp.where(slots == nbr[pl.ds(k, 1), :], 1.0, total)

        listed = lax.fori_loop(0, nbr.shape[0], mark, jnp.zeros((ROWS, ROWS), f32))
        mask[side] = listed.T

    for number in (5, 6, 7):
        small[number].wait()

    def project(rows, first_w, second_w):
        v = mm3(split(rows), first_w)
        return mm3(split(v * sigmoid(v)), second_w)

    w1 = (w1i_s[0], w1i_s[1]), (w1o_s[0], w1o_s[1])
    phi[0:ROWS, :] = project(emb[...], *w1)
    for j in range(6):
        colb[j] = jnp.broadcast_to(c8[j : j + 1, :], (ROWS, ROWS)).T

    def put2(refs, value, start):
        hi, lo = split(value)
        refs[0, pl.ds(start, value.shape[0]), :] = hi
        refs[1, pl.ds(start, value.shape[0]), :] = lo

    def spread_own(refs, table, filters, at):
        def body(q, carry):
            weights = filters[pl.ds(q, 1), at : at + F]
            put2(refs, table() * weights, pl.multiple_of(q * ROWS, ROWS))
            return carry

        lax.fori_loop(0, NR, body, 0)

    def spread_ghosts(refs, table, filters, at):
        def body(q, carry):
            weights = filters[pl.ds(q, 1), at : at + F]
            put2(refs, table() * weights, pl.multiple_of(NR * ROWS + q * GHOSTS, GHOSTS))
            return carry

        lax.fori_loop(0, NR, body, 0)

    def put_rows(ref, value, first, second, cols):
        hi, lo = split(value)
        ref[first : first + 16, cols] = hi
        ref[second : second + 16, cols] = lo

    spread_own(pfs_s, lambda: phi[0:ROWS, 0:F], f1, 0)
    spread_own(pfv_s, lambda: phi[0:ROWS, F : 2 * F], f1, F)

    scale = 1.0 / math.sqrt(nbr.shape[0])

    def geometry(i, carry, side, table):
        rows = pl.ds(pl.multiple_of(i * 8, 8), 8)
        centre = [colb[j, rows, :] for j in range(6)]
        off = [table[j : j + 1, :] - centre[j] for j in range(3)]
        vel = [table[j : j + 1, :] - centre[j] for j in range(3, 6)]
        listed = mask[side, rows, :]
        sq = off[0] * off[0] + off[1] * off[1] + off[2] * off[2]
        sq = jnp.where(listed > 0.0, sq, 1.0) + SOFT
        inv = lax.rsqrt(sq)
        inv = inv * (1.5 - 0.5 * sq * inv * inv)
        dist = sq * inv
        unit = [x * inv for x in off]
        rate = unit[0] * vel[0] + unit[1] * vel[1] + unit[2] * vel[2]
        s1, c1 = sin_cos(KAPPA * dist)
        weight = scale * listed
        env = 0.5 * (c1 + 1.0)
        env1 = (-0.5 * KAPPA) * s1
        env2 = (-0.5 * KAPPA * KAPPA) * c1
        e0 = weight * env * inv
        slope = env1 - env * inv
        e1 = weight * inv * slope
        e2 = weight * inv * (env2 - 2.0 * inv * slope)
        planes = [e0, e1, e2, rate, inv, s1, c1] + unit
        planes += [(vel[j] - unit[j] * rate) * inv for j in range(3)]
        for number, value in enumerate(planes):
            geo[side, number, rows, :] = value
        for number, (a, s, c) in enumerate(WAVES[side](s1, c1)):
            waves[0, side * NR + number, rows, :] = s
            waves[1, side * NR + number, rows, :] = a * c
        return carry

    lv = (lv0, lv1)

    def build_pairs(m, target):
        side = jnp.where(m < PAIRS, 0, 1)
        cols = pl.ds(pl.multiple_of(m * TILE, TILE), TILE)
        for start in range(0, ROWS, 16):
            rows = slice(start, start + 16)

            def twice(x):
                return jnp.concatenate([x, x], 1)

            e0, e1, rate = (geo[side, number, rows, :] for number in (E0, E1, DD))
            e1d, e0d = twice(e1 * rate), twice(e0 * rate)
            s = jnp.concatenate([waves[0, 2 * m + half, rows, :] for half in range(2)], 1)
            ac = jnp.concatenate([waves[1, 2 * m + half, rows, :] for half in range(2)], 1)
            b = twice(e0) * s
            bd = e1d * s + e0d * ac
            put_rows(lb, bd, start, start + 3 * ROWS, cols)
            put_rows(lb, b, start + ROWS, start + 2 * ROWS, cols)
            for j in range(3):
                u, w = twice(geo[side, U0 + j, rows, :]), twice(geo[side, W0 + j, rows, :])
                first = start + j * ROWS
                put_rows(target, b * u, first, first + 6 * ROWS, slice(None))
                first += 3 * ROWS
                put_rows(target, bd * u + b * w, first, first + 6 * ROWS, slice(None))

    def add_to(ref, rows, value, i):
        if i == 0:
            ref[rows, :] = value
        else:
            ref[rows, :] += value

    def gather_scalar(refs, cols):
        both = mm(lb[:, cols], refs[0, cols, :])
        rest = mm(lb[0 : 2 * ROWS, cols], refs[1, cols, :])
        acc[0:ROWS, :] += both[ROWS : 2 * ROWS] + both[2 * ROWS : 3 * ROWS] + rest[ROWS:]
        acc[ROWS : 2 * ROWS, :] += both[0:ROWS] + both[3 * ROWS :] + rest[0:ROWS]

    def gather_vector(m, near):
        cols = pl.ds(pl.multiple_of(m * TILE, TILE), TILE)
        both = mm(near[...], pfv_s[0, cols, :])
        rest = mm(near[0 : 6 * ROWS, :], pfv_s[1, cols, :])
        accv[...] += both[0 : 6 * ROWS] + both[6 * ROWS :] + rest

    lax.fori_loop(0, ROWS // 8, functools.partial(geometry, side=0, table=c8[...]), 0)
    build_pairs(0, lv0)
    pl.semaphore_wait(barrier, 8)
    coords = copies(csel, crecv, sendc, recvc, 1, True)
    first = copies(sel1, gemb, send1, recv1, 1, False)
    for copy in coords + first:
        copy.start()

    acc[...] = jnp.zeros((2 * ROWS, F), f32)
    accv[...] = jnp.zeros((6 * ROWS, F), f32)

    def two_tiles(k, carry, base, last):
        for half in range(2):
            m = base + 2 * k + half
            gather_vector(m, lv[half])
            build_pairs(jnp.minimum(m + 1, last), lv[1 - half])
        return carry

    lax.fori_loop(0, PAIRS // 2, functools.partial(two_tiles, base=0, last=PAIRS - 1), 0)

    for copy in coords + first:
        copy.wait()
    phi[ROWS:TABLE, :] = project(gemb[...], *w1)
    found = merged(crecv)
    twofold = found + pltpu.roll(found, GHOSTS, 1)
    lax.fori_loop(0, ROWS // 8, functools.partial(geometry, side=1, table=twofold), 0)
    build_pairs(PAIRS, lv0)

    spread_ghosts(pfs_s, lambda: phi[ROWS:TABLE, 0:F], f1, 0)
    spread_ghosts(pfv_s, lambda: phi[ROWS:TABLE, F : 2 * F], f1, F)
    lax.fori_loop(
        0, (TILES - PAIRS) // 2, functools.partial(two_tiles, base=PAIRS, last=TILES - 1), 0
    )
    gather_vector(TILES - 1, lv0)


    def scalar_step(i, carry):
        gather_scalar(pfs_s, pl.ds(pl.multiple_of(i * STEP, STEP), STEP))
        return carry

    lax.fori_loop(0, STEPS, scalar_step, 0)
    lr[...] = mm3(split(accv[...]), (wlr_s[0], wlr_s[1]))

    def part(j, side):
        return lr[j * ROWS : (j + 1) * ROWS, side * F : (side + 1) * F]

    state = emb[...] + acc[0:ROWS, :]
    moved = acc[ROWS : 2 * ROWS, :]
    for j in range(3):
        state = state + part(j, 0) * part(j, 1)
        moved = moved + (part(3 + j, 0) * part(j, 1) + part(j, 0) * part(3 + j, 1))
    node[:, 0:F] = state
    node[:, F : 2 * F] = moved
    sel2[...] = select(node[...])
    second = copies(sel2, gnode, send2, recv2, 1, False)
    for copy in second:
        copy.start()

    w2 = (w2i_s[0], w2i_s[1]), (w2o_s[0], w2o_s[1])

    def table_two(values, moves, at, n):
        v = mm3(split(values), w2[0])
        vd = mm3(split(moves), w2[0])
        sig = sigmoid(v)
        pre2[0, at : at + n, :] = v
        pre2[1, at : at + n, :] = vd
        slope = sig * (1.0 + v * (1.0 - sig))
        phi2[0, at : at + n, :] = mm3(split(v * sig), w2[1])
        phi2[1, at : at + n, :] = mm3(split(slope * vd), w2[1])

    table_two(node[:, 0:F], node[:, F : 2 * F], 0, ROWS)

    for side in range(2):
        rows = ROWS if side == 0 else GHOSTS
        e0, e1, rate = (geo[side, number] for number in (E0, E1, DD))
        pg[side, 0] = e0.T
        pg[side, 1] = (e1 * rate).T
        pg[side, 2] = (e0 * rate).T
        pg[side, 3] = geo[side, S1].T
        pg[side, 4] = geo[side, C1].T

    def turned(side, count):
        def body(i, carry):
            start = pl.multiple_of(i * 16, 16)
            g = [pg[side, number, pl.ds(start, 16), :] for number in range(5)]
            held = None
            for q, (a, s, c) in enumerate(own_waves(g[3], g[4])):
                new = (g[0] * s, g[1] * s + g[2] * (a * c))
                if q % 2 == 0:
                    held = new
                    continue
                cols = slice((q - 1) * ROWS, (q + 1) * ROWS)
                for value, first, second in ((1, 0, 3), (0, 1, 2)):
                    hi, lo = split(jnp.concatenate([held[value], new[value]], 1))
                    at = 4 * side * ROWS
                    lt[pl.ds(start + at + first * count, 16), cols] = hi
                    lt[pl.ds(start + at + second * count, 16), cols] = lo
            return carry

        lax.fori_loop(0, count // 16, body, 0)

    turned(0, ROWS)
    turned(1, GHOSTS)

    spread_own(p2_s, lambda: phi2[0, 0:ROWS, :], f2, 0)
    spread_own(p2d_s, lambda: phi2[1, 0:ROWS, :], f2, 0)
    acc[...] = jnp.zeros((2 * ROWS, F), f32)

    def messages_two(i, carry):
        cols = pl.ds(pl.multiple_of(i * STEP, STEP), STEP)
        gather_scalar(p2_s, cols)
        both = mm(lb[ROWS : 3 * ROWS, cols], p2d_s[0, cols, :])
        rest = mm(lb[ROWS : 2 * ROWS, cols], p2d_s[1, cols, :])
        acc[ROWS : 2 * ROWS, :] += both[0:ROWS] + both[ROWS:] + rest
        return carry

    lax.fori_loop(0, OWN_STEPS, messages_two, 0)

    for copy in second:
        copy.wait()
    table_two(gnode[:, 0:F], gnode[:, F : 2 * F], ROWS, GHOSTS)
    spread_ghosts(p2_s, lambda: phi2[0, ROWS:TABLE, :], f2, 0)
    spread_ghosts(p2d_s, lambda: phi2[1, ROWS:TABLE, :], f2, 0)
    messages_two(OWN_STEPS, 0)
    st = node[:, 0:F] + acc[0:ROWS, :]
    std = node[:, F : 2 * F] + acc[ROWS : 2 * ROWS, :]

    whs = wh_s[0], wh_s[1]
    v = mm3(split(st), whs)
    vd = mm3(split(std), whs)
    sig = sigmoid(v)
    live = lax.broadcasted_iota(jnp.int32, (ROWS, F), 0) < cnt[0]
    top = jnp.where(live, jnp.broadcast_to(we[...], (ROWS, F)), 0.0)
    mu[0] = mm3(split(top * (sig * (1.0 + v * (1.0 - sig)))), whs, NT)
    mu[1] = mm3(
        split(top * (sig * (1.0 - sig) * (2.0 + v * (1.0 - 2.0 * sig))) * vd), whs, NT
    )

    def scaled(i):
        for q in range(4 * i, 4 * i + 4):
            weights = f2[q : q + 1, :]
            rows = slice(q % 4 * ROWS, (q % 4 + 1) * ROWS)
            for number in range(2):
                hi, lo = split(mu[number] * weights)
                muf[i, 2 * number, rows, :] = hi
                muf[i, 2 * number + 1, rows, :] = lo

    def turned_messages(i, at, count):
        cols = slice(i * 4 * ROWS, (i + 1) * 4 * ROWS)
        top = 4 * at
        both = mm(lt[top : top + 4 * count, cols], muf[i, 0])
        rest = mm(lt[top : top + 2 * count, cols], muf[i, 1])
        also = mm(lt[top + count : top + 3 * count, cols], muf[i, 2])
        more = mm(lt[top + count : top + 2 * count, cols], muf[i, 3])
        add_to(
            bar,
            slice(at, at + count),
            both[count : 2 * count] + both[2 * count : 3 * count] + rest[count:],
            i,
        )
        add_to(
            bar,
            slice(TABLE + at, TABLE + at + count),
            (both[0:count] + both[3 * count :] + rest[0:count])
            + (also[0:count] + also[count:] + more),
            i,
        )

    def back_to_states(at, count):
        near, far = slice(at, at + count), slice(TABLE + at, TABLE + at + count)
        v, vd = pre2[0, near, :], pre2[1, near, :]
        sig = sigmoid(v)
        slope = sig * (1.0 + v * (1.0 - sig))
        curve = sig * (1.0 - sig) * (2.0 + v * (1.0 - 2.0 * sig))
        both = mm3(split(jnp.concatenate([bar[near, :], bar[far, :]], 0)), w2[1], NT)
        first, second = both[0:count], both[count:]
        both = jnp.concatenate([first * slope, second * slope + first * curve * vd], 0)
        both = mm3(split(both), w2[0], NT)
        bar[near, :] = both[0:count]
        bar[far, :] = both[count:]

    for i in range(NR // 4 + 1):
        if i < NR // 4:
            scaled(i)
        if i > 0:
            turned_messages(i - 1, ROWS, GHOSTS)
    back_to_states(ROWS, GHOSTS)
    src3[:, 0:F] = bar[ROWS:TABLE, :]
    src3[:, F : 2 * F] = bar[TABLE + ROWS : 2 * TABLE, :]
    third = copies(src3, rnode, send3, recv3, -1, False)
    for copy in third:
        copy.start()

    for i in range(NR // 4):
        turned_messages(i, 0, ROWS)
    back_to_states(0, ROWS)

    m = split(mu[0])
    md = split(mu[1])
    high = jnp.concatenate([m[0], md[0]], 0)
    full = jnp.concatenate([high, m[1], md[1]], 0)
    ours = jnp.concatenate(m, 0)

    def pairs_two(i, carry):
        cols = pl.ds(pl.multiple_of(i * 3 * TILE, 3 * TILE), 3 * TILE)
        both = mm(full, p2_s[0, cols, :], NT)
        rest = mm(high, p2_s[1, cols, :], NT)
        also = mm(ours, p2d_s[0, cols, :], NT)
        more = mm(m[0], p2d_s[1, cols, :], NT)
        two[0:ROWS, cols] = both[0:ROWS] + both[2 * ROWS : 3 * ROWS] + rest[0:ROWS]
        two[ROWS : 2 * ROWS, cols] = (
            both[ROWS : 2 * ROWS] + both[3 * ROWS :] + rest[ROWS:]
        ) + (also[0:ROWS] + also[ROWS:] + more)
        return carry

    lax.fori_loop(0, TILES // 3, pairs_two, 0)

    for copy in third:
        copy.wait()
    rows_back = onehot[0, :, 0:GHOSTS].astype(bf16)
    hi, lo = split(rnode[...])
    returned = mm(rows_back, hi) + mm(rows_back, lo)
    nu = mu[0] + bar[0:ROWS, :] + returned[:, 0:F]
    nud = mu[1] + bar[TABLE : TABLE + ROWS, :] + returned[:, F : 2 * F]
    mu[0] = nu
    mu[1] = nud

    wlr = wlr_s[0], wlr_s[1]
    for j in range(3):
        nu, nud = mu[0], mu[1]
        l, r, ld, rd = part(j, 0), part(j, 1), part(3 + j, 0), part(3 + j, 1)
        lr[j * ROWS : (j + 1) * ROWS, 0:F] = nu * r
        lr[j * ROWS : (j + 1) * ROWS, F : 2 * F] = nu * l
        lr[(3 + j) * ROWS : (4 + j) * ROWS, 0:F] = nud * r + nu * rd
        lr[(3 + j) * ROWS : (4 + j) * ROWS, F : 2 * F] = nud * l + nu * ld
    hi, lo = split(mm3(split(lr[...]), wlr, NT))
    vbar[0 : 6 * ROWS, :] = hi
    vbar[6 * ROWS :, :] = lo
    for number in range(2):
        hi, lo = split(mu[number])
        nus[number * ROWS : (number + 1) * ROWS, :] = hi
        nus[(2 + number) * ROWS : (3 + number) * ROWS, :] = lo
    out = (out0, out1)

    def pairs_one(m, target, count):
        width = count * TILE
        cols = pl.ds(pl.multiple_of(m * TILE, TILE), width)
        both = mm(nus[...], pfs_s[0, cols, :], NT)
        rest = mm(nus[0 : 2 * ROWS, :], pfs_s[1, cols, :], NT)
        target[0 : 2 * ROWS, 0:width] = two[:, cols] + (
            both[0 : 2 * ROWS] + both[2 * ROWS :] + rest
        )
        both = mm(vbar[...], pfv_s[0, cols, :], NT)
        rest = mm(vbar[0 : 6 * ROWS, :], pfv_s[1, cols, :], NT)
        target[2 * ROWS :, 0:width] = both[0 : 6 * ROWS] + both[6 * ROWS :] + rest

    upper = lax.broadcasted_iota(jnp.int32, (8, ROWS), 1) >= GHOSTS

    def sum_waves(m, source, place):
        m = jnp.int32(m)
        side = jnp.where(m < PAIRS, 0, 1)
        base = jnp.where(m < PAIRS, 2 * m + 1, 4 * (m - PAIRS) + 1).astype(f32)
        jump = jnp.where(m < PAIRS, 1.0, 2.0)
        ghosts_on = jnp.where(m < PAIRS, 0.0, 1.0)
        a = [
            KAPPA * (base + half * jump + ghosts_on * jnp.where(upper, 1.0, 0.0))
            for half in range(2)
        ]
        aa = [x * x for x in a]
        for start in range(0, ROWS, 8):
            rows = slice(start, start + 8)
            u = [geo[side, U0 + j, rows, :] for j in range(3)]
            total = [sums[side, number, rows, :] for number in range(14)]
            for half in range(2):
                s = waves[0, 2 * m + half, rows, :]
                ac = waves[1, 2 * m + half, rows, :]
                ss = s * aa[half]
                cols = slice(place * TILE + half * ROWS, place * TILE + (half + 1) * ROWS)
                y = [source[start + k * ROWS : start + k * ROWS + 8, cols] for k in range(8)]
                along = y[0] + u[0] * y[2] + u[1] * y[3] + u[2] * y[4]
                along_d = y[1] + u[0] * y[5] + u[1] * y[6] + u[2] * y[7]
                for j in range(3):
                    total[j] += s * y[2 + j]
                    total[3 + j] += ac * y[2 + j]
                    total[6 + j] += s * y[5 + j]
                total[9] += s * y[0]
                total[10] += ac * y[0]
                total[11] += ss * along
                total[12] += s * y[1]
                total[13] += ac * along_d
            for number in range(14):
                sums[side, number, rows, :] = total[number]

    sums[...] = jnp.zeros(sums.shape, f32)
    def sum_both(m, source):
        sum_waves(m, source, 0)
        sum_waves(m + 1, source, 1)

    pairs_one(PAIRS, out0, 2)
    pairs_one(PAIRS + 2, out1, 2)
    sum_both(PAIRS, out0)
    pairs_one(PAIRS + 4, out0, 1)
    sum_both(PAIRS + 2, out1)
    pairs_one(0, out1, 2)
    sum_waves(PAIRS + 4, out0, 0)

    def offsets_back(i, carry, side):
        rows = pl.ds(pl.multiple_of(i * 8, 8), 8)
        e0, e1, e2, rate, inv = (geo[side, number, rows, :] for number in range(5))
        unit = [geo[side, U0 + j, rows, :] for j in range(3)]
        turn = [geo[side, W0 + j, rows, :] for j in range(3)]
        z = [sums[side, number, rows, :] for number in range(14)]
        db = e1 * z[9] + e0 * z[10]
        dbd = e2 * z[9] + 2.0 * e1 * z[10] - e0 * z[11]
        inner = z[12]
        w = jnp.zeros((8, ROWS), f32)
        wd = w
        spin = w
        ub, ubd = [], []
        for j in range(3):
            slope = e1 * z[j] + e0 * z[3 + j]
            ub.append(e0 * z[j])
            ubd.append(rate * slope + e0 * z[6 + j])
            db = db + unit[j] * slope
            dbd = dbd + unit[j] * (e2 * z[j] + 2.0 * e1 * z[3 + j])
            inner = inner + unit[j] * z[6 + j]
            spin = spin + turn[j] * slope
            w = w + unit[j] * ub[j]
            wd = wd + turn[j] * ub[j] + unit[j] * ubd[j]
        dbd = rate * dbd + e1 * inner + e0 * z[13] + spin
        for j in range(3):
            t = (ub[j] - unit[j] * w) * inv
            pg[side, j, rows, :] = db * unit[j] + t
            pg[side, 3 + j, rows, :] = (
                dbd * unit[j]
                + db * turn[j]
                + (ubd[j] - turn[j] * w - unit[j] * wd - t * rate) * inv
            )
        return carry

    lax.fori_loop(0, ROWS // 8, functools.partial(offsets_back, side=1), 0)
    gpos[...] = jnp.zeros((8, ROWS), f32)
    c8[...] = jnp.zeros((8, ROWS), f32)
    for j in range(6):
        ghosts = pg[1, j]
        gpos[j : j + 1, :] = jnp.sum(ghosts, axis=0, keepdims=True)
        c8[j : j + 1, :] = jnp.sum(ghosts.T, axis=0, keepdims=True)
    both = gpos[...]
    gpos[...] = both + pltpu.roll(both, GHOSTS, 1)
    last = copies(gpos, rpos, send4, recv4, -1, True)
    for copy in last:
        copy.start()

    def two_sums(k, carry):
        pairs_one(4 * k + 2, out0, 2)
        sum_both(4 * k, out1)
        pairs_one(4 * k + 4, out1, 2)
        sum_both(4 * k + 2, out0)
        return carry

    lax.fori_loop(0, 2, two_sums, 0)
    sum_both(8, out1)
    lax.fori_loop(0, ROWS // 8, functools.partial(offsets_back, side=0), 0)
    for j in range(6):
        own = pg[0, j]
        c8[j : j + 1, :] = jnp.sum(own - own.T, axis=0, keepdims=True) - c8[j : j + 1, :]
    for copy in last:
        copy.wait()
    hi, mid, lo = split3(merged(rpos))
    slots = onehot[1].astype(bf16)
    total = c8[...] + (mm(hi, slots) + (mm(mid, slots) + mm(lo, slots)))
    force[...] = -total[0:3, :]
    hess[...] = -total[3:6, :]


def per_device(nx, ny, *arrays):
    arrays = list(arrays)
    arrays[15] = arrays[15].reshape(1, F)
    vmem = pl.BlockSpec(memory_space=pltpu.VMEM)
    in_specs = [pl.BlockSpec(memory_space=pl.ANY)] * 16
    in_specs[3] = pl.BlockSpec(memory_space=pltpu.SMEM)

    def v32(*shape):
        return pltpu.VMEM(shape, f32)

    def v16(*shape):
        return pltpu.VMEM(shape, bf16)

    dma = pltpu.SemaphoreType.DMA((8,))
    scratch = [
        v32(3, ROWS),
        v32(3, ROWS),
        v32(ROWS, F),
        pltpu.VMEM(arrays[4].shape, jnp.int32),
        pltpu.VMEM((1, GHOSTS), jnp.int32),
        v32(NR, 2 * F),
        v32(NR, F),
        v32(1, F),
        v16(2, F, F),
        v16(2, F, 2 * F),
        v16(2, F, 2 * F),
        v16(2, F, F),
        v16(2, F, F),
        v16(2, F, F),
        pltpu.VMEM((8, ROWS), jnp.int32),
        v32(8, ROWS),
        v32(8, ROWS),
        v32(8, 8, ROWS),
        v32(GHOSTS, F),
        v32(GHOSTS, F),
        v32(GHOSTS, 2 * F),
        v32(GHOSTS, 2 * F),
        v32(GHOSTS, 2 * F),
        v32(GHOSTS, 2 * F),
        v32(8, ROWS),
        v32(8, 8, ROWS),
        v32(2, ROWS, ROWS),
        v32(2, ROWS, ROWS),
        v32(6, ROWS, ROWS),
        v32(2, 13, ROWS, ROWS),
        v32(2, NR + PAIRS, ROWS, ROWS),
        v16(4 * ROWS, WIDE),
        v16(12 * ROWS, TILE),
        v16(12 * ROWS, TILE),
        v16(4 * TABLE, NR * ROWS),
        v16(2, WIDE, F),
        v16(2, WIDE, F),
        v16(2, WIDE, F),
        v16(2, WIDE, F),
        v16(NR // 4, 4, 4 * ROWS, F),
        v32(TABLE, 2 * F),
        v32(2 * ROWS, F),
        v32(6 * ROWS, F),
        v32(6 * ROWS, 2 * F),
        v32(ROWS, 2 * F),
        v32(2, TABLE, F),
        v32(2, TABLE, F),
        v32(2, ROWS, F),
        v32(2 * TABLE, F),
        v32(8 * ROWS, 2 * TILE),
        v32(8 * ROWS, 2 * TILE),
        v32(3 * F, 3 * F),
        v32(2 * ROWS, WIDE),
        v32(2, 14, ROWS, ROWS),
        v16(12 * ROWS, F),
        v16(4 * ROWS, F),
        v32(2, 6, ROWS, ROWS),
    ] + [dma] * 10 + [pltpu.SemaphoreType.DMA((15,))]
    out = jax.ShapeDtypeStruct((3, ROWS), f32)
    return pl.pallas_call(
        functools.partial(kernel, nx, ny),
        out_shape=(out, out),
        in_specs=in_specs,
        out_specs=(vmem, vmem),
        scratch_shapes=scratch,
        compiler_params=pltpu.CompilerParams(
            collective_id=0, has_side_effects=True, vmem_limit_bytes=67043328
        ),
    )(*arrays)


def solution(mesh):
    placed = (
        P(None, ("bx", "by")),
        P(None, ("bx", "by")),
        P(("bx", "by"), None),
        P(("bx", "by")),
        P(None, ("bx", "by")),
        P(("bx", "by"), None),
    ) + (P(),) * 10
    return jax.shard_map(
        functools.partial(per_device, mesh.shape["bx"], mesh.shape["by"]),
        mesh=mesh,
        in_specs=placed,
        out_specs=(P(None, ("bx", "by")), P(None, ("bx", "by"))),
        check_vma=False,
    )
```

```python
import functools
import math

import jax
import jax.numpy as jnp
from jax import lax
from jax.experimental import pallas as pl
from jax.experimental.pallas import tpu as pltpu
from jax.sharding import PartitionSpec as P

MESH = pl.DeviceIdType.MESH
f32 = jnp.float32
bf16 = jnp.bfloat16
offsets = ((-1, -1), (-1, 0), (-1, 1), (0, -1), (0, 1), (1, -1), (1, 0), (1, 1))
NN = (((1,), (0,)), ((), ()))
NT = (((1,), (1,)), ((), ()))
KAPPA = math.pi / 3.0
SOFT = 0.01
ROWS = 128
GHOSTS = 64
TABLE = ROWS + GHOSTS
F = 256
NR = 20
PAIRS = NR // 2
TILE = 256
TILES = NR * TABLE // TILE
WIDE = TILES * TILE
STEP = 5 * TILE
STEPS = WIDE // STEP
OWN_STEPS = 2


def split(x):
    hi = x.astype(bf16)
    return hi, (x - hi.astype(f32)).astype(bf16)


def split3(x):
    hi = x.astype(bf16)
    rest = x - hi.astype(f32)
    mid = rest.astype(bf16)
    return hi, mid, (rest - mid.astype(f32)).astype(bf16)


def mm(a, b, dims=NN):
    return lax.dot_general(a, b, dims, preferred_element_type=f32)


def mm3(a, b, dims=NN):
    return mm(a[0], b[0], dims) + (mm(a[1], b[0], dims) + mm(a[0], b[1], dims))


def pick(refs, *index):
    return refs[0][index], refs[1][index]


def put(refs, value, *index):
    hi, lo = split(value)
    refs[0][index] = hi
    refs[1][index] = lo


def sin_cos(angle):
    turns = jnp.floor(angle * (0.5 / math.pi) + 0.5)
    half = 0.5 * ((angle - turns * 6.28125) - turns * (2.0 * math.pi - 6.28125))
    sq = half * half
    odd = 1.0 / 39916800.0
    for c in (1.0 / 362880.0, 1.0 / 5040.0, 1.0 / 120.0, 1.0 / 6.0, 1.0):
        odd = c - sq * odd
    sh = half * odd
    even = 1.0 / 479001600.0
    for c in (1.0 / 3628800.0, 1.0 / 40320.0, 1.0 / 720.0, 1.0 / 24.0, 0.5, 1.0):
        even = c - sq * even
    return 2.0 * sh * even, 1.0 - 2.0 * sh * sh


def sigmoid(v):
    return 1.0 / (1.0 + jnp.exp(-v))


def own_waves(s1, c1):
    twice = 2.0 * c1
    before_s, before_c = jnp.zeros_like(s1), jnp.ones_like(c1)
    s, c = s1, c1
    for q in range(NR):
        yield (q + 1) * KAPPA, s, c
        if q < NR - 1:
            s, before_s = twice * s - before_s, s
            c, before_c = twice * c - before_c, c


def ghost_waves(s1, c1):
    upper = lax.broadcasted_iota(jnp.int32, s1.shape, 1) >= GHOSTS
    s2, c2 = 2.0 * s1 * c1, 1.0 - 2.0 * s1 * s1
    twice = 2.0 * c2
    s, before_s = jnp.where(upper, s2, s1), jnp.where(upper, 0.0, -s1)
    c, before_c = jnp.where(upper, c2, c1), jnp.where(upper, 1.0, c1)
    shift = jnp.where(upper, 2.0 * KAPPA, KAPPA)
    for p in range(PAIRS):
        yield shift + 2.0 * p * KAPPA, s, c
        if p < PAIRS - 1:
            s, before_s = twice * s - before_s, s
            c, before_c = twice * c - before_c, c


E0, E1, E2, DD, IV, S1, C1, U0, W0 = 0, 1, 2, 3, 4, 5, 6, 7, 10
WAVES = (own_waves, ghost_waves)


def kernel(
    nx,
    ny,
    pos_in,
    tan_in,
    emb_in,
    cnt,
    nbr_in,
    snd_in,
    w1i,
    w1o,
    f1_in,
    wl,
    wr,
    w2i,
    w2o,
    f2_in,
    wh,
    we_in,
    result,
    pos,
    tan,
    emb,
    nbr,
    snd,
    f1,
    f2,
    we,
    w1i_s,
    w1o_s,
    wlr_s,
    w2i_s,
    w2o_s,
    wh_s,
    sndpad,
    c8,
    csel,
    crecv,
    sel1,
    gemb,
    sel2,
    gnode,
    src3,
    rnode,
    gpos,
    rpos,
    onehot,
    mask,
    colb,
    geo,
    waves,
    lb,
    lv0,
    lv1,
    lt,
    pfs_s,
    pfv_s,
    p2_s,
    p2d_s,
    muf,
    phi,
    acc,
    accv,
    lr,
    node,
    pre2,
    phi2,
    mu,
    bar,
    out0,
    out1,
    landing,
    two,
    sums,
    vbar,
    nus,
    pg,
    send1,
    recv1,
    sendc,
    recvc,
    send2,
    recv2,
    send3,
    recv3,
    send4,
    recv4,
    loads,
):
    ix, iy = lax.axis_index("bx"), lax.axis_index("by")

    def device(g, sign):
        dx, dy = offsets[g]
        return (lax.rem(ix + sign * dx + nx, nx), lax.rem(iy + sign * dy + ny, ny))

    barrier = pltpu.get_barrier_semaphore()
    for g in range(8):
        pl.semaphore_signal(barrier, inc=1, device_id=device(g, 1), device_id_type=MESH)

    def block(ref, g):
        return ref.at[pl.ds(g * 8, 8), :]

    def copies(source, target, sends, recvs, sign, whole):
        return [
            pltpu.make_async_remote_copy(
                src_ref=source if whole else block(source, g),
                dst_ref=target.at[g] if whole else block(target, g),
                send_sem=sends.at[g],
                recv_sem=recvs.at[g],
                device_id=device(g, sign),
                device_id_type=MESH,
            )
            for g in range(8)
        ]

    def select(x):
        hi, lo = split(x)
        rows = onehot[1, 0:GHOSTS, :].astype(bf16)
        return mm(rows, hi) + mm(rows, lo)

    lane = lax.broadcasted_iota(jnp.int32, (8, ROWS), 1)
    group = lax.div(lane, 8)

    def merged(ref):
        total = jnp.where(group == 0, ref[0], 0.0)
        for g in range(1, 8):
            total = total + jnp.where(group == g, ref[g], 0.0)
        return total

    weights = []
    spots = ((0, 0), (0, F), (1, 0), (1, F), (1, 2 * F), (2, 0), (2, F))
    for number, (w, (down, at)) in enumerate(zip((w1i, w1o, wl, wr, w2i, w2o, wh), spots)):
        place = landing.at[down * F : (down + 1) * F, at : at + w.shape[1]]
        weights.append((pltpu.make_async_copy(w, place, loads.at[number]), place))
    small = {}
    named = ((snd_in, snd), (pos_in, pos), (tan_in, tan), (emb_in, emb), (nbr_in, nbr))
    named += ((f1_in, f1), (f2_in, f2), (we_in, we))
    for number, (source, place) in enumerate(named):
        small[number] = pltpu.make_async_copy(source, place, loads.at[7 + number])
        small[number].start()
    for copy, _ in weights:
        copy.start()
    for number in range(4):
        small[number].wait()

    sndpad[...] = jnp.full((8, ROWS), -1, jnp.int32)
    sndpad[0:1, 0:GHOSTS] = snd[...]
    hot = jnp.where(
        lax.broadcasted_iota(jnp.int32, (ROWS, ROWS), 0) == sndpad[0:1, :], 1.0, 0.0
    )
    onehot[0] = hot
    onehot[1] = hot.T
    c8[...] = jnp.zeros((8, ROWS), f32)
    c8[0:3, :] = pos[...]
    c8[3:6, :] = tan[...]
    hi, mid, lo = split3(c8[...])
    hot16 = hot.astype(bf16)
    csel[...] = mm(hi, hot16) + (mm(mid, hot16) + mm(lo, hot16))
    sel1[...] = select(emb[...])
    stores = ((w1i_s, 0), (w1o_s, 0), (wlr_s, 0), (wlr_s, F), (w2i_s, 0), (w2o_s, 0), (wh_s, 0))
    for (refs, at), (copy, place) in zip(stores, weights):
        copy.wait()
        hi, lo = split(place[...])
        refs[0, :, at : at + hi.shape[1]] = hi
        refs[1, :, at : at + hi.shape[1]] = lo

    small[4].wait()
    row = lax.broadcasted_iota(jnp.int32, (ROWS, ROWS), 0)
    ghost = lax.rem(row, GHOSTS)
    for side, slots in ((0, row), (1, ROWS + (7 - lax.div(ghost, 8)) * 8 + lax.rem(ghost, 8))):

        def mark(k, total, slots=slots):
            return jnp.where(slots == nbr[pl.ds(k, 1), :], 1.0, total)

        listed = lax.fori_loop(0, nbr.shape[0], mark, jnp.zeros((ROWS, ROWS), f32))
        mask[side] = listed.T

    for number in (5, 6, 7):
        small[number].wait()

    def project(rows, first_w, second_w):
        v = mm3(split(rows), first_w)
        return mm3(split(v * sigmoid(v)), second_w)

    w1 = (w1i_s[0], w1i_s[1]), (w1o_s[0], w1o_s[1])
    phi[0:ROWS, :] = project(emb[...], *w1)
    for j in range(6):
        colb[j] = jnp.broadcast_to(c8[j : j + 1, :], (ROWS, ROWS)).T

    def put2(refs, value, start):
        hi, lo = split(value)
        refs[0, pl.ds(start, value.shape[0]), :] = hi
        refs[1, pl.ds(start, value.shape[0]), :] = lo

    def spread_own(refs, table, filters, at):
        def body(q, carry):
            weights = filters[pl.ds(q, 1), at : at + F]
            put2(refs, table() * weights, pl.multiple_of(q * ROWS, ROWS))
            return carry

        lax.fori_loop(0, NR, body, 0)

    def spread_ghosts(refs, table, filters, at):
        def body(q, carry):
            weights = filters[pl.ds(q, 1), at : at + F]
            put2(refs, table() * weights, pl.multiple_of(NR * ROWS + q * GHOSTS, GHOSTS))
            return carry

        lax.fori_loop(0, NR, body, 0)

    def put_rows(ref, value, first, second, cols):
        hi, lo = split(value)
        ref[first : first + 16, cols] = hi
        ref[second : second + 16, cols] = lo

    spread_own(pfs_s, lambda: phi[0:ROWS, 0:F], f1, 0)
    spread_own(pfv_s, lambda: phi[0:ROWS, F : 2 * F], f1, F)

    scale = 1.0 / math.sqrt(nbr.shape[0])

    def geometry(i, carry, side, table):
        rows = pl.ds(pl.multiple_of(i * 8, 8), 8)
        centre = [colb[j, rows, :] for j in range(6)]
        off = [table[j : j + 1, :] - centre[j] for j in range(3)]
        vel = [table[j : j + 1, :] - centre[j] for j in range(3, 6)]
        listed = mask[side, rows, :]
        sq = off[0] * off[0] + off[1] * off[1] + off[2] * off[2]
        sq = jnp.where(listed > 0.0, sq, 1.0) + SOFT
        inv = lax.rsqrt(sq)
        inv = inv * (1.5 - 0.5 * sq * inv * inv)
        dist = sq * inv
        unit = [x * inv for x in off]
        rate = unit[0] * vel[0] + unit[1] * vel[1] + unit[2] * vel[2]
        s1, c1 = sin_cos(KAPPA * dist)
        weight = scale * listed
        env = 0.5 * (c1 + 1.0)
        env1 = (-0.5 * KAPPA) * s1
        env2 = (-0.5 * KAPPA * KAPPA) * c1
        e0 = weight * env * inv
        slope = env1 - env * inv
        e1 = weight * inv * slope
        e2 = weight * inv * (env2 - 2.0 * inv * slope)
        planes = [e0, e1, e2, rate, inv, s1, c1] + unit
        planes += [(vel[j] - unit[j] * rate) * inv for j in range(3)]
        for number, value in enumerate(planes):
            geo[side, number, rows, :] = value
        for number, (a, s, c) in enumerate(WAVES[side](s1, c1)):
            waves[0, side * NR + number, rows, :] = s
            waves[1, side * NR + number, rows, :] = a * c
        return carry

    lv = (lv0, lv1)

    def build_pairs(m, target):
        side = jnp.where(m < PAIRS, 0, 1)
        cols = pl.ds(pl.multiple_of(m * TILE, TILE), TILE)
        for start in range(0, ROWS, 16):
            rows = slice(start, start + 16)

            def twice(x):
                return jnp.concatenate([x, x], 1)

            e0, e1, rate = (geo[side, number, rows, :] for number in (E0, E1, DD))
            e1d, e0d = twice(e1 * rate), twice(e0 * rate)
            s = jnp.concatenate([waves[0, 2 * m + half, rows, :] for half in range(2)], 1)
            ac = jnp.concatenate([waves[1, 2 * m + half, rows, :] for half in range(2)], 1)
            b = twice(e0) * s
            bd = e1d * s + e0d * ac
            put_rows(lb, bd, start, start + 3 * ROWS, cols)
            put_rows(lb, b, start + ROWS, start + 2 * ROWS, cols)
            for j in range(3):
                u, w = twice(geo[side, U0 + j, rows, :]), twice(geo[side, W0 + j, rows, :])
                first = start + j * ROWS
                put_rows(target, b * u, first, first + 6 * ROWS, slice(None))
                first += 3 * ROWS
                put_rows(target, bd * u + b * w, first, first + 6 * ROWS, slice(None))

    def add_to(ref, rows, value, i):
        if i == 0:
            ref[rows, :] = value
        else:
            ref[rows, :] += value

    def gather_scalar(refs, cols):
        both = mm(lb[:, cols], refs[0, cols, :])
        rest = mm(lb[0 : 2 * ROWS, cols], refs[1, cols, :])
        acc[0:ROWS, :] += both[ROWS : 2 * ROWS] + both[2 * ROWS : 3 * ROWS] + rest[ROWS:]
        acc[ROWS : 2 * ROWS, :] += both[0:ROWS] + both[3 * ROWS :] + rest[0:ROWS]

    def gather_vector(m, near):
        cols = pl.ds(pl.multiple_of(m * TILE, TILE), TILE)
        both = mm(near[...], pfv_s[0, cols, :])
        rest = mm(near[0 : 6 * ROWS, :], pfv_s[1, cols, :])
        accv[...] += both[0 : 6 * ROWS] + both[6 * ROWS :] + rest

    lax.fori_loop(0, ROWS // 8, functools.partial(geometry, side=0, table=c8[...]), 0)
    build_pairs(0, lv0)
    pl.semaphore_wait(barrier, 8)
    coords = copies(csel, crecv, sendc, recvc, 1, True)
    first = copies(sel1, gemb, send1, recv1, 1, False)
    for copy in coords + first:
        copy.start()

    acc[...] = jnp.zeros((2 * ROWS, F), f32)
    accv[...] = jnp.zeros((6 * ROWS, F), f32)

    def two_tiles(k, carry, base, last):
        for half in range(2):
            m = base + 2 * k + half
            gather_vector(m, lv[half])
            build_pairs(jnp.minimum(m + 1, last), lv[1 - half])
        return carry

    lax.fori_loop(0, PAIRS // 2, functools.partial(two_tiles, base=0, last=PAIRS - 1), 0)

    for copy in coords + first:
        copy.wait()
    phi[ROWS:TABLE, :] = project(gemb[...], *w1)
    found = merged(crecv)
    twofold = found + pltpu.roll(found, GHOSTS, 1)
    lax.fori_loop(0, ROWS // 8, functools.partial(geometry, side=1, table=twofold), 0)
    build_pairs(PAIRS, lv0)

    spread_ghosts(pfs_s, lambda: phi[ROWS:TABLE, 0:F], f1, 0)
    spread_ghosts(pfv_s, lambda: phi[ROWS:TABLE, F : 2 * F], f1, F)
    lax.fori_loop(
        0, (TILES - PAIRS) // 2, functools.partial(two_tiles, base=PAIRS, last=TILES - 1), 0
    )
    gather_vector(TILES - 1, lv0)


    def scalar_step(i, carry):
        gather_scalar(pfs_s, pl.ds(pl.multiple_of(i * STEP, STEP), STEP))
        return carry

    lax.fori_loop(0, STEPS, scalar_step, 0)
    lr[...] = mm3(split(accv[...]), (wlr_s[0], wlr_s[1]))

    def part(j, side):
        return lr[j * ROWS : (j + 1) * ROWS, side * F : (side + 1) * F]

    state = emb[...] + acc[0:ROWS, :]
    moved = acc[ROWS : 2 * ROWS, :]
    for j in range(3):
        state = state + part(j, 0) * part(j, 1)
        moved = moved + (part(3 + j, 0) * part(j, 1) + part(j, 0) * part(3 + j, 1))
    node[:, 0:F] = state
    node[:, F : 2 * F] = moved
    sel2[...] = select(node[...])
    second = copies(sel2, gnode, send2, recv2, 1, False)
    for copy in second:
        copy.start()

    w2 = (w2i_s[0], w2i_s[1]), (w2o_s[0], w2o_s[1])

    def table_two(values, moves, at, n):
        v = mm3(split(values), w2[0])
        vd = mm3(split(moves), w2[0])
        sig = sigmoid(v)
        pre2[0, at : at + n, :] = v
        pre2[1, at : at + n, :] = vd
        slope = sig * (1.0 + v * (1.0 - sig))
        phi2[0, at : at + n, :] = mm3(split(v * sig), w2[1])
        phi2[1, at : at + n, :] = mm3(split(slope * vd), w2[1])

    table_two(node[:, 0:F], node[:, F : 2 * F], 0, ROWS)

    for side in range(2):
        rows = ROWS if side == 0 else GHOSTS
        e0, e1, rate = (geo[side, number] for number in (E0, E1, DD))
        pg[side, 0] = e0.T
        pg[side, 1] = (e1 * rate).T
        pg[side, 2] = (e0 * rate).T
        pg[side, 3] = geo[side, S1].T
        pg[side, 4] = geo[side, C1].T

    def turned(side, count):
        def body(i, carry):
            start = pl.multiple_of(i * 16, 16)
            g = [pg[side, number, pl.ds(start, 16), :] for number in range(5)]
            held = None
            for q, (a, s, c) in enumerate(own_waves(g[3], g[4])):
                new = (g[0] * s, g[1] * s + g[2] * (a * c))
                if q % 2 == 0:
                    held = new
                    continue
                cols = slice((q - 1) * ROWS, (q + 1) * ROWS)
                for value, first, second in ((1, 0, 3), (0, 1, 2)):
                    hi, lo = split(jnp.concatenate([held[value], new[value]], 1))
                    at = 4 * side * ROWS
                    lt[pl.ds(start + at + first * count, 16), cols] = hi
                    lt[pl.ds(start + at + second * count, 16), cols] = lo
            return carry

        lax.fori_loop(0, count // 16, body, 0)

    turned(0, ROWS)
    turned(1, GHOSTS)

    spread_own(p2_s, lambda: phi2[0, 0:ROWS, :], f2, 0)
    spread_own(p2d_s, lambda: phi2[1, 0:ROWS, :], f2, 0)
    acc[...] = jnp.zeros((2 * ROWS, F), f32)

    def messages_two(i, carry):
        cols = pl.ds(pl.multiple_of(i * STEP, STEP), STEP)
        gather_scalar(p2_s, cols)
        both = mm(lb[ROWS : 3 * ROWS, cols], p2d_s[0, cols, :])
        rest = mm(lb[ROWS : 2 * ROWS, cols], p2d_s[1, cols, :])
        acc[ROWS : 2 * ROWS, :] += both[0:ROWS] + both[ROWS:] + rest
        return carry

    lax.fori_loop(0, OWN_STEPS, messages_two, 0)

    for copy in second:
        copy.wait()
    table_two(gnode[:, 0:F], gnode[:, F : 2 * F], ROWS, GHOSTS)
    spread_ghosts(p2_s, lambda: phi2[0, ROWS:TABLE, :], f2, 0)
    spread_ghosts(p2d_s, lambda: phi2[1, ROWS:TABLE, :], f2, 0)
    messages_two(OWN_STEPS, 0)
    st = node[:, 0:F] + acc[0:ROWS, :]
    std = node[:, F : 2 * F] + acc[ROWS : 2 * ROWS, :]

    whs = wh_s[0], wh_s[1]
    v = mm3(split(st), whs)
    vd = mm3(split(std), whs)
    sig = sigmoid(v)
    live = lax.broadcasted_iota(jnp.int32, (ROWS, F), 0) < cnt[0]
    top = jnp.where(live, jnp.broadcast_to(we[...], (ROWS, F)), 0.0)
    mu[0] = mm3(split(top * (sig * (1.0 + v * (1.0 - sig)))), whs, NT)
    mu[1] = mm3(
        split(top * (sig * (1.0 - sig) * (2.0 + v * (1.0 - 2.0 * sig))) * vd), whs, NT
    )

    def scaled(i):
        for q in range(4 * i, 4 * i + 4):
            weights = f2[q : q + 1, :]
            rows = slice(q % 4 * ROWS, (q % 4 + 1) * ROWS)
            for number in range(2):
                hi, lo = split(mu[number] * weights)
                muf[i, 2 * number, rows, :] = hi
                muf[i, 2 * number + 1, rows, :] = lo

    def turned_messages(i, at, count):
        cols = slice(i * 4 * ROWS, (i + 1) * 4 * ROWS)
        top = 4 * at
        both = mm(lt[top : top + 4 * count, cols], muf[i, 0])
        rest = mm(lt[top : top + 2 * count, cols], muf[i, 1])
        also = mm(lt[top + count : top + 3 * count, cols], muf[i, 2])
        more = mm(lt[top + count : top + 2 * count, cols], muf[i, 3])
        add_to(
            bar,
            slice(at, at + count),
            both[count : 2 * count] + both[2 * count : 3 * count] + rest[count:],
            i,
        )
        add_to(
            bar,
            slice(TABLE + at, TABLE + at + count),
            (both[0:count] + both[3 * count :] + rest[0:count])
            + (also[0:count] + also[count:] + more),
            i,
        )

    def back_to_states(at, count):
        near, far = slice(at, at + count), slice(TABLE + at, TABLE + at + count)
        v, vd = pre2[0, near, :], pre2[1, near, :]
        sig = sigmoid(v)
        slope = sig * (1.0 + v * (1.0 - sig))
        curve = sig * (1.0 - sig) * (2.0 + v * (1.0 - 2.0 * sig))
        both = mm3(split(jnp.concatenate([bar[near, :], bar[far, :]], 0)), w2[1], NT)
        first, second = both[0:count], both[count:]
        both = jnp.concatenate([first * slope, second * slope + first * curve * vd], 0)
        both = mm3(split(both), w2[0], NT)
        bar[near, :] = both[0:count]
        bar[far, :] = both[count:]

    for i in range(NR // 4 + 1):
        if i < NR // 4:
            scaled(i)
        if i > 0:
            turned_messages(i - 1, ROWS, GHOSTS)
    back_to_states(ROWS, GHOSTS)
    src3[:, 0:F] = bar[ROWS:TABLE, :]
    src3[:, F : 2 * F] = bar[TABLE + ROWS : 2 * TABLE, :]
    third = copies(src3, rnode, send3, recv3, -1, False)
    for copy in third:
        copy.start()

    for i in range(NR // 4):
        turned_messages(i, 0, ROWS)
    back_to_states(0, ROWS)

    m = split(mu[0])
    md = split(mu[1])
    high = jnp.concatenate([m[0], md[0]], 0)
    full = jnp.concatenate([high, m[1], md[1]], 0)
    ours = jnp.concatenate(m, 0)

    def pairs_two(i, carry):
        cols = pl.ds(pl.multiple_of(i * STEP, TILE), STEP)
        both = mm(full, p2_s[0, cols, :], NT)
        rest = mm(high, p2_s[1, cols, :], NT)
        also = mm(ours, p2d_s[0, cols, :], NT)
        more = mm(m[0], p2d_s[1, cols, :], NT)
        two[0:ROWS, cols] = both[0:ROWS] + both[2 * ROWS : 3 * ROWS] + rest[0:ROWS]
        two[ROWS : 2 * ROWS, cols] = (
            both[ROWS : 2 * ROWS] + both[3 * ROWS :] + rest[ROWS:]
        ) + (also[0:ROWS] + also[ROWS:] + more)
        return carry

    lax.fori_loop(0, STEPS, pairs_two, 0)

    for copy in third:
        copy.wait()
    rows_back = onehot[0, :, 0:GHOSTS].astype(bf16)
    hi, lo = split(rnode[...])
    returned = mm(rows_back, hi) + mm(rows_back, lo)
    nu = mu[0] + bar[0:ROWS, :] + returned[:, 0:F]
    nud = mu[1] + bar[TABLE : TABLE + ROWS, :] + returned[:, F : 2 * F]
    mu[0] = nu
    mu[1] = nud

    wlr = wlr_s[0], wlr_s[1]
    for j in range(3):
        nu, nud = mu[0], mu[1]
        l, r, ld, rd = part(j, 0), part(j, 1), part(3 + j, 0), part(3 + j, 1)
        lr[j * ROWS : (j + 1) * ROWS, 0:F] = nu * r
        lr[j * ROWS : (j + 1) * ROWS, F : 2 * F] = nu * l
        lr[(3 + j) * ROWS : (4 + j) * ROWS, 0:F] = nud * r + nu * rd
        lr[(3 + j) * ROWS : (4 + j) * ROWS, F : 2 * F] = nud * l + nu * ld
    hi, lo = split(mm3(split(lr[...]), wlr, NT))
    vbar[0 : 6 * ROWS, :] = hi
    vbar[6 * ROWS :, :] = lo
    for number in range(2):
        hi, lo = split(mu[number])
        nus[number * ROWS : (number + 1) * ROWS, :] = hi
        nus[(2 + number) * ROWS : (3 + number) * ROWS, :] = lo
    out = (out0, out1)

    def pairs_one(m, target, count):
        width = count * TILE
        cols = pl.ds(pl.multiple_of(m * TILE, TILE), width)
        both = mm(nus[...], pfs_s[0, cols, :], NT)
        rest = mm(nus[0 : 2 * ROWS, :], pfs_s[1, cols, :], NT)
        target[0 : 2 * ROWS, 0:width] = two[:, cols] + (
            both[0 : 2 * ROWS] + both[2 * ROWS :] + rest
        )
        both = mm(vbar[...], pfv_s[0, cols, :], NT)
        rest = mm(vbar[0 : 6 * ROWS, :], pfv_s[1, cols, :], NT)
        target[2 * ROWS :, 0:width] = both[0 : 6 * ROWS] + both[6 * ROWS :] + rest

    upper = lax.broadcasted_iota(jnp.int32, (8, ROWS), 1) >= GHOSTS

    def sum_waves(m, source, place):
        m = jnp.int32(m)
        side = jnp.where(m < PAIRS, 0, 1)
        base = jnp.where(m < PAIRS, 2 * m + 1, 4 * (m - PAIRS) + 1).astype(f32)
        jump = jnp.where(m < PAIRS, 1.0, 2.0)
        ghosts_on = jnp.where(m < PAIRS, 0.0, 1.0)
        a = [
            KAPPA * (base + half * jump + ghosts_on * jnp.where(upper, 1.0, 0.0))
            for half in range(2)
        ]
        aa = [x * x for x in a]
        for start in range(0, ROWS, 8):
            rows = slice(start, start + 8)
            u = [geo[side, U0 + j, rows, :] for j in range(3)]
            total = [sums[side, number, rows, :] for number in range(14)]
            for half in range(2):
                s = waves[0, 2 * m + half, rows, :]
                ac = waves[1, 2 * m + half, rows, :]
                ss = s * aa[half]
                cols = slice(place * TILE + half * ROWS, place * TILE + (half + 1) * ROWS)
                y = [source[start + k * ROWS : start + k * ROWS + 8, cols] for k in range(8)]
                along = y[0] + u[0] * y[2] + u[1] * y[3] + u[2] * y[4]
                along_d = y[1] + u[0] * y[5] + u[1] * y[6] + u[2] * y[7]
                for j in range(3):
                    total[j] += s * y[2 + j]
                    total[3 + j] += ac * y[2 + j]
                    total[6 + j] += s * y[5 + j]
                total[9] += s * y[0]
                total[10] += ac * y[0]
                total[11] += ss * along
                total[12] += s * y[1]
                total[13] += ac * along_d
            for number in range(14):
                sums[side, number, rows, :] = total[number]

    sums[...] = jnp.zeros(sums.shape, f32)
    def sum_both(m, source):
        sum_waves(m, source, 0)
        sum_waves(m + 1, source, 1)

    pairs_one(PAIRS, out0, 2)
    pairs_one(PAIRS + 2, out1, 2)
    sum_both(PAIRS, out0)
    pairs_one(PAIRS + 4, out0, 1)
    sum_both(PAIRS + 2, out1)
    pairs_one(0, out1, 2)
    sum_waves(PAIRS + 4, out0, 0)

    def offsets_back(i, carry, side):
        rows = pl.ds(pl.multiple_of(i * 8, 8), 8)
        e0, e1, e2, rate, inv = (geo[side, number, rows, :] for number in range(5))
        unit = [geo[side, U0 + j, rows, :] for j in range(3)]
        turn = [geo[side, W0 + j, rows, :] for j in range(3)]
        z = [sums[side, number, rows, :] for number in range(14)]
        db = e1 * z[9] + e0 * z[10]
        dbd = e2 * z[9] + 2.0 * e1 * z[10] - e0 * z[11]
        inner = z[12]
        w = jnp.zeros((8, ROWS), f32)
        wd = w
        spin = w
        ub, ubd = [], []
        for j in range(3):
            slope = e1 * z[j] + e0 * z[3 + j]
            ub.append(e0 * z[j])
            ubd.append(rate * slope + e0 * z[6 + j])
            db = db + unit[j] * slope
            dbd = dbd + unit[j] * (e2 * z[j] + 2.0 * e1 * z[3 + j])
            inner = inner + unit[j] * z[6 + j]
            spin = spin + turn[j] * slope
            w = w + unit[j] * ub[j]
            wd = wd + turn[j] * ub[j] + unit[j] * ubd[j]
        dbd = rate * dbd + e1 * inner + e0 * z[13] + spin
        for j in range(3):
            t = (ub[j] - unit[j] * w) * inv
            pg[side, j, rows, :] = db * unit[j] + t
            pg[side, 3 + j, rows, :] = (
                dbd * unit[j]
                + db * turn[j]
                + (ubd[j] - turn[j] * w - unit[j] * wd - t * rate) * inv
            )
        return carry

    lax.fori_loop(0, ROWS // 8, functools.partial(offsets_back, side=1), 0)
    gpos[...] = jnp.zeros((8, ROWS), f32)
    c8[...] = jnp.zeros((8, ROWS), f32)
    for j in range(6):
        ghosts = pg[1, j]
        gpos[j : j + 1, :] = jnp.sum(ghosts, axis=0, keepdims=True)
        c8[j : j + 1, :] = jnp.sum(ghosts.T, axis=0, keepdims=True)
    both = gpos[...]
    gpos[...] = both + pltpu.roll(both, GHOSTS, 1)
    last = copies(gpos, rpos, send4, recv4, -1, True)
    for copy in last:
        copy.start()

    def two_sums(k, carry):
        pairs_one(4 * k + 2, out0, 2)
        sum_both(4 * k, out1)
        pairs_one(4 * k + 4, out1, 2)
        sum_both(4 * k + 2, out0)
        return carry

    lax.fori_loop(0, 2, two_sums, 0)
    sum_both(8, out1)
    lax.fori_loop(0, ROWS // 8, functools.partial(offsets_back, side=0), 0)
    for j in range(6):
        own = pg[0, j]
        c8[j : j + 1, :] = jnp.sum(own - own.T, axis=0, keepdims=True) - c8[j : j + 1, :]
    for copy in last:
        copy.wait()
    hi, mid, lo = split3(merged(rpos))
    slots = onehot[1].astype(bf16)
    total = c8[...] + (mm(hi, slots) + (mm(mid, slots) + mm(lo, slots)))
    result[...] = -total


def per_device(nx, ny, *arrays):
    arrays = list(arrays)
    arrays[15] = arrays[15].reshape(1, F)
    vmem = pl.BlockSpec(memory_space=pltpu.VMEM)
    in_specs = [pl.BlockSpec(memory_space=pl.ANY)] * 16
    in_specs[3] = pl.BlockSpec(memory_space=pltpu.SMEM)

    def v32(*shape):
        return pltpu.VMEM(shape, f32)

    def v16(*shape):
        return pltpu.VMEM(shape, bf16)

    dma = pltpu.SemaphoreType.DMA((8,))
    scratch = [
        v32(3, ROWS),
        v32(3, ROWS),
        v32(ROWS, F),
        pltpu.VMEM(arrays[4].shape, jnp.int32),
        pltpu.VMEM((1, GHOSTS), jnp.int32),
        v32(NR, 2 * F),
        v32(NR, F),
        v32(1, F),
        v16(2, F, F),
        v16(2, F, 2 * F),
        v16(2, F, 2 * F),
        v16(2, F, F),
        v16(2, F, F),
        v16(2, F, F),
        pltpu.VMEM((8, ROWS), jnp.int32),
        v32(8, ROWS),
        v32(8, ROWS),
        v32(8, 8, ROWS),
        v32(GHOSTS, F),
        v32(GHOSTS, F),
        v32(GHOSTS, 2 * F),
        v32(GHOSTS, 2 * F),
        v32(GHOSTS, 2 * F),
        v32(GHOSTS, 2 * F),
        v32(8, ROWS),
        v32(8, 8, ROWS),
        v32(2, ROWS, ROWS),
        v32(2, ROWS, ROWS),
        v32(6, ROWS, ROWS),
        v32(2, 13, ROWS, ROWS),
        v32(2, NR + PAIRS, ROWS, ROWS),
        v16(4 * ROWS, WIDE),
        v16(12 * ROWS, TILE),
        v16(12 * ROWS, TILE),
        v16(4 * TABLE, NR * ROWS),
        v16(2, WIDE, F),
        v16(2, WIDE, F),
        v16(2, WIDE, F),
        v16(2, WIDE, F),
        v16(NR // 4, 4, 4 * ROWS, F),
        v32(TABLE, 2 * F),
        v32(2 * ROWS, F),
        v32(6 * ROWS, F),
        v32(6 * ROWS, 2 * F),
        v32(ROWS, 2 * F),
        v32(2, TABLE, F),
        v32(2, TABLE, F),
        v32(2, ROWS, F),
        v32(2 * TABLE, F),
        v32(8 * ROWS, 2 * TILE),
        v32(8 * ROWS, 2 * TILE),
        v32(3 * F, 3 * F),
        v32(2 * ROWS, WIDE),
        v32(2, 14, ROWS, ROWS),
        v16(12 * ROWS, F),
        v16(4 * ROWS, F),
        v32(2, 6, ROWS, ROWS),
    ] + [dma] * 10 + [pltpu.SemaphoreType.DMA((15,))]
    result = pl.pallas_call(
        functools.partial(kernel, nx, ny),
        out_shape=jax.ShapeDtypeStruct((8, ROWS), f32),
        in_specs=in_specs,
        out_specs=vmem,
        scratch_shapes=scratch,
        compiler_params=pltpu.CompilerParams(
            collective_id=0, has_side_effects=True, vmem_limit_bytes=67043328
        ),
    )(*arrays)
    return result[0:3], result[3:6]


def solution(mesh):
    placed = (
        P(None, ("bx", "by")),
        P(None, ("bx", "by")),
        P(("bx", "by"), None),
        P(("bx", "by")),
        P(None, ("bx", "by")),
        P(("bx", "by"), None),
    ) + (P(),) * 10
    return jax.shard_map(
        functools.partial(per_device, mesh.shape["bx"], mesh.shape["by"]),
        mesh=mesh,
        in_specs=placed,
        out_specs=(P(None, ("bx", "by")), P(None, ("bx", "by"))),
        check_vma=False,
    )
```
